32 devices in a mesh: dp: 8 (over z, x), seq: 4 (over y, core).
Axes of the slice: x: 2, y: 2, z: 4, core: 2. Of those that a mesh axis runs over, the one named last changes fastest.
Arguments:
- tokens: bfloat16 [2, 16384, 768], P(None, ('dp', 'seq')), may hold values from -6 to 6
- cotangent: bfloat16 [2, 16384, 768], P(None, ('dp', 'seq')), may hold values from -6 to 6
- lengths: int32 [2, 8, 4], P(None, 'dp'), may hold values from 1 to 1365, 2048 in all within a row
- gain_first: bfloat16 [768], P(('dp', 'seq')), may hold values from 0.5 to 1.5
- shift_first: bfloat16 [768], P(('dp', 'seq')), may hold values from -3 to 3
- packed_weight: bfloat16 [768, 2304], P(('dp', 'seq')), may hold values from -0.21875 to 0.21875
- packed_bias: bfloat16 [1536], P(('dp', 'seq')), may hold values from -3 to 3
- output_weight: bfloat16 [768, 768], P(('dp', 'seq')), may hold values from -6 to 6
- output_bias: bfloat16 [768], P(('dp', 'seq')), may hold values from -3 to 3
- gain_second: bfloat16 [768], P(('dp', 'seq')), may hold values from 0.5 to 1.5
- shift_second: bfloat16 [768], P(('dp', 'seq')), may hold values from -3 to 3
- expand_weight: bfloat16 [768, 3072], P(('dp', 'seq')), may hold values from -0.21875 to 0.21875
- expand_bias: bfloat16 [3072], P(('dp', 'seq')), may hold values from -3 to 3
- reduce_weight: bfloat16 [3072, 768], P(('dp', 'seq')), may hold values from -0.375 to 0.375
- reduce_bias: bfloat16 [768], P(('dp', 'seq')), may hold values from -3 to 3
Outputs:
- layer_output: bfloat16 [2, 16384, 768], P(None, ('dp', 'seq'))
- input_grad: bfloat16 [2, 16384, 768], P(None, ('dp', 'seq'))
- gain_first_grad: float32 [768], P(('dp', 'seq'))
- shift_first_grad: float32 [768], P(('dp', 'seq'))
- packed_weight_grad: float32 [768, 2304], P(('dp', 'seq'))
- packed_bias_grad: float32 [1536], P(('dp', 'seq'))
- output_weight_grad: float32 [768, 768], P(('dp', 'seq'))
- output_bias_grad: float32 [768], P(('dp', 'seq'))
- gain_second_grad: float32 [768], P(('dp', 'seq'))
- shift_second_grad: float32 [768], P(('dp', 'seq'))
- expand_weight_grad: float32 [768, 3072], P(('dp', 'seq'))
- expand_bias_grad: float32 [3072], P(('dp', 'seq'))
- reduce_weight_grad: float32 [3072, 768], P(('dp', 'seq'))
- reduce_bias_grad: float32 [768], P(('dp', 'seq'))
The draws below stay inside these ranges and needn't reach their ends.
Inputs may be any that keep to these rules, and one draw needn't show every extreme that they name: Each row lengths[m, g] has 3 sequence lengths in order, then the padding length; it sums to 2048 and its largest entry is exactly 1365. Every entry, sequences and padding alike, lies anywhere from 1 to 1365; there is no larger lower bound. The padding mask is not an argument: it follows from the lengths.
All inputs are finite; a program needn't handle non-finite values.
Results may differ from the reference program's by a relative error of at most 0.011.
Values may be sent and summed in bfloat16 or wider, within the bound.
A program may use at most 192 MiB of HBM per device.

```python
import math
import jax
import jax.numpy as jnp
import numpy as np
from jax import lax

D = 768
H = 12
HD = 64
FF = 3072
MB = 2
SLOTS = 4
BUCKET = 2048
MOST = 1365
TOKENS_MB = 16384
N_DP = 8


def level_of(own_key, shape, split, low, top_value):
    gain, own = 1.0, jax.random.fold_in(own_key, 6)
    for dim, shards_of in split:
        draws = jnp.exp(jax.random.uniform(jax.random.fold_in(own, dim), (shards_of,), jnp.float32, low / len(split), top_value / len(split)))
        gain = gain * jnp.repeat(draws, shape[dim] // shards_of).reshape([-1 if axis == dim else 1 for axis in range(len(shape))])
    return gain


def split_up(number_of, total, bound, lean):
    weights = [(1 << 20) // math.isqrt(grade ** lean) + 1 for grade in range(2, number_of + 1)]
    surplus, counts = total - bound - (number_of - 1), [1] * (number_of - 1)
    while surplus > 0:
        candidates = [i for i in range(number_of - 1) if counts[i] < bound]
        pool, left = sum([weights[i] for i in candidates]), surplus
        for i in candidates:
            more = min(bound - counts[i], max(1, left * weights[i] // pool), surplus)
            counts[i] = counts[i] + more
            surplus = surplus - more
    return np.array([bound] + counts)


def uneven(key, amount, total, reach, slope):
    if amount == 2:
        one = jax.random.randint(key, (), max(1, total - reach), min(reach, total - 1) + 1)
        return jnp.stack([one, total - one])
    sizes = jnp.asarray(split_up(amount, total, reach, slope), jnp.int32)
    couples = (amount - 1) // 2
    source_of, taker = sizes[1:1 + 2 * couples:2], sizes[2:2 + 2 * couples:2]
    margin = jnp.minimum(source_of - 1, reach - taker)
    moved = jax.random.randint(jax.random.fold_in(key, 1), (couples,), 0, 1 << 20) % (margin + 1)
    sizes = sizes.at[1:1 + 2 * couples:2].set(source_of - moved).at[2:2 + 2 * couples:2].set(taker + moved)
    return sizes[jax.random.permutation(jax.random.fold_in(key, 2), amount)]


def normal_values(key, dims, scale, limit, shards=(), kind=jnp.bfloat16):
    entries = scale * jax.random.normal(key, dims, jnp.float32)
    if shards:
        entries = entries * level_of(key, dims, shards, -0.22, 0.18)
    return jnp.clip(entries, -limit, limit).astype(kind)


def setup_inputs(seed: int = 0) -> dict:
    key_of = jax.random.split(jax.random.key(seed), 16)
    tokens = normal_values(key_of[0], (MB, TOKENS_MB, D), 1.0, 6.0, ((1, 32),))
    cotangent = normal_values(key_of[1], (MB, TOKENS_MB, D), 1.0, 6.0, ((1, 32),))
    lengths = jax.vmap(lambda own: uneven(own, SLOTS, BUCKET, MOST, 2))(jax.random.split(key_of[2], MB * N_DP)).reshape((MB, N_DP, SLOTS)).astype(jnp.int32)
    gain_first = jnp.clip(1.0 + 0.1 * jax.random.normal(key_of[3], (D,), jnp.float32), 0.5, 1.5).astype(jnp.bfloat16)
    shift_first = normal_values(key_of[4], (D,), 0.5, 3.0, ((0, 32),))
    packed_weight = normal_values(key_of[5], (D, 3 * D), D ** -0.5, 0.21875, ((0, 32),))
    packed_bias = normal_values(key_of[6], (2 * D,), 0.5, 3.0, ((0, 32),))
    output_weight = normal_values(key_of[7], (D, D), 1 ** -0.5, 6.0, ((0, 32),))
    output_bias = normal_values(key_of[8], (D,), 0.5, 3.0, ((0, 32),))
    gain_second = jnp.clip(1.0 + 0.1 * jax.random.normal(key_of[9], (D,), jnp.float32), 0.5, 1.5).astype(jnp.bfloat16)
    shift_second = normal_values(key_of[10], (D,), 0.5, 3.0, ((0, 32),))
    expand_weight = normal_values(key_of[11], (D, FF), D ** -0.5, 0.21875, ((0, 32),))
    expand_bias = normal_values(key_of[12], (FF,), 0.5, 3.0, ((0, 32),))
    reduce_weight = normal_values(key_of[13], (FF, D), (FF // 12) ** -0.5, 0.375, ((0, 32),))
    reduce_bias = normal_values(key_of[14], (D,), 0.5, 3.0, ((0, 32),))
    return {"tokens": tokens, "cotangent": cotangent, "lengths": lengths, "gain_first": gain_first, "shift_first": shift_first, "packed_weight": packed_weight, "packed_bias": packed_bias, "output_weight": output_weight, "output_bias": output_bias, "gain_second": gain_second, "shift_second": shift_second, "expand_weight": expand_weight, "expand_bias": expand_bias, "reduce_weight": reduce_weight, "reduce_bias": reduce_bias}


BRANCH_SCALE = 12 ** (-0.5)
EPSILON = 1e-05

@jax.custom_vjp
def low(v):
    return lax.optimization_barrier(v.astype(jnp.bfloat16)).astype(jnp.float32)

@jax.custom_vjp
def low_back(v):
    return v

def low_keep(v):
    return (low(v), None)

def low_pass(kept, grad):
    return (grad,)

def back_keep(v):
    return (v, None)

def back_low(kept, grad):
    return (low(grad),)
low.defvjp(low_keep, low_pass)
low_back.defvjp(back_keep, back_low)

def matmul(first_operand, second_operand):
    return jnp.dot(first_operand, second_operand, precision=lax.Precision.HIGHEST)

def layer_norm(values, norm_gain, norm_shift):
    center = values - lax.optimization_barrier(jnp.mean(values, axis=-1, keepdims=True))
    spread = lax.optimization_barrier(jnp.mean(center * center, axis=-1, keepdims=True))
    return center * lax.rsqrt(spread + EPSILON) * norm_gain + norm_shift

def segment_ids(bucket_lengths, places):
    segment_ends = jnp.cumsum(bucket_lengths)
    return lax.optimization_barrier(jnp.sum((places[:, None] >= segment_ends[None, :]).astype(jnp.int32), axis=1))

def attend_rows(query_rows, row_ids, row_places, key_rows, value_rows, key_ids, key_places):
    score_scale = HD ** (-0.5)
    scores = jnp.einsum('qhd,khd->hqk', query_rows, key_rows, precision=lax.Precision.HIGHEST) * score_scale
    scores = low_back(scores)
    allowed = (row_ids[:, None] == key_ids[None, :]) & (key_places[None, :] <= row_places[:, None])
    scores = jnp.where(allowed[None], scores, -1e+30)
    highest = lax.optimization_barrier(jnp.max(scores, axis=-1, keepdims=True))
    weights = jnp.exp(scores - highest)
    probabilities = low(weights / lax.optimization_barrier(jnp.sum(weights, axis=-1, keepdims=True)))
    return jnp.einsum('hqk,khd->qhd', probabilities, value_rows, precision=lax.Precision.HIGHEST)

def bucket_layer(params, inputs, bucket_lengths):
    gain_one, shift_one, packed_w, packed_b, output_w, output_b, gain_two, shift_two, expand_w, expand_b, reduce_w, reduce_b = params
    places = jnp.arange(BUCKET, dtype=jnp.int32)
    ids = segment_ids(bucket_lengths, places)
    valid = (ids < SLOTS - 1).astype(jnp.float32)[:, None]
    normed = low(layer_norm(inputs, gain_one, shift_one))
    bias_row = jnp.concatenate([packed_b[:D], jnp.zeros((D,), jnp.float32), packed_b[D:]])
    packed = low(low_back(matmul(normed, packed_w) + bias_row))
    queries = packed[:, :D].reshape(BUCKET, H, HD)
    key_rows = packed[:, D:2 * D].reshape(BUCKET, H, HD)
    value_rows = packed[:, 2 * D:].reshape(BUCKET, H, HD)
    block_rows = min(512, BUCKET)
    blocks = BUCKET // block_rows

    def block_step(block_args):
        return attend_rows(block_args[0], block_args[1], block_args[2], key_rows, value_rows, ids, places)
    attended = lax.map(jax.checkpoint(block_step), (queries.reshape(blocks, block_rows, H, HD), ids.reshape(blocks, block_rows), places.reshape(blocks, block_rows)))
    attended = low(low_back(attended.reshape(BUCKET, D)))
    projected = low_back(matmul(attended, output_w) + output_b)
    middle = inputs + BRANCH_SCALE * projected
    normed_two = low(layer_norm(middle, gain_two, shift_two))
    hidden = low_back(matmul(normed_two, expand_w) + expand_b)
    active = low(jax.nn.gelu(hidden, approximate=True))
    branch_out = low_back(matmul(active, reduce_w) + reduce_b)
    return (middle + BRANCH_SCALE * branch_out) * valid

def reference(tokens, cotangent, lengths, gain_first, shift_first, packed_weight, packed_bias, output_weight, output_bias, gain_second, shift_second, expand_weight, expand_bias, reduce_weight, reduce_bias):
    params = tuple((weight.astype(jnp.float32) for weight in (gain_first, shift_first, packed_weight, packed_bias, output_weight, output_bias, gain_second, shift_second, expand_weight, expand_bias, reduce_weight, reduce_bias)))
    inputs = tokens.astype(jnp.float32).reshape(MB * N_DP, BUCKET, D)
    grad_rows = cotangent.astype(jnp.float32).reshape(MB * N_DP, BUCKET, D)
    bucket_lengths = lengths.reshape(MB * N_DP, SLOTS)
    checked_layer = jax.checkpoint(bucket_layer)

    def forward(layer_params, layer_inputs):
        return lax.map(lambda pair: checked_layer(layer_params, pair[0], pair[1]), (layer_inputs, bucket_lengths))
    outputs, pullback = jax.vjp(forward, params, inputs)
    param_grads, input_grads = pullback(grad_rows)
    layer_output = outputs.astype(jnp.bfloat16).reshape(MB, N_DP * BUCKET, D)
    input_grad = input_grads.astype(jnp.bfloat16).reshape(MB, N_DP * BUCKET, D)
    return (layer_output, input_grad, param_grads[0], param_grads[1], param_grads[2], param_grads[3], param_grads[4], param_grads[5], param_grads[6], param_grads[7], param_grads[8], param_grads[9], param_grads[10], param_grads[11])
```

```python
import functools

import jax
import jax.numpy as jnp
from jax import lax
from jax.experimental import pallas as pl
from jax.experimental.pallas import tpu as pltpu
from jax.sharding import PartitionSpec as P

H = 12
HD = 64
BRANCH_SCALE = 12 ** (-0.5)
EPSILON = 1e-05
F32 = jnp.float32
BF16 = jnp.bfloat16
TILE = 256
PAIR = 2 * HD
MASKED = -1e30


def outer_sum(first, second):
    return lax.dot_general(first, second, (((0,), (0,)), ((), ())), preferred_element_type=F32)


def against_rows(first, second):
    return lax.dot_general(first, second, (((1,), (1,)), ((), ())), preferred_element_type=F32)


def layer_norm(values, norm_gain, norm_shift):
    center = values - jnp.mean(values, axis=-1, keepdims=True)
    spread = jnp.mean(center * center, axis=-1, keepdims=True)
    return center * lax.rsqrt(spread + EPSILON) * norm_gain + norm_shift


def gelu_tanh(values):
    return jax.nn.gelu(values, approximate=True)


def split_pair(rows):
    lane = lax.broadcasted_iota(jnp.int32, rows.shape, 1)
    nothing = jnp.zeros_like(rows)
    return jnp.where(lane < HD, rows, nothing), jnp.where(lane < HD, nothing, rows)


def allowed_in(key_block, row_block, begins, diagonal):
    keys = key_block * TILE + lax.broadcasted_iota(jnp.int32, (TILE, TILE), 0)
    allowed = keys >= begins
    if diagonal:
        rows = row_block * TILE + lax.broadcasted_iota(jnp.int32, (TILE, TILE), 1)
        allowed = allowed & (keys <= rows)
    return allowed


def attend_kernel(low_ref, q_ref, k_ref, v_ref, begin_ref, out_ref, logsum_ref, value_t):
    blocks = q_ref.shape[0] // TILE
    for block in range(blocks):
        at = slice(block * TILE, (block + 1) * TILE)
        value_t[:, at] = v_ref[at, :].T

    def one_row_block(i, carry):
        here = pl.ds(pl.multiple_of(i * TILE, TILE), TILE)
        heads = split_pair(q_ref[here, :] * HD ** (-0.5))
        begins = begin_ref[:, here]

        def visit(j, state, diagonal):
            there = pl.ds(pl.multiple_of(j * TILE, TILE), TILE)
            key_rows = k_ref[there, :]
            allowed = allowed_in(j, i, begins, diagonal)
            new_state = []
            for which in range(2):
                scores = against_rows(key_rows, heads[which])
                scores = jnp.where(allowed, scores, MASKED)
                top = jnp.max(scores, axis=0, keepdims=True)
                if state is not None:
                    old_top, old_total, old_mix = state[which]
                    top = jnp.maximum(top, old_top)
                weights = jnp.exp(scores - top)
                total = jnp.sum(weights, axis=0, keepdims=True)
                mix = jnp.dot(
                    value_t[which * HD : (which + 1) * HD, there],
                    weights.astype(BF16),
                    preferred_element_type=F32,
                )
                if state is not None:
                    fade = jnp.exp(old_top - top)
                    total = total + fade * old_total
                    mix = mix + fade * old_mix
                new_state.append((top, total, mix))
            return tuple(new_state)

        state = visit(i, None, True)
        state = lax.fori_loop(low_ref[i], i, lambda j, s: visit(j, s, False), state)
        mixed = [mix / total for _, total, mix in state]
        out_ref[here, :] = jnp.concatenate(mixed, axis=0).T.astype(BF16)
        logs = [top + jnp.log(total) for top, total, _ in state]
        logsum_ref[0, :, here] = jnp.concatenate(logs, axis=0)
        return carry

    lax.fori_loop(0, blocks, one_row_block, 0)


def attend_forward(packed, low_blocks, begins):
    bucket, columns = packed.shape
    groups = columns // 3 // PAIR
    tall = lambda first: pl.BlockSpec((bucket, PAIR), lambda g, low: (0, first + g))
    return pl.pallas_call(
        attend_kernel,
        name="attend_forward",
        out_shape=(
            jax.ShapeDtypeStruct((bucket, columns // 3), BF16),
            jax.ShapeDtypeStruct((groups, 2, bucket), F32),
        ),
        grid_spec=pltpu.PrefetchScalarGridSpec(
            num_scalar_prefetch=1,
            grid=(groups,),
            in_specs=[
                tall(0),
                tall(groups),
                tall(2 * groups),
                pl.BlockSpec((1, bucket), lambda g, low: (0, 0)),
            ],
            out_specs=[tall(0), pl.BlockSpec((1, 2, bucket), lambda g, low: (g, 0, 0))],
            scratch_shapes=[pltpu.VMEM((PAIR, bucket), BF16)],
        ),
        cost_estimate=pl.CostEstimate(
            flops=4 * 2 * groups * bucket * bucket * HD // 2,
            bytes_accessed=bucket * columns * 3,
            transcendentals=2 * groups * bucket * bucket // 2,
        ),
    )(low_blocks, packed, packed, packed, begins)


def attend_back_kernel(
    high_ref, q_ref, k_ref, v_ref, o_ref, go_ref, begin_ref, logsum_ref, out_ref, key_t, query_t, delta
):
    blocks = q_ref.shape[0] // TILE
    half = lax.broadcasted_iota(jnp.int32, (8, PAIR), 1) // HD
    picks = (half == lax.broadcasted_iota(jnp.int32, (8, PAIR), 0)).astype(F32)
    for block in range(blocks):
        at = slice(block * TILE, (block + 1) * TILE)
        key_t[:, at] = k_ref[at, :].T
        query_t[:, at] = jnp.zeros((PAIR, TILE), F32)
        product = o_ref[at, :].astype(F32) * go_ref[at, :].astype(F32)
        delta[:, at] = lax.dot_general(
            picks,
            product,
            (((1,), (1,)), ((), ())),
            precision=lax.Precision.HIGHEST,
            preferred_element_type=F32,
        )

    def one_key_block(j, carry):
        there = pl.ds(pl.multiple_of(j * TILE, TILE), TILE)
        key_rows = k_ref[there, :]
        value_rows = v_ref[there, :]

        def visit(i, state, diagonal):
            here = pl.ds(pl.multiple_of(i * TILE, TILE), TILE)
            queries = split_pair(q_ref[here, :] * HD ** (-0.5))
            grads = split_pair(go_ref[here, :])
            allowed = allowed_in(j, i, begin_ref[:, here], diagonal)
            key_grad, value_grad = state
            for which in range(2):
                scores = against_rows(key_rows, queries[which])
                scores = jnp.where(allowed, scores, MASKED)
                probs = jnp.exp(scores - logsum_ref[0, which : which + 1, here])
                grad_probs = against_rows(value_rows, grads[which])
                grad_scores = (probs * (grad_probs - delta[which : which + 1, here])).astype(BF16)
                value_grad = value_grad + jnp.dot(
                    probs.astype(BF16), grads[which], preferred_element_type=F32
                )
                key_grad = key_grad + jnp.dot(
                    grad_scores, queries[which], preferred_element_type=F32
                )
                at = slice(which * HD, (which + 1) * HD)
                query_t[at, here] += jnp.dot(
                    key_t[at, there], grad_scores, preferred_element_type=F32
                )
            return key_grad, value_grad

        zero = jnp.zeros((TILE, PAIR), F32)
        state = visit(j, (zero, zero), True)
        state = lax.fori_loop(j + 1, high_ref[j], lambda i, s: visit(i, s, False), state)
        out_ref[1, there, :] = state[0].astype(BF16)
        out_ref[2, there, :] = state[1].astype(BF16)
        return carry

    lax.fori_loop(0, blocks, one_key_block, 0)
    for block in range(blocks):
        at = slice(block * TILE, (block + 1) * TILE)
        out_ref[0, at, :] = (query_t[:, at].T * HD ** (-0.5)).astype(BF16)


def attend_backward(packed, attended, grad_attended, logsum, high_blocks, begins):
    bucket, columns = packed.shape
    groups = columns // 3 // PAIR
    tall = lambda first: pl.BlockSpec((bucket, PAIR), lambda g, high: (0, first + g))
    return pl.pallas_call(
        attend_back_kernel,
        name="attend_backward",
        out_shape=jax.ShapeDtypeStruct((3, bucket, columns // 3), BF16),
        grid_spec=pltpu.PrefetchScalarGridSpec(
            num_scalar_prefetch=1,
            grid=(groups,),
            in_specs=[
                tall(0),
                tall(groups),
                tall(2 * groups),
                tall(0),
                tall(0),
                pl.BlockSpec((1, bucket), lambda g, high: (0, 0)),
                pl.BlockSpec((1, 2, bucket), lambda g, high: (g, 0, 0)),
            ],
            out_specs=pl.BlockSpec((3, bucket, PAIR), lambda g, high: (0, 0, g)),
            scratch_shapes=[
                pltpu.VMEM((PAIR, bucket), BF16),
                pltpu.VMEM((PAIR, bucket), F32),
                pltpu.VMEM((8, bucket), F32),
            ],
        ),
        cost_estimate=pl.CostEstimate(
            flops=10 * 2 * groups * bucket * bucket * HD // 2,
            bytes_accessed=bucket * columns * 6,
            transcendentals=2 * groups * bucket * bucket // 2,
        ),
    )(high_blocks, packed, packed, packed, attended, grad_attended, begins, logsum)


def gather_rows(shard):
    return lax.all_gather(shard, ("dp", "seq"), axis=0, tiled=True)


def scatter_sum(full):
    return lax.psum_scatter(full, ("dp", "seq"), scatter_dimension=0, tiled=True)


def local(
    tokens,
    cotangent,
    lengths,
    gain_first,
    shift_first,
    packed_weight,
    packed_bias,
    output_weight,
    output_bias,
    gain_second,
    shift_second,
    expand_weight,
    expand_bias,
    reduce_weight,
    reduce_bias,
):
    micro_count, local_rows, width = tokens.shape
    groups = lax.axis_size("seq")
    devices = groups * lax.axis_size("dp")
    share = groups // micro_count
    bucket = local_rows * groups
    hidden_width = expand_weight.shape[1]
    columns = width // share
    place = lax.axis_index("seq")
    mine, core = place // share, place % share
    swap_micro = [(s, (s + share) % groups) for s in range(groups)]
    swap_core = [(s, s ^ 1) for s in range(groups)]

    def own_micro(both):
        kept = lax.dynamic_index_in_dim(both, mine, 0, keepdims=False)
        sent = lax.dynamic_index_in_dim(both, 1 - mine, 0, keepdims=False)
        came = lax.ppermute(sent, "seq", swap_micro)
        return jnp.stack([jnp.where(mine == 0, kept, came), jnp.where(mine == 0, came, kept)])

    def home_micro(blocks):
        kept = lax.dynamic_index_in_dim(blocks, mine, 0, keepdims=False)
        sent = lax.dynamic_index_in_dim(blocks, 1 - mine, 0, keepdims=False)
        came = lax.ppermute(sent, "seq", swap_micro)
        return jnp.stack([jnp.where(mine == 0, kept, came), jnp.where(mine == 0, came, kept)])

    def interleave(own, other):
        first, second = jnp.where(core == 0, own, other), jnp.where(core == 0, other, own)
        return jnp.stack([first, second], axis=1).reshape((bucket,) + own.shape[2:])

    own_tokens = own_micro(tokens)
    own_cotangent = own_micro(cotangent)
    other_tokens = lax.ppermute(own_tokens, "seq", swap_core)

    small = jnp.concatenate(
        [gain_first, shift_first, packed_bias, output_bias, gain_second, shift_second, expand_bias, reduce_bias]
    )
    sizes = [v.shape[0] for v in (gain_first, shift_first, packed_bias, output_bias, gain_second, shift_second, expand_bias, reduce_bias)]
    extra = jnp.pad(small, (0, 8 * width - small.shape[0])).reshape(8, width)
    output_rows = output_weight.shape[0]
    full_packed = gather_rows(packed_weight)
    joined = gather_rows(jnp.concatenate([output_weight, extra])).reshape(devices, output_rows + 8, width)
    full_output = joined[:, :output_rows].reshape(width, width)
    small_all = joined[:, output_rows:].reshape(devices, 8 * width)
    full_expand = gather_rows(expand_weight)
    full_reduce = gather_rows(reduce_weight)
    pieces, at = [], 0
    for size in sizes:
        pieces.append(small_all[:, at : at + size].reshape(-1).astype(F32))
        at += size
    gain_one, shift_one, packed_shift, output_shift, gain_two, shift_two, expand_shift, reduce_shift = pieces

    places = jnp.arange(bucket, dtype=jnp.int32)
    bucket_lengths = lax.dynamic_index_in_dim(lengths, mine, 0, keepdims=False)[0]
    slot_count = lengths.shape[-1]
    ends = jnp.cumsum(bucket_lengths)
    past = (places[:, None] >= ends[None, :]).astype(jnp.int32)
    begins = jnp.sum(past * bucket_lengths[None, :], axis=1)
    low_blocks = begins[::TILE] // TILE
    block_ids = jnp.arange(bucket // TILE, dtype=jnp.int32)
    high_blocks = jnp.sum((low_blocks[None, :] <= block_ids[:, None]).astype(jnp.int32), axis=1)
    begins = begins[None, :]
    valid_all = (jnp.sum(past, axis=1) < slot_count - 1).astype(F32).reshape(2, share, local_rows)
    valid = lax.dynamic_index_in_dim(valid_all, core, 1, keepdims=False).reshape(-1, 1)

    inputs = own_tokens.reshape(-1, width).astype(F32)
    everyone = interleave(own_tokens, other_tokens).astype(F32)
    normed_low = layer_norm(everyone, gain_one, shift_one).astype(BF16)
    half_packed = lax.dynamic_index_in_dim(
        full_packed.reshape(width, 3, share, columns), core, 2, keepdims=False
    ).reshape(width, 3 * columns)
    bias_row = jnp.stack([packed_shift[:width], jnp.zeros((width,), F32), packed_shift[width:]])
    half_bias = lax.dynamic_index_in_dim(
        bias_row.reshape(3, share, columns), core, 1, keepdims=False
    ).reshape(-1)
    packed = (jnp.dot(normed_low, half_packed, preferred_element_type=F32) + half_bias).astype(BF16)
    attended_heads, logsum = attend_forward(packed, low_blocks, begins)

    by_core = attended_heads.reshape(2, share, local_rows, columns)
    kept = lax.dynamic_index_in_dim(by_core, core, 1, keepdims=False)
    came = lax.ppermute(lax.dynamic_index_in_dim(by_core, 1 - core, 1, keepdims=False), "seq", swap_core)
    attended = jnp.concatenate(
        [jnp.where(core == 0, kept, came), jnp.where(core == 0, came, kept)], axis=-1
    ).reshape(-1, width)

    middle = inputs + BRANCH_SCALE * (
        jnp.dot(attended, full_output, preferred_element_type=F32) + output_shift
    )
    normed_two, norm_back_two = jax.vjp(layer_norm, middle, gain_two, shift_two)
    normed_two_low = normed_two.astype(BF16)
    activated, gelu_back = jax.vjp(
        gelu_tanh, jnp.dot(normed_two_low, full_expand, preferred_element_type=F32) + expand_shift
    )
    active_low = activated.astype(BF16)
    branch_out = jnp.dot(active_low, full_reduce, preferred_element_type=F32) + reduce_shift
    layer_rows = ((middle + BRANCH_SCALE * branch_out) * valid).astype(BF16)

    grad_rows = own_cotangent.reshape(-1, width).astype(F32) * valid
    grad_branch = (BRANCH_SCALE * grad_rows).astype(BF16)
    reduce_weight_grad = outer_sum(active_low, grad_branch)
    reduce_bias_grad = jnp.sum(grad_branch.astype(F32), axis=0)
    (grad_hidden,) = gelu_back(against_rows(grad_branch, full_reduce))
    grad_hidden = grad_hidden.astype(BF16)
    expand_weight_grad = outer_sum(normed_two_low, grad_hidden)
    expand_bias_grad = jnp.sum(grad_hidden.astype(F32), axis=0)
    middle_part, gain_two_grad, shift_two_grad = norm_back_two(against_rows(grad_hidden, full_expand))
    grad_middle = grad_rows + middle_part
    grad_proj = (BRANCH_SCALE * grad_middle).astype(BF16)
    output_weight_grad = outer_sum(attended, grad_proj)
    output_bias_grad = jnp.sum(grad_proj.astype(F32), axis=0)
    grad_attended = against_rows(grad_proj, full_output).astype(BF16).reshape(2, local_rows, share, columns)
    kept = lax.dynamic_index_in_dim(grad_attended, core, 2, keepdims=False)
    came = lax.ppermute(
        lax.dynamic_index_in_dim(grad_attended, 1 - core, 2, keepdims=False), "seq", swap_core
    )
    grad_heads = interleave(kept, came)
    grad_packed = attend_backward(packed, attended_heads, grad_heads, logsum, high_blocks, begins)
    half_grad = jnp.stack([outer_sum(normed_low, grad_packed[part]) for part in range(3)], axis=1)
    half_sums = jnp.sum(grad_packed.astype(F32), axis=1)
    weights = half_packed.reshape(width, 3, columns)
    part_grad = sum(against_rows(grad_packed[part], weights[:, part]) for part in range(3)).astype(BF16)
    by_core = part_grad.reshape(2, share, local_rows, width)
    kept = lax.dynamic_index_in_dim(by_core, core, 1, keepdims=False)
    came = lax.ppermute(lax.dynamic_index_in_dim(by_core, 1 - core, 1, keepdims=False), "seq", swap_core)
    norm_grad = (kept.astype(F32) + came.astype(F32)).reshape(-1, width)
    _, norm_back_one = jax.vjp(layer_norm, inputs, gain_one, shift_one)
    input_part, gain_one_grad, shift_one_grad = norm_back_one(norm_grad)
    input_rows = (grad_middle + input_part).astype(BF16)

    layer_output = home_micro(layer_rows.reshape(2, local_rows, width))
    input_grad = home_micro(input_rows.reshape(2, local_rows, width))

    spread = lambda half, axis: lax.dynamic_update_index_in_dim(
        jnp.zeros(half.shape[:axis] + (share,) + half.shape[axis:], half.dtype), half, core, axis
    )
    packed_weight_grad = spread(half_grad.astype(BF16), 2).reshape(width, 3 * width)
    packed_sums = spread(half_sums, 1).reshape(3, width)
    packed_bias_grad = jnp.concatenate([packed_sums[0], packed_sums[2]])
    small_grads = [gain_one_grad, shift_one_grad, packed_bias_grad, output_bias_grad, gain_two_grad, shift_two_grad, expand_bias_grad, reduce_bias_grad]
    small_sum = scatter_sum(
        jnp.concatenate([g.reshape(devices, -1) for g in small_grads], axis=1)
    )[0]
    pieces, at = [], 0
    for size in sizes:
        pieces.append(small_sum[at : at + size])
        at += size
    big = [
        scatter_sum(g.astype(BF16)).astype(F32)
        for g in (reduce_weight_grad, expand_weight_grad, output_weight_grad, packed_weight_grad)
    ]
    return (
        layer_output,
        input_grad,
        pieces[0],
        pieces[1],
        big[3],
        pieces[2],
        big[2],
        pieces[3],
        pieces[4],
        pieces[5],
        big[1],
        pieces[6],
        big[0],
        pieces[7],
    )


def solution(mesh):
    both = ("dp", "seq")
    token_spec = P(None, both, None)
    vector, matrix = P(both), P(both, None)
    in_specs = (
        token_spec,
        token_spec,
        P(None, "dp", None),
        vector,
        vector,
        matrix,
        vector,
        matrix,
        vector,
        vector,
        vector,
        matrix,
        vector,
        matrix,
        vector,
    )
    out_specs = (
        token_spec,
        token_spec,
        vector,
        vector,
        matrix,
        vector,
        matrix,
        vector,
        vector,
        vector,
        matrix,
        vector,
        matrix,
        vector,
    )
    return jax.shard_map(local, mesh=mesh, in_specs=in_specs, out_specs=out_specs, check_vma=False)
```

```python
import functools

import jax
import jax.numpy as jnp
from jax import lax
from jax.experimental import pallas as pl
from jax.experimental.pallas import tpu as pltpu
from jax.sharding import PartitionSpec as P

H = 12
HD = 64
BRANCH_SCALE = 12 ** (-0.5)
EPSILON = 1e-05
F32 = jnp.float32
BF16 = jnp.bfloat16
TILE = 256
PAIR = 2 * HD
MASKED = -1e30


def outer_sum(first, second):
    return lax.dot_general(first, second, (((0,), (0,)), ((), ())), preferred_element_type=F32)


def against_rows(first, second):
    return lax.dot_general(first, second, (((1,), (1,)), ((), ())), preferred_element_type=F32)


def layer_norm(values, norm_gain, norm_shift):
    center = values - jnp.mean(values, axis=-1, keepdims=True)
    spread = jnp.mean(center * center, axis=-1, keepdims=True)
    return center * lax.rsqrt(spread + EPSILON) * norm_gain + norm_shift


def gelu_tanh(values):
    return jax.nn.gelu(values, approximate=True)


def split_pair(rows):
    lane = lax.broadcasted_iota(jnp.int32, rows.shape, 1)
    nothing = jnp.zeros_like(rows)
    return jnp.where(lane < HD, rows, nothing), jnp.where(lane < HD, nothing, rows)


def allowed_in(key_block, row_block, begins, diagonal):
    keys = key_block * TILE + lax.broadcasted_iota(jnp.int32, (TILE, TILE), 0)
    allowed = keys >= begins
    if diagonal:
        rows = row_block * TILE + lax.broadcasted_iota(jnp.int32, (TILE, TILE), 1)
        allowed = allowed & (keys <= rows)
    return allowed


def attend_kernel(low_ref, q_ref, k_ref, v_ref, begin_ref, out_ref, logsum_ref, value_t):
    blocks = q_ref.shape[0] // TILE
    for block in range(blocks):
        at = slice(block * TILE, (block + 1) * TILE)
        value_t[:, at] = v_ref[at, :].T

    def one_row_block(i, carry):
        here = pl.ds(pl.multiple_of(i * TILE, TILE), TILE)
        heads = split_pair(q_ref[here, :] * HD ** (-0.5))
        begins = begin_ref[:, here]

        def visit(j, state, diagonal):
            there = pl.ds(pl.multiple_of(j * TILE, TILE), TILE)
            key_rows = k_ref[there, :]
            allowed = allowed_in(j, i, begins, diagonal)
            new_state = []
            for which in range(2):
                scores = against_rows(key_rows, heads[which])
                scores = jnp.where(allowed, scores, MASKED)
                top = jnp.max(scores, axis=0, keepdims=True)
                if state is not None:
                    old_top, old_total, old_mix = state[which]
                    top = jnp.maximum(top, old_top)
                weights = jnp.exp(scores - top)
                total = jnp.sum(weights, axis=0, keepdims=True)
                mix = jnp.dot(
                    value_t[which * HD : (which + 1) * HD, there],
                    weights.astype(BF16),
                    preferred_element_type=F32,
                )
                if state is not None:
                    fade = jnp.exp(old_top - top)
                    total = total + fade * old_total
                    mix = mix + fade * old_mix
                new_state.append((top, total, mix))
            return tuple(new_state)

        state = visit(i, None, True)
        state = lax.fori_loop(low_ref[i], i, lambda j, s: visit(j, s, False), state)
        mixed = [mix / total for _, total, mix in state]
        out_ref[here, :] = jnp.concatenate(mixed, axis=0).T.astype(BF16)
        logs = [top + jnp.log(total) for top, total, _ in state]
        logsum_ref[0, :, here] = jnp.concatenate(logs, axis=0)
        return carry

    lax.fori_loop(0, blocks, one_row_block, 0)


def attend_forward(packed, low_blocks, begins):
    bucket, columns = packed.shape
    groups = columns // 3 // PAIR
    tall = lambda first: pl.BlockSpec((bucket, PAIR), lambda g, low: (0, first + g))
    return pl.pallas_call(
        attend_kernel,
        name="attend_forward",
        out_shape=(
            jax.ShapeDtypeStruct((bucket, columns // 3), BF16),
            jax.ShapeDtypeStruct((groups, 2, bucket), F32),
        ),
        grid_spec=pltpu.PrefetchScalarGridSpec(
            num_scalar_prefetch=1,
            grid=(groups,),
            in_specs=[
                tall(0),
                tall(groups),
                tall(2 * groups),
                pl.BlockSpec((1, bucket), lambda g, low: (0, 0)),
            ],
            out_specs=[tall(0), pl.BlockSpec((1, 2, bucket), lambda g, low: (g, 0, 0))],
            scratch_shapes=[pltpu.VMEM((PAIR, bucket), BF16)],
        ),
        cost_estimate=pl.CostEstimate(
            flops=4 * 2 * groups * bucket * bucket * HD // 2,
            bytes_accessed=bucket * columns * 3,
            transcendentals=2 * groups * bucket * bucket // 2,
        ),
    )(low_blocks, packed, packed, packed, begins)


def attend_back_kernel(
    high_ref, q_ref, k_ref, v_ref, o_ref, go_ref, begin_ref, logsum_ref, out_ref, key_t, query_t, delta
):
    blocks = q_ref.shape[0] // TILE
    half = lax.broadcasted_iota(jnp.int32, (8, PAIR), 1) // HD
    picks = (half == lax.broadcasted_iota(jnp.int32, (8, PAIR), 0)).astype(F32)
    for block in range(blocks):
        at = slice(block * TILE, (block + 1) * TILE)
        key_t[:, at] = k_ref[at, :].T
        query_t[:, at] = jnp.zeros((PAIR, TILE), F32)
        product = o_ref[at, :].astype(F32) * go_ref[at, :].astype(F32)
        delta[:, at] = lax.dot_general(
            picks,
            product,
            (((1,), (1,)), ((), ())),
            precision=lax.Precision.HIGHEST,
            preferred_element_type=F32,
        )

    def one_key_block(j, carry):
        there = pl.ds(pl.multiple_of(j * TILE, TILE), TILE)
        key_rows = k_ref[there, :]
        value_rows = v_ref[there, :]

        def visit(i, state, diagonal):
            here = pl.ds(pl.multiple_of(i * TILE, TILE), TILE)
            queries = split_pair(q_ref[here, :] * HD ** (-0.5))
            grads = split_pair(go_ref[here, :])
            allowed = allowed_in(j, i, begin_ref[:, here], diagonal)
            key_grad, value_grad = state
            for which in range(2):
                scores = against_rows(key_rows, queries[which])
                scores = jnp.where(allowed, scores, MASKED)
                probs = jnp.exp(scores - logsum_ref[0, which : which + 1, here])
                grad_probs = against_rows(value_rows, grads[which])
                grad_scores = (probs * (grad_probs - delta[which : which + 1, here])).astype(BF16)
                value_grad = value_grad + jnp.dot(
                    probs.astype(BF16), grads[which], preferred_element_type=F32
                )
                key_grad = key_grad + jnp.dot(
                    grad_scores, queries[which], preferred_element_type=F32
                )
                at = slice(which * HD, (which + 1) * HD)
                query_t[at, here] += jnp.dot(
                    key_t[at, there], grad_scores, preferred_element_type=F32
                )
            return key_grad, value_grad

        zero = jnp.zeros((TILE, PAIR), F32)
        state = visit(j, (zero, zero), True)
        state = lax.fori_loop(j + 1, high_ref[j], lambda i, s: visit(i, s, False), state)
        out_ref[1, there, :] = state[0].astype(BF16)
        out_ref[2, there, :] = state[1].astype(BF16)
        return carry

    lax.fori_loop(0, blocks, one_key_block, 0)
    for block in range(blocks):
        at = slice(block * TILE, (block + 1) * TILE)
        out_ref[0, at, :] = (query_t[:, at].T * HD ** (-0.5)).astype(BF16)


def attend_backward(packed, attended, grad_attended, logsum, high_blocks, begins):
    bucket, columns = packed.shape
    groups = columns // 3 // PAIR
    tall = lambda first: pl.BlockSpec((bucket, PAIR), lambda g, high: (0, first + g))
    return pl.pallas_call(
        attend_back_kernel,
        name="attend_backward",
        out_shape=jax.ShapeDtypeStruct((3, bucket, columns // 3), BF16),
        grid_spec=pltpu.PrefetchScalarGridSpec(
            num_scalar_prefetch=1,
            grid=(groups,),
            in_specs=[
                tall(0),
                tall(groups),
                tall(2 * groups),
                tall(0),
                tall(0),
                pl.BlockSpec((1, bucket), lambda g, high: (0, 0)),
                pl.BlockSpec((1, 2, bucket), lambda g, high: (g, 0, 0)),
            ],
            out_specs=pl.BlockSpec((3, bucket, PAIR), lambda g, high: (0, 0, g)),
            scratch_shapes=[
                pltpu.VMEM((PAIR, bucket), BF16),
                pltpu.VMEM((PAIR, bucket), F32),
                pltpu.VMEM((8, bucket), F32),
            ],
        ),
        cost_estimate=pl.CostEstimate(
            flops=10 * 2 * groups * bucket * bucket * HD // 2,
            bytes_accessed=bucket * columns * 6,
            transcendentals=2 * groups * bucket * bucket // 2,
        ),
    )(high_blocks, packed, packed, packed, attended, grad_attended, begins, logsum)


def gather_rows(shard):
    return lax.all_gather(shard, ("dp", "seq"), axis=0, tiled=True)


def scatter_sum(full):
    return lax.psum_scatter(full, ("dp", "seq"), scatter_dimension=0, tiled=True)


def local(
    tokens,
    cotangent,
    lengths,
    gain_first,
    shift_first,
    packed_weight,
    packed_bias,
    output_weight,
    output_bias,
    gain_second,
    shift_second,
    expand_weight,
    expand_bias,
    reduce_weight,
    reduce_bias,
):
    micro_count, local_rows, width = tokens.shape
    groups = lax.axis_size("seq")
    devices = groups * lax.axis_size("dp")
    share = groups // micro_count
    bucket = local_rows * groups
    hidden_width = expand_weight.shape[1]
    columns = width // share
    place = lax.axis_index("seq")
    mine, core = place // share, place % share
    swap_micro = [(s, (s + share) % groups) for s in range(groups)]
    swap_core = [(s, s ^ 1) for s in range(groups)]

    def own_micro(both):
        kept = lax.dynamic_index_in_dim(both, mine, 0, keepdims=False)
        sent = lax.dynamic_index_in_dim(both, 1 - mine, 0, keepdims=False)
        came = lax.ppermute(sent, "seq", swap_micro)
        return jnp.stack([jnp.where(mine == 0, kept, came), jnp.where(mine == 0, came, kept)])

    def home_micro(blocks):
        kept = lax.dynamic_index_in_dim(blocks, mine, 0, keepdims=False)
        sent = lax.dynamic_index_in_dim(blocks, 1 - mine, 0, keepdims=False)
        came = lax.ppermute(sent, "seq", swap_micro)
        return jnp.stack([jnp.where(mine == 0, kept, came), jnp.where(mine == 0, came, kept)])

    def interleave(own, other):
        first, second = jnp.where(core == 0, own, other), jnp.where(core == 0, other, own)
        return jnp.stack([first, second], axis=1).reshape((bucket,) + own.shape[2:])

    own_tokens = own_micro(tokens)
    own_cotangent = own_micro(cotangent)
    other_tokens = lax.ppermute(own_tokens, "seq", swap_core)

    vectors = (gain_first, shift_first, packed_bias, output_bias, gain_second, shift_second, expand_bias, reduce_bias)
    sizes = [v.shape[0] for v in vectors]
    small_count = sum(sizes)
    pieces_per_row = hidden_width // width
    rows = output_weight.shape[0]
    extra = jnp.pad(jnp.concatenate(vectors), (0, 8 * 3 * width - small_count)).reshape(8, 3 * width)
    first = gather_rows(jnp.concatenate([packed_weight, extra])).reshape(devices, rows + 8, 3 * width)
    expand_blocks = [expand_weight[:, j * width : (j + 1) * width] for j in range(pieces_per_row)]
    second = gather_rows(jnp.concatenate([output_weight] + expand_blocks + [reduce_weight])).reshape(devices, -1, width)
    full_packed = first[:, :rows].reshape(width, 3 * width)
    small_all = first[:, rows]
    full_output = second[:, :rows].reshape(width, width)
    full_expand = jnp.concatenate(
        [second[:, rows * (j + 1) : rows * (j + 2)].reshape(width, width) for j in range(pieces_per_row)], axis=1
    )
    full_reduce = second[:, rows * (pieces_per_row + 1) :].reshape(hidden_width, width)
    pieces, at = [], 0
    for size in sizes:
        pieces.append(small_all[:, at : at + size].reshape(-1).astype(F32))
        at += size
    gain_one, shift_one, packed_shift, output_shift, gain_two, shift_two, expand_shift, reduce_shift = pieces

    places = jnp.arange(bucket, dtype=jnp.int32)
    bucket_lengths = lax.dynamic_index_in_dim(lengths, mine, 0, keepdims=False)[0]
    slot_count = lengths.shape[-1]
    ends = jnp.cumsum(bucket_lengths)
    past = (places[:, None] >= ends[None, :]).astype(jnp.int32)
    begins = jnp.sum(past * bucket_lengths[None, :], axis=1)
    low_blocks = begins[::TILE] // TILE
    block_ids = jnp.arange(bucket // TILE, dtype=jnp.int32)
    high_blocks = jnp.sum((low_blocks[None, :] <= block_ids[:, None]).astype(jnp.int32), axis=1)
    begins = begins[None, :]
    valid_all = (jnp.sum(past, axis=1) < slot_count - 1).astype(F32).reshape(2, share, local_rows)
    valid = lax.dynamic_index_in_dim(valid_all, core, 1, keepdims=False).reshape(-1, 1)

    inputs = own_tokens.reshape(-1, width).astype(F32)
    everyone = interleave(own_tokens, other_tokens).astype(F32)
    normed_low = layer_norm(everyone, gain_one, shift_one).astype(BF16)
    half_packed = jnp.concatenate(
        [lax.dynamic_slice(full_packed, (0, part * width + core * columns), (width, columns)) for part in range(3)], axis=1
    )
    bias_row = jnp.concatenate([packed_shift[:width], jnp.zeros((width,), F32), packed_shift[width:]])
    half_bias = jnp.concatenate(
        [lax.dynamic_slice(bias_row, (part * width + core * columns,), (columns,)) for part in range(3)]
    )
    packed = (jnp.dot(normed_low, half_packed, preferred_element_type=F32) + half_bias).astype(BF16)
    attended_heads, logsum = attend_forward(packed, low_blocks, begins)

    by_core = attended_heads.reshape(2, share, local_rows, columns)
    kept = lax.dynamic_index_in_dim(by_core, core, 1, keepdims=False)
    came = lax.ppermute(lax.dynamic_index_in_dim(by_core, 1 - core, 1, keepdims=False), "seq", swap_core)
    attended = jnp.concatenate(
        [jnp.where(core == 0, kept, came), jnp.where(core == 0, came, kept)], axis=-1
    ).reshape(-1, width)

    middle = inputs + BRANCH_SCALE * (
        jnp.dot(attended, full_output, preferred_element_type=F32) + output_shift
    )
    normed_two, norm_back_two = jax.vjp(layer_norm, middle, gain_two, shift_two)
    normed_two_low = normed_two.astype(BF16)
    activated, gelu_back = jax.vjp(
        gelu_tanh, jnp.dot(normed_two_low, full_expand, preferred_element_type=F32) + expand_shift
    )
    active_low = activated.astype(BF16)
    branch_out = jnp.dot(active_low, full_reduce, preferred_element_type=F32) + reduce_shift
    layer_rows = ((middle + BRANCH_SCALE * branch_out) * valid).astype(BF16)

    grad_rows = own_cotangent.reshape(-1, width).astype(F32) * valid
    grad_branch = (BRANCH_SCALE * grad_rows).astype(BF16)
    reduce_weight_grad = outer_sum(active_low, grad_branch)
    reduce_bias_grad = jnp.sum(grad_branch.astype(F32), axis=0)
    (grad_hidden,) = gelu_back(against_rows(grad_branch, full_reduce))
    grad_hidden = grad_hidden.astype(BF16)
    expand_weight_grad = outer_sum(normed_two_low, grad_hidden)
    expand_bias_grad = jnp.sum(grad_hidden.astype(F32), axis=0)
    middle_part, gain_two_grad, shift_two_grad = norm_back_two(against_rows(grad_hidden, full_expand))
    grad_middle = grad_rows + middle_part
    grad_proj = (BRANCH_SCALE * grad_middle).astype(BF16)
    output_weight_grad = outer_sum(attended, grad_proj)
    output_bias_grad = jnp.sum(grad_proj.astype(F32), axis=0)
    expand_grads = [
        expand_weight_grad[:, j * width : (j + 1) * width].astype(BF16).reshape(devices, rows, width)
        for j in range(pieces_per_row)
    ]
    early = jnp.concatenate(
        [output_weight_grad.astype(BF16).reshape(devices, rows, width)]
        + expand_grads
        + [reduce_weight_grad.astype(BF16).reshape(devices, -1, width)],
        axis=1,
    )
    early_sum = scatter_sum(early.reshape(-1, width)).astype(F32)
    grad_attended = against_rows(grad_proj, full_output).astype(BF16).reshape(2, local_rows, share, columns)
    kept = lax.dynamic_index_in_dim(grad_attended, core, 2, keepdims=False)
    came = lax.ppermute(
        lax.dynamic_index_in_dim(grad_attended, 1 - core, 2, keepdims=False), "seq", swap_core
    )
    grad_heads = interleave(kept, came)
    grad_packed = attend_backward(packed, attended_heads, grad_heads, logsum, high_blocks, begins)
    half_grads = [outer_sum(normed_low, grad_packed[part]).astype(BF16) for part in range(3)]
    half_sums = jnp.sum(grad_packed.astype(F32), axis=1)
    part_grad = sum(
        against_rows(grad_packed[part], half_packed[:, part * columns : (part + 1) * columns]) for part in range(3)
    ).astype(BF16)
    by_core = part_grad.reshape(2, share, local_rows, width)
    kept = lax.dynamic_index_in_dim(by_core, core, 1, keepdims=False)
    came = lax.ppermute(lax.dynamic_index_in_dim(by_core, 1 - core, 1, keepdims=False), "seq", swap_core)
    norm_grad = (kept.astype(F32) + came.astype(F32)).reshape(-1, width)
    _, norm_back_one = jax.vjp(layer_norm, inputs, gain_one, shift_one)
    input_part, gain_one_grad, shift_one_grad = norm_back_one(norm_grad)
    input_rows = (grad_middle + input_part).astype(BF16)

    layer_output = home_micro(layer_rows.reshape(2, local_rows, width))
    input_grad = home_micro(input_rows.reshape(2, local_rows, width))

    def spread(half):
        nothing = jnp.zeros_like(half)
        return [jnp.where(core == place_of, half, nothing) for place_of in range(share)]

    half_places = [block for half in half_grads for block in spread(half)]
    packed_bias_grad = jnp.concatenate([block for part in (0, 2) for block in spread(half_sums[part])])
    small_grads = [gain_one_grad, shift_one_grad, packed_bias_grad, output_bias_grad, gain_two_grad, shift_two_grad, expand_bias_grad, reduce_bias_grad]
    small_rows = jnp.concatenate([g.reshape(devices, -1) for g in small_grads], axis=1).astype(BF16)
    small_rows = jnp.pad(small_rows, ((0, 0), (0, 8 * 3 * width - small_count))).reshape(devices, 8, 3 * width)
    last = jnp.concatenate(
        [jnp.concatenate(half_places, axis=1).reshape(devices, rows, 3 * width), small_rows], axis=1
    )
    last_sum = scatter_sum(last.reshape(-1, 3 * width)).astype(F32)
    small_sum = last_sum[rows]
    pieces, at = [], 0
    for size in sizes:
        pieces.append(small_sum[at : at + size])
        at += size
    expand_sum = jnp.concatenate(
        [early_sum[rows * (j + 1) : rows * (j + 2)] for j in range(pieces_per_row)], axis=1
    )
    big = (early_sum[rows * (pieces_per_row + 1) :], expand_sum, early_sum[:rows], last_sum[:rows])
    return (
        layer_output,
        input_grad,
        pieces[0],
        pieces[1],
        big[3],
        pieces[2],
        big[2],
        pieces[3],
        pieces[4],
        pieces[5],
        big[1],
        pieces[6],
        big[0],
        pieces[7],
    )


def solution(mesh):
    both = ("dp", "seq")
    token_spec = P(None, both, None)
    vector, matrix = P(both), P(both, None)
    in_specs = (
        token_spec,
        token_spec,
        P(None, "dp", None),
        vector,
        vector,
        matrix,
        vector,
        matrix,
        vector,
        vector,
        vector,
        matrix,
        vector,
        matrix,
        vector,
    )
    out_specs = (
        token_spec,
        token_spec,
        vector,
        vector,
        matrix,
        vector,
        matrix,
        vector,
        vector,
        vector,
        matrix,
        vector,
        matrix,
        vector,
    )
    return jax.shard_map(local, mesh=mesh, in_specs=in_specs, out_specs=out_specs, check_vma=False)
```

```python
import functools

import jax
import jax.numpy as jnp
from jax import lax
from jax.experimental import pallas as pl
from jax.experimental.pallas import tpu as pltpu
from jax.sharding import PartitionSpec as P

H = 12
HD = 64
BRANCH_SCALE = 12 ** (-0.5)
EPSILON = 1e-05
F32 = jnp.float32
BF16 = jnp.bfloat16
TILE = 256
PAIR = 2 * HD
MASKED = -1e30


def outer_sum(first, second):
    return lax.dot_general(first, second, (((0,), (0,)), ((), ())), preferred_element_type=F32)


def against_rows(first, second):
    return lax.dot_general(first, second, (((1,), (1,)), ((), ())), preferred_element_type=F32)


def layer_norm(values, norm_gain, norm_shift):
    center = values - jnp.mean(values, axis=-1, keepdims=True)
    spread = jnp.mean(center * center, axis=-1, keepdims=True)
    return center * lax.rsqrt(spread + EPSILON) * norm_gain + norm_shift


def gelu_tanh(values):
    return jax.nn.gelu(values, approximate=True)


def split_pair(rows):
    lane = lax.broadcasted_iota(jnp.int32, rows.shape, 1)
    nothing = jnp.zeros_like(rows)
    return jnp.where(lane < HD, rows, nothing), jnp.where(lane < HD, nothing, rows)


def allowed_in(key_block, row_block, begins, diagonal):
    keys = key_block * TILE + lax.broadcasted_iota(jnp.int32, (TILE, TILE), 0)
    allowed = keys >= begins
    if diagonal:
        rows = row_block * TILE + lax.broadcasted_iota(jnp.int32, (TILE, TILE), 1)
        allowed = allowed & (keys <= rows)
    return allowed


def attend_kernel(low_ref, q_ref, k_ref, v_ref, begin_ref, out_ref, logsum_ref, value_t):
    blocks = q_ref.shape[0] // TILE
    for block in range(blocks):
        at = slice(block * TILE, (block + 1) * TILE)
        value_t[:, at] = v_ref[at, :].T

    def one_row_block(i, carry):
        here = pl.ds(pl.multiple_of(i * TILE, TILE), TILE)
        heads = split_pair(q_ref[here, :] * HD ** (-0.5))
        begins = begin_ref[:, here]

        def visit(j, state, diagonal):
            there = pl.ds(pl.multiple_of(j * TILE, TILE), TILE)
            key_rows = k_ref[there, :]
            allowed = allowed_in(j, i, begins, diagonal)
            new_state = []
            for which in range(2):
                scores = against_rows(key_rows, heads[which])
                scores = jnp.where(allowed, scores, MASKED)
                top = jnp.max(scores, axis=0, keepdims=True)
                if state is not None:
                    old_top, old_total, old_mix = state[which]
                    top = jnp.maximum(top, old_top)
                weights = jnp.exp(scores - top)
                total = jnp.sum(weights, axis=0, keepdims=True)
                mix = jnp.dot(
                    value_t[which * HD : (which + 1) * HD, there],
                    weights.astype(BF16),
                    preferred_element_type=F32,
                )
                if state is not None:
                    fade = jnp.exp(old_top - top)
                    total = total + fade * old_total
                    mix = mix + fade * old_mix
                new_state.append((top, total, mix))
            return tuple(new_state)

        state = visit(i, None, True)
        state = lax.fori_loop(low_ref[i], i, lambda j, s: visit(j, s, False), state)
        mixed = [mix / total for _, total, mix in state]
        out_ref[here, :] = jnp.concatenate(mixed, axis=0).T.astype(BF16)
        logs = [top + jnp.log(total) for top, total, _ in state]
        logsum_ref[0, :, here] = jnp.concatenate(logs, axis=0)
        return carry

    lax.fori_loop(0, blocks, one_row_block, 0)


def attend_forward(packed, low_blocks, begins):
    bucket, columns = packed.shape
    groups = columns // 3 // PAIR
    tall = lambda part: pl.BlockSpec((bucket, PAIR), lambda g, low: (0, 3 * g + part))
    narrow = pl.BlockSpec((bucket, PAIR), lambda g, low: (0, g))
    return pl.pallas_call(
        attend_kernel,
        name="attend_forward",
        out_shape=(
            jax.ShapeDtypeStruct((bucket, columns // 3), BF16),
            jax.ShapeDtypeStruct((groups, 2, bucket), F32),
        ),
        grid_spec=pltpu.PrefetchScalarGridSpec(
            num_scalar_prefetch=1,
            grid=(groups,),
            in_specs=[
                tall(0),
                tall(1),
                tall(2),
                pl.BlockSpec((1, bucket), lambda g, low: (0, 0)),
            ],
            out_specs=[narrow, pl.BlockSpec((1, 2, bucket), lambda g, low: (g, 0, 0))],
            scratch_shapes=[pltpu.VMEM((PAIR, bucket), BF16)],
        ),
        cost_estimate=pl.CostEstimate(
            flops=4 * 2 * groups * bucket * bucket * HD // 2,
            bytes_accessed=bucket * columns * 3,
            transcendentals=2 * groups * bucket * bucket // 2,
        ),
    )(low_blocks, packed, packed, packed, begins)


def attend_back_kernel(
    high_ref, q_ref, k_ref, v_ref, o_ref, go_ref, begin_ref, logsum_ref, out_ref, key_t, query_t, delta
):
    blocks = q_ref.shape[0] // TILE
    half = lax.broadcasted_iota(jnp.int32, (8, PAIR), 1) // HD
    picks = (half == lax.broadcasted_iota(jnp.int32, (8, PAIR), 0)).astype(F32)
    for block in range(blocks):
        at = slice(block * TILE, (block + 1) * TILE)
        key_t[:, at] = k_ref[at, :].T
        query_t[:, at] = jnp.zeros((PAIR, TILE), F32)
        product = o_ref[at, :].astype(F32) * go_ref[at, :].astype(F32)
        delta[:, at] = lax.dot_general(
            picks,
            product,
            (((1,), (1,)), ((), ())),
            precision=lax.Precision.HIGHEST,
            preferred_element_type=F32,
        )

    def one_key_block(j, carry):
        there = pl.ds(pl.multiple_of(j * TILE, TILE), TILE)
        key_rows = k_ref[there, :]
        value_rows = v_ref[there, :]

        def visit(i, state, diagonal):
            here = pl.ds(pl.multiple_of(i * TILE, TILE), TILE)
            queries = split_pair(q_ref[here, :] * HD ** (-0.5))
            grads = split_pair(go_ref[here, :])
            allowed = allowed_in(j, i, begin_ref[:, here], diagonal)
            key_grad, value_grad = state
            for which in range(2):
                scores = against_rows(key_rows, queries[which])
                scores = jnp.where(allowed, scores, MASKED)
                probs = jnp.exp(scores - logsum_ref[0, which : which + 1, here])
                grad_probs = against_rows(value_rows, grads[which])
                grad_scores = (probs * (grad_probs - delta[which : which + 1, here])).astype(BF16)
                value_grad = value_grad + jnp.dot(
                    probs.astype(BF16), grads[which], preferred_element_type=F32
                )
                key_grad = key_grad + jnp.dot(
                    grad_scores, queries[which], preferred_element_type=F32
                )
                at = slice(which * HD, (which + 1) * HD)
                query_t[at, here] += jnp.dot(
                    key_t[at, there], grad_scores, preferred_element_type=F32
                )
            return key_grad, value_grad

        zero = jnp.zeros((TILE, PAIR), F32)
        state = visit(j, (zero, zero), True)
        state = lax.fori_loop(j + 1, high_ref[j], lambda i, s: visit(i, s, False), state)
        out_ref[there, PAIR : 2 * PAIR] = state[0].astype(BF16)
        out_ref[there, 2 * PAIR :] = state[1].astype(BF16)
        return carry

    lax.fori_loop(0, blocks, one_key_block, 0)
    for block in range(blocks):
        at = slice(block * TILE, (block + 1) * TILE)
        out_ref[at, :PAIR] = (query_t[:, at].T * HD ** (-0.5)).astype(BF16)


def attend_backward(packed, attended, grad_attended, logsum, high_blocks, begins):
    bucket, columns = packed.shape
    groups = columns // 3 // PAIR
    tall = lambda part: pl.BlockSpec((bucket, PAIR), lambda g, high: (0, 3 * g + part))
    narrow = pl.BlockSpec((bucket, PAIR), lambda g, high: (0, g))
    return pl.pallas_call(
        attend_back_kernel,
        name="attend_backward",
        out_shape=jax.ShapeDtypeStruct((bucket, columns), BF16),
        grid_spec=pltpu.PrefetchScalarGridSpec(
            num_scalar_prefetch=1,
            grid=(groups,),
            in_specs=[
                tall(0),
                tall(1),
                tall(2),
                narrow,
                narrow,
                pl.BlockSpec((1, bucket), lambda g, high: (0, 0)),
                pl.BlockSpec((1, 2, bucket), lambda g, high: (g, 0, 0)),
            ],
            out_specs=pl.BlockSpec((bucket, 3 * PAIR), lambda g, high: (0, g)),
            scratch_shapes=[
                pltpu.VMEM((PAIR, bucket), BF16),
                pltpu.VMEM((PAIR, bucket), F32),
                pltpu.VMEM((8, bucket), F32),
            ],
        ),
        cost_estimate=pl.CostEstimate(
            flops=10 * 2 * groups * bucket * bucket * HD // 2,
            bytes_accessed=bucket * columns * 6,
            transcendentals=2 * groups * bucket * bucket // 2,
        ),
    )(high_blocks, packed, packed, packed, attended, grad_attended, begins, logsum)


def position():
    dp, seq = lax.axis_index("dp"), lax.axis_index("seq")
    return lax.div(dp, 2), lax.rem(dp, 2), lax.div(seq, 2), lax.rem(seq, 2)


def device(z, x, y, core):
    return (2 * z + x, 2 * y + core)


def send(source, target, semaphores, index, to):
    leave, arrive = semaphores
    copy = pltpu.make_async_remote_copy(
        src_ref=source,
        dst_ref=target,
        send_sem=leave.at[index],
        recv_sem=arrive.at[index],
        device_id=to,
        device_id_type=pl.DeviceIdType.MESH,
    )
    copy.start()
    return copy


def meet(z, x, y, core):
    barrier = pltpu.get_barrier_semaphore()
    others = [device(z, 1 - x, y, core), device(z, x, 1 - y, core), device(z, x, y, 1 - core)]
    others += [device(lax.rem(z + t, 4), x, y, core) for t in (1, 2, 3)]
    for other in others:
        pl.semaphore_signal(barrier, inc=1, device_id=other, device_id_type=pl.DeviceIdType.MESH)
    pl.semaphore_wait(barrier, len(others))


def gather_kernel(token_ref, half_ref, tiny_ref, all_tokens, all_half, all_tiny, local_sem, *semaphores):
    z, x, y, core = position()
    token_sems, half_sems, tiny_sems = [semaphores[2 * i : 2 * i + 2] for i in range(3)]
    meet(z, x, y, core)
    core_twin, y_twin, x_twin = device(z, x, y, 1 - core), device(z, x, 1 - y, core), device(z, 1 - x, y, core)
    streams = [
        (half_ref.at[core], half_ref.at[1 - core], all_half, half_sems),
        (tiny_ref, tiny_ref, all_tiny, tiny_sems),
    ]
    sent = []
    local = [pltpu.make_async_copy(token_ref.at[y], all_tokens.at[y, core], local_sem.at[2])]
    for i, (mine, _, whole, _) in enumerate(streams):
        local.append(pltpu.make_async_copy(mine, whole.at[z, x, y, core], local_sem.at[i]))
    for copy in local:
        copy.start()
    swaps = [send(twins, whole.at[z, x, y, core], sems, 0, core_twin) for _, twins, whole, sems in streams]
    for copy in local[1:]:
        copy.wait()
    for copy in swaps:
        copy.wait_recv()
    sent += swaps
    own = [(whole.at[z, x, y], sems) for _, _, whole, sems in streams]
    over_y = [send(piece, piece, sems, 1, y_twin) for piece, sems in own]
    token_y = send(token_ref.at[1 - y], all_tokens.at[y, core], token_sems, 0, y_twin)
    token_own = send(token_ref.at[y], all_tokens.at[y, core], token_sems, 1, core_twin)
    along_z, over_x = {}, []

    def spread_piece(p, pieces):
        for t in (1, 2, 3):
            for i, (piece, sems) in enumerate(pieces):
                along_z[p, t, i] = send(piece, piece, sems, 1 + 3 * p + t, device(lax.rem(z + t, 4), x, y, core))
        for piece, sems in pieces:
            over_x.append(send(piece, piece, sems, 8 + 4 * p, x_twin))

    spread_piece(0, own)
    for copy in over_y:
        copy.wait_recv()
    spread_piece(1, [(whole.at[z, x, 1 - y], sems) for _, _, whole, sems in streams])
    token_y.wait_recv()
    token_next = send(all_tokens.at[1 - y, core], all_tokens.at[1 - y, core], token_sems, 2, core_twin)
    for p in (0, 1):
        row = y if p == 0 else 1 - y
        for t in (1, 2, 3):
            source = lax.rem(z + 4 - t, 4)
            for i, (_, _, whole, sems) in enumerate(streams):
                along_z[p, t, i].wait_recv()
                piece = whole.at[source, x, row]
                over_x.append(send(piece, piece, sems, 8 + 4 * p + t, x_twin))
    for copy in over_x + [token_own, token_next]:
        copy.wait_recv()
    for copy in sent + over_y + [token_y, token_own, token_next] + list(along_z.values()) + over_x:
        copy.wait_send()
    local[0].wait()


def gather_first(tokens, half_shard, tiny_shard):
    _, local_rows, width = tokens.shape
    _, rows, half_columns = half_shard.shape
    anywhere = pl.BlockSpec(memory_space=pl.ANY)
    near = pl.BlockSpec(memory_space=pltpu.VMEM)
    sems = pltpu.SemaphoreType.DMA
    return pl.pallas_call(
        gather_kernel,
        name="gather_first",
        out_shape=(
            jax.ShapeDtypeStruct((2, 2, local_rows, width), BF16),
            jax.ShapeDtypeStruct((4, 2, 2, 2, rows, half_columns), BF16),
            jax.ShapeDtypeStruct((4, 2, 2, 2, 8, 128), F32),
        ),
        in_specs=[near, near, near],
        out_specs=[anywhere, anywhere, anywhere],
        scratch_shapes=[sems((3,)), sems((3,)), sems((3,)), sems((16,)), sems((16,)), sems((16,)), sems((16,))],
        compiler_params=pltpu.CompilerParams(collective_id=1, has_side_effects=True),
    )(tokens, half_shard, tiny_shard)


def reduce_kernel(big_ref, tiny_ref, own_ref, other_ref, sum_ref, *scratch):
    z, x, y, core = position()
    meet(z, x, y, core)
    streams = []
    for i, source in enumerate((big_ref, tiny_ref)):
        streams.append((source,) + scratch[10 * i : 10 * i + 10])
    first_twin = device(z, x + (1 - core) * (1 - 2 * x), y + core * (1 - 2 * y), core)
    second_twin = device(z, x + core * (1 - 2 * x), y + (1 - core) * (1 - 2 * y), core)
    keep = (1 - core) * y + core * x
    order = (1, 2, 3, 0)
    one, two, three = {}, {}, {}
    for t in order:
        k = lax.rem(z + t, 4)
        for j in (0, 1):
            ix = (1 - core) * (1 - x) + core * j
            iy = (1 - core) * j + core * (1 - y)
            for i, (source, came_one, *_, leave, arrive) in enumerate(streams):
                one[t, j, i] = send(source.at[k, ix, iy], came_one.at[t, j], (leave, arrive), 2 * t + j, first_twin)
    for t in order:
        k = lax.rem(z + t, 4)
        for i, (source, came_one, sum_one, came_two, *_, leave, arrive) in enumerate(streams):
            for j in (0, 1):
                one[t, j, i].wait_recv()
                ix = (1 - core) * x + core * j
                iy = (1 - core) * j + core * y
                total = source[k, ix, iy].astype(F32) + came_one[t, j].astype(F32)
                sum_one[t, j] = total.astype(sum_one.dtype)
            two[t, i] = send(sum_one.at[t, 1 - keep], came_two.at[t], (leave, arrive), 8 + t, second_twin)
    for t in order:
        for i, (_, _, sum_one, came_two, sum_two, came_three, total_ref, _, leave, arrive) in enumerate(
            [(s[0], s[1], s[2], s[3], s[4], s[5], s[6], s[7], s[9], s[10]) for s in streams]
        ):
            two[t, i].wait_recv()
            total = sum_one[t, keep].astype(F32) + came_two[t].astype(F32)
            if t == 0:
                total_ref[...] = total
            else:
                sum_two[t - 1] = total.astype(sum_two.dtype)
                to = device(lax.rem(z + t, 4), x, y, core)
                three[t, i] = send(sum_two.at[t - 1], came_three.at[t - 1], (leave, arrive), 11 + t, to)
    last = []
    for i, s in enumerate(streams):
        came_three, total_ref, came_last, leave, arrive = s[5], s[6], s[7], s[9], s[10]
        for t in (1, 2, 3):
            three[t, i].wait_recv()
        total_ref[...] += sum(came_three[t].astype(F32) for t in range(3))
        rows = came_last.shape[0]
        piece = total_ref if i == 1 else total_ref.at[pl.ds(pl.multiple_of((1 - core) * rows, 8), rows)]
        last.append(send(piece, came_last, (leave, arrive), 15, device(z, x, y, 1 - core)))
    rows = own_ref.shape[0]
    own_ref[...] = streams[0][6][pl.ds(pl.multiple_of(core * rows, 8), rows)]
    for copy in last:
        copy.wait_recv()
    other_ref[...] = streams[0][7][...]
    sum_ref[...] = streams[1][6][...] + streams[1][7][...]
    for copy in list(one.values()) + list(two.values()) + list(three.values()) + last:
        copy.wait_send()


def reduce_last(big, tiny):
    rows, half_columns = big.shape[3:]
    near = pl.BlockSpec(memory_space=pltpu.VMEM)
    scratch = []
    for shape, kind, kept in (((rows, half_columns), BF16, (rows // 2, half_columns)), ((8, 128), F32, (8, 128))):
        scratch += [
            pltpu.VMEM((4, 2) + shape, kind),
            pltpu.VMEM((4, 2) + shape, kind),
            pltpu.VMEM((4,) + shape, kind),
            pltpu.VMEM((3,) + shape, kind),
            pltpu.VMEM((3,) + shape, kind),
            pltpu.VMEM(shape, F32),
            pltpu.VMEM(kept, F32),
            pltpu.SemaphoreType.DMA((1,)),
            pltpu.SemaphoreType.DMA((16,)),
            pltpu.SemaphoreType.DMA((16,)),
        ]
    return pl.pallas_call(
        reduce_kernel,
        name="reduce_last",
        out_shape=(
            jax.ShapeDtypeStruct((rows // 2, half_columns), F32),
            jax.ShapeDtypeStruct((rows // 2, half_columns), F32),
            jax.ShapeDtypeStruct((8, 128), F32),
        ),
        in_specs=[near, near],
        out_specs=[near, near, near],
        scratch_shapes=scratch,
        compiler_params=pltpu.CompilerParams(collective_id=2, has_side_effects=True),
    )(big, tiny)


def gather_rows(shard):
    return lax.all_gather(shard, ("dp", "seq"), axis=0, tiled=True)


def scatter_sum(full):
    return lax.psum_scatter(full, ("dp", "seq"), scatter_dimension=0, tiled=True)


def local(
    tokens,
    cotangent,
    lengths,
    gain_first,
    shift_first,
    packed_weight,
    packed_bias,
    output_weight,
    output_bias,
    gain_second,
    shift_second,
    expand_weight,
    expand_bias,
    reduce_weight,
    reduce_bias,
):
    micro_count, local_rows, width = tokens.shape
    groups = lax.axis_size("seq")
    devices = groups * lax.axis_size("dp")
    share = groups // micro_count
    bucket = local_rows * groups
    hidden_width = expand_weight.shape[1]
    columns = width // share
    place = lax.axis_index("seq")
    mine, core = place // share, place % share
    swap_micro = [(s, (s + share) % groups) for s in range(groups)]
    swap_core = [(s, s ^ 1) for s in range(groups)]

    def own_micro(both):
        kept = lax.dynamic_index_in_dim(both, mine, 0, keepdims=False)
        sent = lax.dynamic_index_in_dim(both, 1 - mine, 0, keepdims=False)
        came = lax.ppermute(sent, "seq", swap_micro)
        return jnp.stack([jnp.where(mine == 0, kept, came), jnp.where(mine == 0, came, kept)])

    def home_micro(blocks):
        kept = lax.dynamic_index_in_dim(blocks, mine, 0, keepdims=False)
        sent = lax.dynamic_index_in_dim(blocks, 1 - mine, 0, keepdims=False)
        came = lax.ppermute(sent, "seq", swap_micro)
        return jnp.stack([jnp.where(mine == 0, kept, came), jnp.where(mine == 0, came, kept)])

    def interleave(own, other):
        first, second = jnp.where(core == 0, own, other), jnp.where(core == 0, other, own)
        return jnp.stack([first, second], axis=1).reshape((bucket,) + own.shape[2:])

    own_cotangent = own_micro(cotangent)

    vectors = (gain_first, shift_first, packed_bias, output_bias, gain_second, shift_second, expand_bias, reduce_bias)
    sizes = [v.shape[0] for v in vectors]
    small_count = sum(sizes)
    pieces_per_row = hidden_width // width
    rows = output_weight.shape[0]
    blocks = columns // PAIR
    tiny = jnp.pad(jnp.concatenate(vectors).astype(F32), (0, 1024 - small_count)).reshape(8, 128)
    halves = jnp.stack(
        [
            jnp.concatenate(
                [
                    packed_weight[:, part * width + c * columns + g * PAIR :][:, :PAIR]
                    for g in range(blocks)
                    for part in range(3)
                ],
                axis=1,
            )
            for c in range(share)
        ]
    )
    own_kernels = devices == 32 and groups == 4
    if own_kernels:
        all_tokens, half_packed, all_tiny = gather_first(tokens, halves, tiny)
        everyone = all_tokens.reshape(bucket, width)
        own_tokens = lax.dynamic_index_in_dim(all_tokens, core, 1, keepdims=False)
        half_packed = half_packed.reshape(width, 3 * columns)
    else:
        own_tokens = own_micro(tokens)
        everyone = interleave(own_tokens, lax.ppermute(own_tokens, "seq", swap_core))
        half_packed = lax.all_gather(halves, ("dp", "seq"), axis=1, tiled=True)
        half_packed = lax.dynamic_index_in_dim(half_packed, core, 0, keepdims=False)
        all_tiny = gather_rows(tiny)
    small_all = all_tiny.reshape(devices, 1024)
    expand_blocks = [expand_weight[:, j * width : (j + 1) * width] for j in range(pieces_per_row)]
    second = gather_rows(jnp.concatenate([output_weight] + expand_blocks + [reduce_weight])).reshape(devices, -1, width)
    full_output = second[:, :rows].reshape(width, width)
    full_expand = jnp.concatenate(
        [second[:, rows * (j + 1) : rows * (j + 2)].reshape(width, width) for j in range(pieces_per_row)], axis=1
    )
    full_reduce = second[:, rows * (pieces_per_row + 1) :].reshape(hidden_width, width)
    pieces, at = [], 0
    for size in sizes:
        pieces.append(small_all[:, at : at + size].reshape(-1))
        at += size
    gain_one, shift_one, packed_shift, output_shift, gain_two, shift_two, expand_shift, reduce_shift = pieces

    places = jnp.arange(bucket, dtype=jnp.int32)
    bucket_lengths = lax.dynamic_index_in_dim(lengths, mine, 0, keepdims=False)[0]
    slot_count = lengths.shape[-1]
    ends = jnp.cumsum(bucket_lengths)
    past = (places[:, None] >= ends[None, :]).astype(jnp.int32)
    begins = jnp.sum(past * bucket_lengths[None, :], axis=1)
    low_blocks = begins[::TILE] // TILE
    block_ids = jnp.arange(bucket // TILE, dtype=jnp.int32)
    high_blocks = jnp.sum((low_blocks[None, :] <= block_ids[:, None]).astype(jnp.int32), axis=1)
    begins = begins[None, :]
    valid_all = (jnp.sum(past, axis=1) < slot_count - 1).astype(F32).reshape(2, share, local_rows)
    valid = lax.dynamic_index_in_dim(valid_all, core, 1, keepdims=False).reshape(-1, 1)

    inputs = own_tokens.reshape(-1, width).astype(F32)
    normed_low = layer_norm(everyone.astype(F32), gain_one, shift_one).astype(BF16)
    bias_row = jnp.concatenate([packed_shift[:width], jnp.zeros((width,), F32), packed_shift[width:]])
    bias_row = bias_row.reshape(3, share, blocks, PAIR)
    half_bias = jnp.swapaxes(lax.dynamic_index_in_dim(bias_row, core, 1, keepdims=False), 0, 1).reshape(-1)
    packed = (jnp.dot(normed_low, half_packed, preferred_element_type=F32) + half_bias).astype(BF16)
    attended_heads, logsum = attend_forward(packed, low_blocks, begins)

    by_core = attended_heads.reshape(2, share, local_rows, columns)
    kept = lax.dynamic_index_in_dim(by_core, core, 1, keepdims=False)
    came = lax.ppermute(lax.dynamic_index_in_dim(by_core, 1 - core, 1, keepdims=False), "seq", swap_core)
    attended = jnp.concatenate(
        [jnp.where(core == 0, kept, came), jnp.where(core == 0, came, kept)], axis=-1
    ).reshape(-1, width)

    middle = inputs + BRANCH_SCALE * (
        jnp.dot(attended, full_output, preferred_element_type=F32) + output_shift
    )
    normed_two, norm_back_two = jax.vjp(layer_norm, middle, gain_two, shift_two)
    normed_two_low = normed_two.astype(BF16)
    activated, gelu_back = jax.vjp(
        gelu_tanh, jnp.dot(normed_two_low, full_expand, preferred_element_type=F32) + expand_shift
    )
    active_low = activated.astype(BF16)
    branch_out = jnp.dot(active_low, full_reduce, preferred_element_type=F32) + reduce_shift
    layer_rows = ((middle + BRANCH_SCALE * branch_out) * valid).astype(BF16)

    grad_rows = own_cotangent.reshape(-1, width).astype(F32) * valid
    grad_branch = (BRANCH_SCALE * grad_rows).astype(BF16)
    reduce_weight_grad = outer_sum(active_low, grad_branch)
    reduce_bias_grad = jnp.sum(grad_branch.astype(F32), axis=0)
    (grad_hidden,) = gelu_back(against_rows(grad_branch, full_reduce))
    grad_hidden = grad_hidden.astype(BF16)
    expand_weight_grad = outer_sum(normed_two_low, grad_hidden)
    expand_bias_grad = jnp.sum(grad_hidden.astype(F32), axis=0)
    middle_part, gain_two_grad, shift_two_grad = norm_back_two(against_rows(grad_hidden, full_expand))
    grad_middle = grad_rows + middle_part
    grad_proj = (BRANCH_SCALE * grad_middle).astype(BF16)
    output_weight_grad = outer_sum(attended, grad_proj)
    output_bias_grad = jnp.sum(grad_proj.astype(F32), axis=0)
    expand_grads = [
        expand_weight_grad[:, j * width : (j + 1) * width].astype(BF16).reshape(devices, rows, width)
        for j in range(pieces_per_row)
    ]
    early = jnp.concatenate(
        [output_weight_grad.astype(BF16).reshape(devices, rows, width)]
        + expand_grads
        + [reduce_weight_grad.astype(BF16).reshape(devices, -1, width)],
        axis=1,
    )
    grad_attended = against_rows(grad_proj, full_output).astype(BF16).reshape(2, local_rows, share, columns)
    kept = lax.dynamic_index_in_dim(grad_attended, core, 2, keepdims=False)
    came = lax.ppermute(
        lax.dynamic_index_in_dim(grad_attended, 1 - core, 2, keepdims=False), "seq", swap_core
    )
    grad_heads, early = lax.optimization_barrier((interleave(kept, came), early))
    early_sum = scatter_sum(early.reshape(-1, width)).astype(F32)
    grad_packed = attend_backward(packed, attended_heads, grad_heads, logsum, high_blocks, begins)
    half_grad = outer_sum(normed_low, grad_packed).astype(BF16)
    half_sums = jnp.sum(grad_packed.astype(F32), axis=0).reshape(blocks, 3, PAIR)
    part_grad = against_rows(grad_packed, half_packed).astype(BF16)
    by_core = part_grad.reshape(2, share, local_rows, width)
    kept = lax.dynamic_index_in_dim(by_core, core, 1, keepdims=False)
    came = lax.ppermute(lax.dynamic_index_in_dim(by_core, 1 - core, 1, keepdims=False), "seq", swap_core)
    norm_grad = (kept.astype(F32) + came.astype(F32)).reshape(-1, width)
    _, norm_back_one = jax.vjp(layer_norm, inputs, gain_one, shift_one)
    input_part, gain_one_grad, shift_one_grad = norm_back_one(norm_grad)
    input_rows = (grad_middle + input_part).astype(BF16)

    layer_output = home_micro(layer_rows.reshape(2, local_rows, width))
    input_grad = home_micro(input_rows.reshape(2, local_rows, width))

    def spread(half):
        nothing = jnp.zeros_like(half)
        return [jnp.where(core == place_of, half, nothing) for place_of in range(share)]

    packed_bias_grad = jnp.concatenate([block for part in (0, 2) for block in spread(half_sums[:, part].reshape(-1))])
    small_grads = [gain_one_grad, shift_one_grad, packed_bias_grad, output_bias_grad, gain_two_grad, shift_two_grad, expand_bias_grad, reduce_bias_grad]
    if own_kernels:
        chips = devices // share
        small_rows = jnp.concatenate([g.reshape(chips, -1) for g in small_grads], axis=1)
        small_rows = jnp.pad(small_rows, ((0, 0), (0, 1024 - share * small_count))).reshape(4, 2, 2, 8, 128)
        own_half, other_half, small_sum = reduce_last(half_grad.reshape(4, 2, 2, share * rows, 3 * columns), small_rows)
        packed_halves = [jnp.where(core == c, own_half, other_half) for c in range(share)]
        chip_sum, at, small_sum = small_sum.reshape(-1), 0, []
        for size in sizes:
            small_sum.append(lax.dynamic_slice(chip_sum, (at + core * size,), (size,)))
            at += share * size
        small_sum = jnp.concatenate(small_sum)
    else:
        both_halves = scatter_sum(jnp.concatenate(spread(half_grad), axis=1)).astype(F32)
        packed_halves = [both_halves[:, c * 3 * columns : (c + 1) * 3 * columns] for c in range(share)]
        small_sum = scatter_sum(jnp.concatenate([g.reshape(devices, -1) for g in small_grads], axis=1))[0]
    packed_sum = jnp.concatenate(
        [
            packed_halves[c][:, (3 * g + part) * PAIR : (3 * g + part + 1) * PAIR]
            for part in range(3)
            for c in range(share)
            for g in range(blocks)
        ],
        axis=1,
    )
    pieces, at = [], 0
    for size in sizes:
        pieces.append(small_sum[at : at + size])
        at += size
    expand_sum = jnp.concatenate(
        [early_sum[rows * (j + 1) : rows * (j + 2)] for j in range(pieces_per_row)], axis=1
    )
    big = (early_sum[rows * (pieces_per_row + 1) :], expand_sum, early_sum[:rows], packed_sum)
    return (
        layer_output,
        input_grad,
        pieces[0],
        pieces[1],
        big[3],
        pieces[2],
        big[2],
        pieces[3],
        pieces[4],
        pieces[5],
        big[1],
        pieces[6],
        big[0],
        pieces[7],
    )


def solution(mesh):
    both = ("dp", "seq")
    token_spec = P(None, both, None)
    vector, matrix = P(both), P(both, None)
    in_specs = (
        token_spec,
        token_spec,
        P(None, "dp", None),
        vector,
        vector,
        matrix,
        vector,
        matrix,
        vector,
        vector,
        vector,
        matrix,
        vector,
        matrix,
        vector,
    )
    out_specs = (
        token_spec,
        token_spec,
        vector,
        vector,
        matrix,
        vector,
        matrix,
        vector,
        vector,
        vector,
        matrix,
        vector,
        matrix,
        vector,
    )
    return jax.shard_map(local, mesh=mesh, in_specs=in_specs, out_specs=out_specs, check_vma=False)
```

```python
import functools

import jax
import jax.numpy as jnp
from jax import lax
from jax.experimental import pallas as pl
from jax.experimental.pallas import tpu as pltpu
from jax.sharding import PartitionSpec as P

H = 12
HD = 64
BRANCH_SCALE = 12 ** (-0.5)
EPSILON = 1e-05
F32 = jnp.float32
BF16 = jnp.bfloat16
TILE = 256
PAIR = 2 * HD
MASKED = -1e30


def outer_sum(first, second):
    return lax.dot_general(first, second, (((0,), (0,)), ((), ())), preferred_element_type=F32)


def against_rows(first, second):
    return lax.dot_general(first, second, (((1,), (1,)), ((), ())), preferred_element_type=F32)


def layer_norm(values, norm_gain, norm_shift):
    center = values - jnp.mean(values, axis=-1, keepdims=True)
    spread = jnp.mean(center * center, axis=-1, keepdims=True)
    return center * lax.rsqrt(spread + EPSILON) * norm_gain + norm_shift


def gelu_tanh(values):
    return jax.nn.gelu(values, approximate=True)


def split_pair(rows):
    lane = lax.broadcasted_iota(jnp.int32, rows.shape, 1)
    nothing = jnp.zeros_like(rows)
    return jnp.where(lane < HD, rows, nothing), jnp.where(lane < HD, nothing, rows)


def third(packed, part, g):
    first = part * (packed.shape[1] // 3) + g * PAIR
    return slice(first, first + PAIR)


def allowed_in(key_block, row_block, begins, diagonal):
    keys = key_block * TILE + lax.broadcasted_iota(jnp.int32, (TILE, TILE), 0)
    allowed = keys >= begins
    if diagonal:
        rows = row_block * TILE + lax.broadcasted_iota(jnp.int32, (TILE, TILE), 1)
        allowed = allowed & (keys <= rows)
    return allowed


def attend_kernel(bounds_ref, packed_ref, begin_ref, out_ref, logsum_ref, value_t, held):
    blocks = packed_ref.shape[0] // TILE
    groups = out_ref.shape[1] // PAIR
    count = 2 * groups
    for g in range(groups):
        for block in range(blocks):
            at = slice(block * TILE, (block + 1) * TILE)
            value_t[g * PAIR : (g + 1) * PAIR, at] = packed_ref[at, third(packed_ref, 2, g)].T

    def one_row_block(i, carry):
        here = pl.ds(pl.multiple_of(i * TILE, TILE), TILE)
        begins = begin_ref[:, here]
        heads = []
        for g in range(groups):
            heads += split_pair(packed_ref[here, third(packed_ref, 0, g)] * HD ** (-0.5))

        def score(j, tops, masked, diagonal):
            there = pl.ds(pl.multiple_of(j * TILE, TILE), TILE)
            allowed = allowed_in(j, i, begins, diagonal) if masked else None
            new_tops = []
            for h in range(count):
                g = h // 2
                key_rows = packed_ref[there, third(packed_ref, 1, g)]
                scores = against_rows(key_rows, heads[h])
                if masked:
                    scores = jnp.where(allowed, scores, MASKED)
                held[h, there, :] = scores
                top = jnp.max(scores, axis=0, keepdims=True)
                new_tops.append(top if tops is None else jnp.maximum(top, tops[h]))
            return tuple(new_tops)

        tops = score(i, None, True, True)
        tops = lax.fori_loop(bounds_ref[0, i], bounds_ref[1, i], lambda j, s: score(j, s, True, False), tops)
        tops = lax.fori_loop(bounds_ref[1, i], i, lambda j, s: score(j, s, False, False), tops)

        def mix(j, state):
            there = pl.ds(pl.multiple_of(j * TILE, TILE), TILE)
            new_state = []
            for h in range(count):
                weights = jnp.exp(held[h, there, :] - tops[h])
                total, mixed = state[h]
                total = total + jnp.sum(weights, axis=0, keepdims=True)
                mixed = mixed + jnp.dot(
                    value_t[h * HD : (h + 1) * HD, there], weights.astype(BF16), preferred_element_type=F32
                )
                new_state.append((total, mixed))
            return tuple(new_state)

        empty = (jnp.zeros((1, TILE), F32), jnp.zeros((HD, TILE), F32))
        state = lax.fori_loop(bounds_ref[0, i], i + 1, mix, (empty,) * count)
        for g in range(groups):
            mixed = [mix / total for total, mix in state[2 * g : 2 * g + 2]]
            out_ref[here, g * PAIR : (g + 1) * PAIR] = jnp.concatenate(mixed, axis=0).T.astype(BF16)
        logs = [top + jnp.log(total) for top, (total, _) in zip(tops, state)]
        logsum_ref[:, here] = jnp.concatenate(logs, axis=0)
        return carry

    lax.fori_loop(0, blocks, one_row_block, 0)


def attend_forward(packed, low_blocks, begins):
    bucket, columns = packed.shape
    groups = columns // 3 // PAIR
    return pl.pallas_call(
        attend_kernel,
        name="attend_forward",
        out_shape=(
            jax.ShapeDtypeStruct((bucket, columns // 3), BF16),
            jax.ShapeDtypeStruct((2 * groups, bucket), F32),
        ),
        grid_spec=pltpu.PrefetchScalarGridSpec(
            num_scalar_prefetch=1,
            grid=(1,),
            in_specs=[
                pl.BlockSpec((bucket, columns), lambda g, low: (0, 0)),
                pl.BlockSpec((1, bucket), lambda g, low: (0, 0)),
            ],
            out_specs=[
                pl.BlockSpec((bucket, columns // 3), lambda g, low: (0, 0)),
                pl.BlockSpec((2 * groups, bucket), lambda g, low: (0, 0)),
            ],
            scratch_shapes=[
                pltpu.VMEM((groups * PAIR, bucket), BF16),
                pltpu.VMEM((2 * groups, bucket, TILE), F32),
            ],
        ),
        cost_estimate=pl.CostEstimate(
            flops=4 * 2 * groups * bucket * bucket * HD // 2,
            bytes_accessed=bucket * columns * 3,
            transcendentals=2 * groups * bucket * bucket // 2,
        ),
    )(low_blocks, packed, begins)


def attend_back_kernel(
    bounds_ref, packed_ref, o_ref, go_ref, begin_ref, logsum_ref, out_ref, key_t, query_t, delta
):
    blocks = packed_ref.shape[0] // TILE
    groups = o_ref.shape[1] // PAIR
    half = lax.broadcasted_iota(jnp.int32, (8, PAIR), 1) // HD
    picks = (half == lax.broadcasted_iota(jnp.int32, (8, PAIR), 0)).astype(F32)
    for g in range(groups):
        column = slice(g * PAIR, (g + 1) * PAIR)
        for block in range(blocks):
            at = slice(block * TILE, (block + 1) * TILE)
            key_t[column, at] = packed_ref[at, third(packed_ref, 1, g)].T
            query_t[column, at] = jnp.zeros((PAIR, TILE), F32)
            product = o_ref[at, column].astype(F32) * go_ref[at, column].astype(F32)
            delta[g * 8 : (g + 1) * 8, at] = lax.dot_general(
                picks,
                product,
                (((1,), (1,)), ((), ())),
                precision=lax.Precision.HIGHEST,
                preferred_element_type=F32,
            )

    def one_key_block(j, carry):
        there = pl.ds(pl.multiple_of(j * TILE, TILE), TILE)

        def visit(i, state, masked, diagonal):
            here = pl.ds(pl.multiple_of(i * TILE, TILE), TILE)
            allowed = allowed_in(j, i, begin_ref[:, here], diagonal) if masked else None
            new_state = []
            for g in range(groups):
                key_rows = packed_ref[there, third(packed_ref, 1, g)]
                value_rows = packed_ref[there, third(packed_ref, 2, g)]
                queries = split_pair(packed_ref[here, third(packed_ref, 0, g)] * HD ** (-0.5))
                grads = split_pair(go_ref[here, g * PAIR : (g + 1) * PAIR])
                key_grad, value_grad = state[g]
                for which in range(2):
                    h = 2 * g + which
                    scores = against_rows(key_rows, queries[which])
                    if masked:
                        scores = jnp.where(allowed, scores, MASKED)
                    probs = jnp.exp(scores - logsum_ref[h : h + 1, here])
                    grad_probs = against_rows(value_rows, grads[which])
                    row = 8 * g + which
                    grad_scores = (probs * (grad_probs - delta[row : row + 1, here])).astype(BF16)
                    value_grad = value_grad + jnp.dot(
                        probs.astype(BF16), grads[which], preferred_element_type=F32
                    )
                    key_grad = key_grad + jnp.dot(
                        grad_scores, queries[which], preferred_element_type=F32
                    )
                    at = slice(h * HD, (h + 1) * HD)
                    query_t[at, here] += jnp.dot(
                        key_t[at, there], grad_scores, preferred_element_type=F32
                    )
                new_state.append((key_grad, value_grad))
            return tuple(new_state)

        zero = jnp.zeros((TILE, PAIR), F32)
        state = visit(j, ((zero, zero),) * groups, True, True)
        state = lax.fori_loop(j + 1, bounds_ref[1, j], lambda i, s: visit(i, s, False, False), state)
        state = lax.fori_loop(bounds_ref[1, j], bounds_ref[0, j], lambda i, s: visit(i, s, True, False), state)
        for g in range(groups):
            out_ref[there, third(packed_ref, 1, g)] = state[g][0].astype(BF16)
            out_ref[there, third(packed_ref, 2, g)] = state[g][1].astype(BF16)
        return carry

    lax.fori_loop(0, blocks, one_key_block, 0)
    for g in range(groups):
        for block in range(blocks):
            at = slice(block * TILE, (block + 1) * TILE)
            rows = query_t[g * PAIR : (g + 1) * PAIR, at].T * HD ** (-0.5)
            out_ref[at, third(packed_ref, 0, g)] = rows.astype(BF16)


def attend_backward(packed, attended, grad_attended, logsum, high_blocks, begins):
    bucket, columns = packed.shape
    groups = columns // 3 // PAIR
    whole = lambda rows, width: pl.BlockSpec((rows, width), lambda g, high: (0, 0))
    return pl.pallas_call(
        attend_back_kernel,
        name="attend_backward",
        out_shape=jax.ShapeDtypeStruct((bucket, columns), BF16),
        grid_spec=pltpu.PrefetchScalarGridSpec(
            num_scalar_prefetch=1,
            grid=(1,),
            in_specs=[
                whole(bucket, columns),
                whole(bucket, columns // 3),
                whole(bucket, columns // 3),
                whole(1, bucket),
                whole(2 * groups, bucket),
            ],
            out_specs=whole(bucket, columns),
            scratch_shapes=[
                pltpu.VMEM((groups * PAIR, bucket), BF16),
                pltpu.VMEM((groups * PAIR, bucket), F32),
                pltpu.VMEM((groups * 8, bucket), F32),
            ],
        ),
        cost_estimate=pl.CostEstimate(
            flops=10 * 2 * groups * bucket * bucket * HD // 2,
            bytes_accessed=bucket * columns * 6,
            transcendentals=2 * groups * bucket * bucket // 2,
        ),
    )(high_blocks, packed, attended, grad_attended, begins, logsum)


def position():
    dp, seq = lax.axis_index("dp"), lax.axis_index("seq")
    return lax.div(dp, 2), lax.rem(dp, 2), lax.div(seq, 2), lax.rem(seq, 2)


def device(z, x, y, core):
    return (2 * z + x, 2 * y + core)


def send(source, target, semaphores, index, to):
    leave, arrive = semaphores
    copy = pltpu.make_async_remote_copy(
        src_ref=source,
        dst_ref=target,
        send_sem=leave.at[index],
        recv_sem=arrive.at[index],
        device_id=to,
        device_id_type=pl.DeviceIdType.MESH,
    )
    copy.start()
    return copy


def meet(z, x, y, core):
    barrier = pltpu.get_barrier_semaphore()
    others = [device(z, 1 - x, y, core), device(z, x, 1 - y, core), device(z, x, y, 1 - core)]
    others += [device(lax.rem(z + t, 4), x, y, core) for t in (1, 2, 3)]
    for other in others:
        pl.semaphore_signal(barrier, inc=1, device_id=other, device_id_type=pl.DeviceIdType.MESH)
    pl.semaphore_wait(barrier, len(others))


def gather_kernel(
    token_ref, cotangent_ref, weight_ref, tiny_ref, all_tokens, all_cotangent, all_half, all_tiny, local_sem, *semaphores
):
    z, x, y, core = position()
    token_sems, half_sems, tiny_sems = [semaphores[2 * i : 2 * i + 2] for i in range(3)]
    meet(z, x, y, core)
    core_twin, y_twin, x_twin = device(z, x, y, 1 - core), device(z, x, 1 - y, core), device(z, 1 - x, y, core)
    columns = all_half.shape[5] // 3

    def weight_part(part, c):
        first = pl.multiple_of(part * 2 * columns + c * columns, PAIR)
        return weight_ref.at[:, pl.ds(first, columns)]

    streams = [(all_half, half_sems), (all_tiny, tiny_sems)]
    sent = []
    local = [
        pltpu.make_async_copy(token_ref.at[y], all_tokens.at[y, core], local_sem.at[0]),
        pltpu.make_async_copy(cotangent_ref.at[y], all_cotangent.at[y], local_sem.at[1]),
        pltpu.make_async_copy(tiny_ref, all_tiny.at[z, x, y, core], local_sem.at[2]),
    ]
    swaps = [send(tiny_ref, all_tiny.at[z, x, y, core], tiny_sems, 0, core_twin)]
    for part in range(3):
        mine = all_half.at[z, x, y, core, :, part * columns : (part + 1) * columns]
        local.append(pltpu.make_async_copy(weight_part(part, core), mine, local_sem.at[3 + part]))
        swaps.append(send(weight_part(part, 1 - core), mine, half_sems, (0, 16, 17)[part], core_twin))
    for copy in local[2:] + local[:2]:
        copy.start()
    for copy in local[2:]:
        copy.wait()
    for copy in swaps:
        copy.wait_recv()
    sent += swaps
    own = [(whole.at[z, x, y], sems) for whole, sems in streams]
    over_y = [send(piece, piece, sems, 1, y_twin) for piece, sems in own]
    token_y = send(token_ref.at[1 - y], all_tokens.at[y, core], token_sems, 0, y_twin)
    cotangent_y = send(cotangent_ref.at[1 - y], all_cotangent.at[y], token_sems, 3, y_twin)
    token_own = send(token_ref.at[y], all_tokens.at[y, core], token_sems, 1, core_twin)
    along_z, over_x = {}, []

    def spread_piece(p, pieces):
        for t in (1, 2, 3):
            for i, (piece, sems) in enumerate(pieces):
                along_z[p, t, i] = send(piece, piece, sems, 1 + 3 * p + t, device(lax.rem(z + t, 4), x, y, core))
        for piece, sems in pieces:
            over_x.append(send(piece, piece, sems, 8 + 4 * p, x_twin))

    spread_piece(0, own)
    for copy in over_y:
        copy.wait_recv()
    spread_piece(1, [(whole.at[z, x, 1 - y], sems) for whole, sems in streams])
    token_y.wait_recv()
    token_next = send(all_tokens.at[1 - y, core], all_tokens.at[1 - y, core], token_sems, 2, core_twin)
    for p in (0, 1):
        row = y if p == 0 else 1 - y
        for t in (1, 2, 3):
            source = lax.rem(z + 4 - t, 4)
            for i, (whole, sems) in enumerate(streams):
                along_z[p, t, i].wait_recv()
                piece = whole.at[source, x, row]
                over_x.append(send(piece, piece, sems, 8 + 4 * p + t, x_twin))
    for copy in over_x + [token_own, token_next, cotangent_y]:
        copy.wait_recv()
    for copy in sent + over_y + [token_y, token_own, token_next, cotangent_y] + list(along_z.values()) + over_x:
        copy.wait_send()
    local[0].wait()
    local[1].wait()


def gather_first(tokens, cotangent, weight, tiny):
    _, local_rows, width = tokens.shape
    rows, columns = weight.shape
    anywhere = pl.BlockSpec(memory_space=pl.ANY)
    near = pl.BlockSpec(memory_space=pltpu.VMEM)
    sems = pltpu.SemaphoreType.DMA
    return pl.pallas_call(
        gather_kernel,
        name="gather_first",
        out_shape=(
            jax.ShapeDtypeStruct((2, 2, local_rows, width), BF16),
            jax.ShapeDtypeStruct((2, local_rows, width), BF16),
            jax.ShapeDtypeStruct((4, 2, 2, 2, rows, columns // 2), BF16),
            jax.ShapeDtypeStruct((4, 2, 2, 2, 8, 128), F32),
        ),
        in_specs=[near] * 4,
        out_specs=[anywhere] * 4,
        scratch_shapes=[sems((6,)), sems((4,)), sems((4,)), sems((18,)), sems((18,)), sems((16,)), sems((16,))],
        compiler_params=pltpu.CompilerParams(collective_id=1, has_side_effects=True),
    )(tokens, cotangent, weight, tiny)


def reduce_kernel(big_ref, tiny_ref, own_ref, other_ref, sum_ref, *scratch):
    z, x, y, core = position()
    meet(z, x, y, core)
    streams = []
    for i, source in enumerate((big_ref, tiny_ref)):
        streams.append((source,) + scratch[10 * i : 10 * i + 10])
    first_twin = device(z, x + (1 - core) * (1 - 2 * x), y + core * (1 - 2 * y), core)
    second_twin = device(z, x + core * (1 - 2 * x), y + (1 - core) * (1 - 2 * y), core)
    keep = (1 - core) * y + core * x
    order = (1, 2, 3, 0)
    one, two, three = {}, {}, {}
    for t in order:
        k = lax.rem(z + t, 4)
        for j in (0, 1):
            ix = (1 - core) * (1 - x) + core * j
            iy = (1 - core) * j + core * (1 - y)
            for i, (source, came_one, *_, leave, arrive) in enumerate(streams):
                one[t, j, i] = send(source.at[k, ix, iy], came_one.at[t, j], (leave, arrive), 2 * t + j, first_twin)
    for t in order:
        k = lax.rem(z + t, 4)
        for i, (source, came_one, sum_one, came_two, *_, leave, arrive) in enumerate(streams):
            for j in (0, 1):
                one[t, j, i].wait_recv()
                ix = (1 - core) * x + core * j
                iy = (1 - core) * j + core * y
                total = source[k, ix, iy].astype(F32) + came_one[t, j].astype(F32)
                sum_one[t, j] = total.astype(sum_one.dtype)
            two[t, i] = send(sum_one.at[t, 1 - keep], came_two.at[t], (leave, arrive), 8 + t, second_twin)
    for t in order:
        for i, (_, _, sum_one, came_two, sum_two, came_three, total_ref, _, leave, arrive) in enumerate(
            [(s[0], s[1], s[2], s[3], s[4], s[5], s[6], s[7], s[9], s[10]) for s in streams]
        ):
            two[t, i].wait_recv()
            total = sum_one[t, keep].astype(F32) + came_two[t].astype(F32)
            if t == 0:
                total_ref[...] = total
            else:
                sum_two[t - 1] = total.astype(sum_two.dtype)
                to = device(lax.rem(z + t, 4), x, y, core)
                three[t, i] = send(sum_two.at[t - 1], came_three.at[t - 1], (leave, arrive), 11 + t, to)
    last = []
    for i, s in enumerate(streams):
        came_three, total_ref, came_last, leave, arrive = s[5], s[6], s[7], s[9], s[10]
        for t in (1, 2, 3):
            three[t, i].wait_recv()
        total_ref[...] += sum(came_three[t].astype(F32) for t in range(3))
        rows = came_last.shape[0]
        piece = total_ref.at[pl.ds(pl.multiple_of((1 - core) * rows, 8), rows)]
        last.append(send(piece, came_last, (leave, arrive), 15, device(z, x, y, 1 - core)))
    rows = own_ref.shape[0]
    own_ref[...] = streams[0][6][pl.ds(pl.multiple_of(core * rows, 8), rows)]
    for copy in last:
        copy.wait_recv()
    other_ref[...] = streams[0][7][...]
    sum_ref[...] = streams[1][6][pl.ds(pl.multiple_of(core * 8, 8), 8)] + streams[1][7][...]
    for copy in list(one.values()) + list(two.values()) + list(three.values()) + last:
        copy.wait_send()


def reduce_last(big, tiny):
    rows, half_columns = big.shape[3:]
    near = pl.BlockSpec(memory_space=pltpu.VMEM)
    scratch = []
    for shape, kind, kept in (((rows, half_columns), BF16, (rows // 2, half_columns)), ((16, 128), F32, (8, 128))):
        scratch += [
            pltpu.VMEM((4, 2) + shape, kind),
            pltpu.VMEM((4, 2) + shape, kind),
            pltpu.VMEM((4,) + shape, kind),
            pltpu.VMEM((3,) + shape, kind),
            pltpu.VMEM((3,) + shape, kind),
            pltpu.VMEM(shape, F32),
            pltpu.VMEM(kept, F32),
            pltpu.SemaphoreType.DMA((1,)),
            pltpu.SemaphoreType.DMA((16,)),
            pltpu.SemaphoreType.DMA((16,)),
        ]
    return pl.pallas_call(
        reduce_kernel,
        name="reduce_last",
        out_shape=(
            jax.ShapeDtypeStruct((rows // 2, half_columns), F32),
            jax.ShapeDtypeStruct((rows // 2, half_columns), F32),
            jax.ShapeDtypeStruct((8, 128), F32),
        ),
        in_specs=[near, near],
        out_specs=[near, near, near],
        scratch_shapes=scratch,
        compiler_params=pltpu.CompilerParams(collective_id=2, has_side_effects=True),
    )(big, tiny)


def gather_rows(shard):
    return lax.all_gather(shard, ("dp", "seq"), axis=0, tiled=True)


def scatter_sum(full):
    return lax.psum_scatter(full, ("dp", "seq"), scatter_dimension=0, tiled=True)


def local(
    tokens,
    cotangent,
    lengths,
    gain_first,
    shift_first,
    packed_weight,
    packed_bias,
    output_weight,
    output_bias,
    gain_second,
    shift_second,
    expand_weight,
    expand_bias,
    reduce_weight,
    reduce_bias,
):
    micro_count, local_rows, width = tokens.shape
    groups = lax.axis_size("seq")
    devices = groups * lax.axis_size("dp")
    share = groups // micro_count
    bucket = local_rows * groups
    hidden_width = expand_weight.shape[1]
    columns = width // share
    place = lax.axis_index("seq")
    mine, core = place // share, place % share
    swap_micro = [(s, (s + share) % groups) for s in range(groups)]
    swap_core = [(s, s ^ 1) for s in range(groups)]

    def own_micro(both):
        kept = lax.dynamic_index_in_dim(both, mine, 0, keepdims=False)
        sent = lax.dynamic_index_in_dim(both, 1 - mine, 0, keepdims=False)
        came = lax.ppermute(sent, "seq", swap_micro)
        return jnp.stack([jnp.where(mine == 0, kept, came), jnp.where(mine == 0, came, kept)])

    def home_micro(blocks):
        kept = lax.dynamic_index_in_dim(blocks, mine, 0, keepdims=False)
        sent = lax.dynamic_index_in_dim(blocks, 1 - mine, 0, keepdims=False)
        came = lax.ppermute(sent, "seq", swap_micro)
        return jnp.stack([jnp.where(mine == 0, kept, came), jnp.where(mine == 0, came, kept)])

    def interleave(own, other):
        first, second = jnp.where(core == 0, own, other), jnp.where(core == 0, other, own)
        return jnp.stack([first, second], axis=1).reshape((bucket,) + own.shape[2:])


    vectors = (gain_first, shift_first, packed_bias, output_bias, gain_second, shift_second, expand_bias, reduce_bias)
    sizes = [v.shape[0] for v in vectors]
    small_count = sum(sizes)
    pieces_per_row = hidden_width // width
    rows = output_weight.shape[0]
    tiny = jnp.concatenate([jnp.pad(v.astype(F32), (0, 128 - v.shape[0])) for v in vectors]).reshape(8, 128)
    own_kernels = devices == 32 and groups == 4
    if own_kernels:
        all_tokens, own_cotangent, half_packed, all_tiny = gather_first(tokens, cotangent, packed_weight, tiny)
        everyone = all_tokens.reshape(bucket, width)
        own_tokens = lax.dynamic_index_in_dim(all_tokens, core, 1, keepdims=False)
        half_packed = half_packed.reshape(width, 3 * columns)
    else:
        own_tokens, own_cotangent = own_micro(tokens), own_micro(cotangent)
        everyone = interleave(own_tokens, lax.ppermute(own_tokens, "seq", swap_core))
        full_packed = gather_rows(packed_weight)
        half_packed = jnp.concatenate(
            [lax.dynamic_slice(full_packed, (0, part * width + core * columns), (width, columns)) for part in range(3)], axis=1
        )
        all_tiny = gather_rows(tiny)
    small_all = all_tiny.reshape(devices, 8, 128)
    expand_blocks = [expand_weight[:, j * width : (j + 1) * width] for j in range(pieces_per_row)]
    second_shard = jnp.concatenate([output_weight] + expand_blocks + [reduce_weight])
    small_all, second_shard = lax.optimization_barrier((small_all, second_shard))
    second = gather_rows(second_shard).reshape(devices, -1, width)
    full_output = second[:, :rows].reshape(width, width)
    full_expand = jnp.concatenate(
        [second[:, rows * (j + 1) : rows * (j + 2)].reshape(width, width) for j in range(pieces_per_row)], axis=1
    )
    full_reduce = second[:, rows * (pieces_per_row + 1) :].reshape(hidden_width, width)
    pieces = [small_all[:, i, :size].reshape(-1) for i, size in enumerate(sizes)]
    gain_one, shift_one, packed_shift, output_shift, gain_two, shift_two, expand_shift, reduce_shift = pieces

    places = jnp.arange(bucket, dtype=jnp.int32)
    bucket_lengths = lax.dynamic_index_in_dim(lengths, mine, 0, keepdims=False)[0]
    slot_count = lengths.shape[-1]
    ends = jnp.cumsum(bucket_lengths)
    past = (places[:, None] >= ends[None, :]).astype(jnp.int32)
    begins = jnp.sum(past * bucket_lengths[None, :], axis=1)
    block_ids = jnp.arange(bucket // TILE, dtype=jnp.int32)
    first_begin, last_begin = begins[::TILE], begins[TILE - 1 :: TILE]
    low = first_begin // TILE
    low_blocks = jnp.stack([low, jnp.minimum(-(-last_begin // TILE), block_ids)])
    high = jnp.sum((low[None, :] <= block_ids[:, None]).astype(jnp.int32), axis=1)
    free = jnp.sum((last_begin[None, :] <= block_ids[:, None] * TILE).astype(jnp.int32), axis=1)
    high_blocks = jnp.stack([high, jnp.clip(free, block_ids + 1, high)])
    begins = begins[None, :]
    valid_all = (jnp.sum(past, axis=1) < slot_count - 1).astype(F32).reshape(2, share, local_rows)
    valid = lax.dynamic_index_in_dim(valid_all, core, 1, keepdims=False).reshape(-1, 1)

    inputs = own_tokens.reshape(-1, width).astype(F32)
    normed_low = layer_norm(everyone.astype(F32), gain_one, shift_one).astype(BF16)
    bias_row = jnp.concatenate([packed_shift[:width], jnp.zeros((width,), F32), packed_shift[width:]])
    half_bias = jnp.concatenate(
        [lax.dynamic_slice(bias_row, (part * width + core * columns,), (columns,)) for part in range(3)]
    )
    packed = (jnp.dot(normed_low, half_packed, preferred_element_type=F32) + half_bias).astype(BF16)
    attended_heads, logsum = attend_forward(packed, low_blocks, begins)

    by_core = attended_heads.reshape(2, share, local_rows, columns)
    kept = lax.dynamic_index_in_dim(by_core, core, 1, keepdims=False)
    came = lax.ppermute(lax.dynamic_index_in_dim(by_core, 1 - core, 1, keepdims=False), "seq", swap_core)
    attended = jnp.concatenate(
        [jnp.where(core == 0, kept, came), jnp.where(core == 0, came, kept)], axis=-1
    ).reshape(-1, width)

    middle = inputs + BRANCH_SCALE * (
        jnp.dot(attended, full_output, preferred_element_type=F32) + output_shift
    )
    normed_two, norm_back_two = jax.vjp(layer_norm, middle, gain_two, shift_two)
    normed_two_low = normed_two.astype(BF16)
    activated, gelu_back = jax.vjp(
        gelu_tanh, jnp.dot(normed_two_low, full_expand, preferred_element_type=F32) + expand_shift
    )
    active_low = activated.astype(BF16)
    branch_out = jnp.dot(active_low, full_reduce, preferred_element_type=F32) + reduce_shift
    layer_rows = ((middle + BRANCH_SCALE * branch_out) * valid).astype(BF16)

    grad_rows = own_cotangent.reshape(-1, width).astype(F32) * valid
    grad_branch = (BRANCH_SCALE * grad_rows).astype(BF16)
    reduce_weight_grad = outer_sum(active_low, grad_branch)
    reduce_bias_grad = jnp.sum(grad_branch.astype(F32), axis=0)
    (grad_hidden,) = gelu_back(against_rows(grad_branch, full_reduce))
    grad_hidden = grad_hidden.astype(BF16)
    expand_weight_grad = outer_sum(normed_two_low, grad_hidden)
    expand_bias_grad = jnp.sum(grad_hidden.astype(F32), axis=0)
    middle_part, gain_two_grad, shift_two_grad = norm_back_two(against_rows(grad_hidden, full_expand))
    grad_middle = grad_rows + middle_part
    grad_proj = (BRANCH_SCALE * grad_middle).astype(BF16)
    output_weight_grad = outer_sum(attended, grad_proj)
    output_bias_grad = jnp.sum(grad_proj.astype(F32), axis=0)
    expand_grads = [
        expand_weight_grad[:, j * width : (j + 1) * width].astype(BF16).reshape(devices, rows, width)
        for j in range(pieces_per_row)
    ]
    early = jnp.concatenate(
        [output_weight_grad.astype(BF16).reshape(devices, rows, width)]
        + expand_grads
        + [reduce_weight_grad.astype(BF16).reshape(devices, -1, width)],
        axis=1,
    )
    grad_attended = against_rows(grad_proj, full_output).astype(BF16)
    take = lambda c: lax.dynamic_slice(grad_attended, (0, c * columns), (2 * local_rows, columns))
    kept = take(core).reshape(2, local_rows, columns)
    came = lax.ppermute(take(1 - core), "seq", swap_core).reshape(2, local_rows, columns)
    grad_heads, early = lax.optimization_barrier((interleave(kept, came), early))
    early_sum = scatter_sum(early.reshape(-1, width)).astype(F32)
    grad_packed = attend_backward(packed, attended_heads, grad_heads, logsum, high_blocks, begins)
    half_grad = outer_sum(normed_low, grad_packed).astype(BF16)
    half_sums = jnp.sum(grad_packed.astype(F32), axis=0).reshape(3, columns)
    part_grad = against_rows(grad_packed, half_packed).astype(BF16)
    by_core = part_grad.reshape(2, share, local_rows, width)
    kept = lax.dynamic_index_in_dim(by_core, core, 1, keepdims=False)
    came = lax.ppermute(lax.dynamic_index_in_dim(by_core, 1 - core, 1, keepdims=False), "seq", swap_core)
    norm_grad = (kept.astype(F32) + came.astype(F32)).reshape(-1, width)
    _, norm_back_one = jax.vjp(layer_norm, inputs, gain_one, shift_one)
    input_part, gain_one_grad, shift_one_grad = norm_back_one(norm_grad)
    input_rows = (grad_middle + input_part).astype(BF16)

    layer_output = home_micro(layer_rows.reshape(2, local_rows, width))
    input_grad = home_micro(input_rows.reshape(2, local_rows, width))

    def spread(half):
        nothing = jnp.zeros_like(half)
        return [jnp.where(core == place_of, half, nothing) for place_of in range(share)]

    packed_bias_grad = jnp.concatenate([block for part in (0, 2) for block in spread(half_sums[part])])
    small_grads = [gain_one_grad, shift_one_grad, packed_bias_grad, output_bias_grad, gain_two_grad, shift_two_grad, expand_bias_grad, reduce_bias_grad]
    if own_kernels:
        small_rows = jnp.stack(
            [jnp.pad(g.reshape(devices, -1), ((0, 0), (0, 128 - g.size // devices))) for g in small_grads], axis=1
        ).reshape(4, 2, 2, share * 8, 128)
        own_half, other_half, small_sum = reduce_last(half_grad.reshape(4, 2, 2, share * rows, 3 * columns), small_rows)
        packed_halves = [jnp.where(core == c, own_half, other_half) for c in range(share)]
        pieces = [small_sum[i, :size] for i, size in enumerate(sizes)]
    else:
        both_halves = scatter_sum(jnp.concatenate(spread(half_grad), axis=1)).astype(F32)
        packed_halves = [both_halves[:, c * 3 * columns : (c + 1) * 3 * columns] for c in range(share)]
        small_sum = scatter_sum(jnp.concatenate([g.reshape(devices, -1) for g in small_grads], axis=1))[0]
        pieces, at = [], 0
        for size in sizes:
            pieces.append(small_sum[at : at + size])
            at += size
    packed_sum = jnp.concatenate(
        [
            packed_halves[c][:, part * columns : (part + 1) * columns]
            for part in range(3)
            for c in range(share)
        ],
        axis=1,
    )
    expand_sum = jnp.concatenate(
        [early_sum[rows * (j + 1) : rows * (j + 2)] for j in range(pieces_per_row)], axis=1
    )
    big = (early_sum[rows * (pieces_per_row + 1) :], expand_sum, early_sum[:rows], packed_sum)
    return (
        layer_output,
        input_grad,
        pieces[0],
        pieces[1],
        big[3],
        pieces[2],
        big[2],
        pieces[3],
        pieces[4],
        pieces[5],
        big[1],
        pieces[6],
        big[0],
        pieces[7],
    )


def solution(mesh):
    both = ("dp", "seq")
    token_spec = P(None, both, None)
    vector, matrix = P(both), P(both, None)
    in_specs = (
        token_spec,
        token_spec,
        P(None, "dp", None),
        vector,
        vector,
        matrix,
        vector,
        matrix,
        vector,
        vector,
        vector,
        matrix,
        vector,
        matrix,
        vector,
    )
    out_specs = (
        token_spec,
        token_spec,
        vector,
        vector,
        matrix,
        vector,
        matrix,
        vector,
        vector,
        vector,
        matrix,
        vector,
        matrix,
        vector,
    )
    return jax.shard_map(local, mesh=mesh, in_specs=in_specs, out_specs=out_specs, check_vma=False)
```

```python
import functools

import jax
import jax.numpy as jnp
from jax import lax
from jax.experimental import pallas as pl
from jax.experimental.pallas import tpu as pltpu
from jax.sharding import PartitionSpec as P

H = 12
HD = 64
BRANCH_SCALE = 12 ** (-0.5)
EPSILON = 1e-05
F32 = jnp.float32
BF16 = jnp.bfloat16
TILE = 256
PAIR = 2 * HD
MASKED = -1e30


def outer_sum(first, second):
    return lax.dot_general(first, second, (((0,), (0,)), ((), ())), preferred_element_type=F32)


def against_rows(first, second):
    return lax.dot_general(first, second, (((1,), (1,)), ((), ())), preferred_element_type=F32)


def layer_norm(values, norm_gain, norm_shift):
    center = values - jnp.mean(values, axis=-1, keepdims=True)
    spread = jnp.mean(center * center, axis=-1, keepdims=True)
    return center * lax.rsqrt(spread + EPSILON) * norm_gain + norm_shift


def gelu_tanh(values):
    return jax.nn.gelu(values, approximate=True)


def split_pair(rows):
    lane = lax.broadcasted_iota(jnp.int32, rows.shape, 1)
    nothing = jnp.zeros_like(rows)
    return jnp.where(lane < HD, rows, nothing), jnp.where(lane < HD, nothing, rows)


def third(packed, part, g):
    first = part * (packed.shape[1] // 3) + g * PAIR
    return slice(first, first + PAIR)


def allowed_in(key_block, row_block, begins, diagonal):
    keys = key_block * TILE + lax.broadcasted_iota(jnp.int32, (TILE, TILE), 0)
    allowed = keys >= begins
    if diagonal:
        rows = row_block * TILE + lax.broadcasted_iota(jnp.int32, (TILE, TILE), 1)
        allowed = allowed & (keys <= rows)
    return allowed


def attend_kernel(bounds_ref, packed_ref, begin_ref, out_ref, logsum_ref, value_t, held):
    blocks = packed_ref.shape[0] // TILE
    groups = out_ref.shape[1] // PAIR
    count = 2 * groups
    for g in range(groups):
        for block in range(blocks):
            at = slice(block * TILE, (block + 1) * TILE)
            value_t[g * PAIR : (g + 1) * PAIR, at] = packed_ref[at, third(packed_ref, 2, g)].T

    def one_row_block(i, carry):
        here = pl.ds(pl.multiple_of(i * TILE, TILE), TILE)
        begins = begin_ref[:, here]
        heads = []
        for g in range(groups):
            heads += split_pair(packed_ref[here, third(packed_ref, 0, g)] * HD ** (-0.5))

        def score(j, tops, masked, diagonal):
            there = pl.ds(pl.multiple_of(j * TILE, TILE), TILE)
            allowed = allowed_in(j, i, begins, diagonal) if masked else None
            new_tops = []
            for h in range(count):
                g = h // 2
                key_rows = packed_ref[there, third(packed_ref, 1, g)]
                scores = against_rows(key_rows, heads[h])
                if masked:
                    scores = jnp.where(allowed, scores, MASKED)
                held[h, there, :] = scores
                top = jnp.max(scores, axis=0, keepdims=True)
                new_tops.append(top if tops is None else jnp.maximum(top, tops[h]))
            return tuple(new_tops)

        tops = score(i, None, True, True)
        tops = lax.fori_loop(bounds_ref[0, i], bounds_ref[1, i], lambda j, s: score(j, s, True, False), tops)
        tops = lax.fori_loop(bounds_ref[1, i], i, lambda j, s: score(j, s, False, False), tops)

        def mix(j, state):
            there = pl.ds(pl.multiple_of(j * TILE, TILE), TILE)
            new_state = []
            for h in range(count):
                weights = jnp.exp(held[h, there, :] - tops[h])
                total, mixed = state[h]
                total = total + jnp.sum(weights, axis=0, keepdims=True)
                mixed = mixed + jnp.dot(
                    value_t[h * HD : (h + 1) * HD, there], weights.astype(BF16), preferred_element_type=F32
                )
                new_state.append((total, mixed))
            return tuple(new_state)

        empty = (jnp.zeros((1, TILE), F32), jnp.zeros((HD, TILE), F32))
        state = lax.fori_loop(bounds_ref[0, i], i + 1, mix, (empty,) * count)
        for g in range(groups):
            mixed = [mix / total for total, mix in state[2 * g : 2 * g + 2]]
            out_ref[here, g * PAIR : (g + 1) * PAIR] = jnp.concatenate(mixed, axis=0).T.astype(BF16)
        logs = [top + jnp.log(total) for top, (total, _) in zip(tops, state)]
        logsum_ref[:, here] = jnp.concatenate(logs, axis=0)
        return carry

    lax.fori_loop(0, blocks, one_row_block, 0)


def attend_forward(packed, low_blocks, begins):
    bucket, columns = packed.shape
    groups = columns // 3 // PAIR
    return pl.pallas_call(
        attend_kernel,
        name="attend_forward",
        out_shape=(
            jax.ShapeDtypeStruct((bucket, columns // 3), BF16),
            jax.ShapeDtypeStruct((2 * groups, bucket), F32),
        ),
        grid_spec=pltpu.PrefetchScalarGridSpec(
            num_scalar_prefetch=1,
            grid=(1,),
            in_specs=[
                pl.BlockSpec((bucket, columns), lambda g, low: (0, 0)),
                pl.BlockSpec((1, bucket), lambda g, low: (0, 0)),
            ],
            out_specs=[
                pl.BlockSpec((bucket, columns // 3), lambda g, low: (0, 0)),
                pl.BlockSpec((2 * groups, bucket), lambda g, low: (0, 0)),
            ],
            scratch_shapes=[
                pltpu.VMEM((groups * PAIR, bucket), BF16),
                pltpu.VMEM((2 * groups, bucket, TILE), F32),
            ],
        ),
        cost_estimate=pl.CostEstimate(
            flops=4 * 2 * groups * bucket * bucket * HD // 2,
            bytes_accessed=bucket * columns * 3,
            transcendentals=2 * groups * bucket * bucket // 2,
        ),
    )(low_blocks, packed, begins)


def attend_back_kernel(
    bounds_ref, packed_ref, o_ref, go_ref, begin_ref, logsum_ref, out_ref, key_t, query_t, delta
):
    blocks = packed_ref.shape[0] // TILE
    groups = o_ref.shape[1] // PAIR
    half = lax.broadcasted_iota(jnp.int32, (8, PAIR), 1) // HD
    picks = (half == lax.broadcasted_iota(jnp.int32, (8, PAIR), 0)).astype(F32).astype(BF16)
    for g in range(groups):
        column = slice(g * PAIR, (g + 1) * PAIR)
        for block in range(blocks):
            at = slice(block * TILE, (block + 1) * TILE)
            key_t[column, at] = packed_ref[at, third(packed_ref, 1, g)].T
            query_t[column, at] = jnp.zeros((PAIR, TILE), F32)
            product = o_ref[at, column].astype(F32) * go_ref[at, column].astype(F32)
            coarse = product.astype(BF16)
            fine = (product - coarse.astype(F32)).astype(BF16)
            delta[g * 8 : (g + 1) * 8, at] = against_rows(picks, coarse) + against_rows(picks, fine)

    def one_key_block(j, carry):
        there = pl.ds(pl.multiple_of(j * TILE, TILE), TILE)

        def visit(i, state, masked, diagonal):
            here = pl.ds(pl.multiple_of(i * TILE, TILE), TILE)
            allowed = allowed_in(j, i, begin_ref[:, here], diagonal) if masked else None
            new_state = []
            for g in range(groups):
                key_rows = packed_ref[there, third(packed_ref, 1, g)]
                value_rows = packed_ref[there, third(packed_ref, 2, g)]
                queries = split_pair(packed_ref[here, third(packed_ref, 0, g)] * HD ** (-0.5))
                grads = split_pair(go_ref[here, g * PAIR : (g + 1) * PAIR])
                key_grad, value_grad = state[g]
                for which in range(2):
                    h = 2 * g + which
                    scores = against_rows(key_rows, queries[which])
                    if masked:
                        scores = jnp.where(allowed, scores, MASKED)
                    probs = jnp.exp(scores - logsum_ref[h : h + 1, here])
                    grad_probs = against_rows(value_rows, grads[which])
                    row = 8 * g + which
                    grad_scores = (probs * (grad_probs - delta[row : row + 1, here])).astype(BF16)
                    value_grad = value_grad + jnp.dot(
                        probs.astype(BF16), grads[which], preferred_element_type=F32
                    )
                    key_grad = key_grad + jnp.dot(
                        grad_scores, queries[which], preferred_element_type=F32
                    )
                    at = slice(h * HD, (h + 1) * HD)
                    query_t[at, here] += jnp.dot(
                        key_t[at, there], grad_scores, preferred_element_type=F32
                    )
                new_state.append((key_grad, value_grad))
            return tuple(new_state)

        zero = jnp.zeros((TILE, PAIR), F32)
        state = visit(j, ((zero, zero),) * groups, True, True)
        state = lax.fori_loop(j + 1, bounds_ref[1, j], lambda i, s: visit(i, s, False, False), state)
        state = lax.fori_loop(bounds_ref[1, j], bounds_ref[0, j], lambda i, s: visit(i, s, True, False), state)
        for g in range(groups):
            out_ref[there, third(packed_ref, 1, g)] = state[g][0].astype(BF16)
            out_ref[there, third(packed_ref, 2, g)] = state[g][1].astype(BF16)
        return carry

    lax.fori_loop(0, blocks, one_key_block, 0)
    for g in range(groups):
        for block in range(blocks):
            at = slice(block * TILE, (block + 1) * TILE)
            rows = query_t[g * PAIR : (g + 1) * PAIR, at].T * HD ** (-0.5)
            out_ref[at, third(packed_ref, 0, g)] = rows.astype(BF16)


def attend_backward(packed, attended, grad_attended, logsum, high_blocks, begins):
    bucket, columns = packed.shape
    groups = columns // 3 // PAIR
    whole = lambda rows, width: pl.BlockSpec((rows, width), lambda g, high: (0, 0))
    return pl.pallas_call(
        attend_back_kernel,
        name="attend_backward",
        out_shape=jax.ShapeDtypeStruct((bucket, columns), BF16),
        grid_spec=pltpu.PrefetchScalarGridSpec(
            num_scalar_prefetch=1,
            grid=(1,),
            in_specs=[
                whole(bucket, columns),
                whole(bucket, columns // 3),
                whole(bucket, columns // 3),
                whole(1, bucket),
                whole(2 * groups, bucket),
            ],
            out_specs=whole(bucket, columns),
            scratch_shapes=[
                pltpu.VMEM((groups * PAIR, bucket), BF16),
                pltpu.VMEM((groups * PAIR, bucket), F32),
                pltpu.VMEM((groups * 8, bucket), F32),
            ],
        ),
        cost_estimate=pl.CostEstimate(
            flops=10 * 2 * groups * bucket * bucket * HD // 2,
            bytes_accessed=bucket * columns * 6,
            transcendentals=2 * groups * bucket * bucket // 2,
        ),
    )(high_blocks, packed, attended, grad_attended, begins, logsum)


def position():
    dp, seq = lax.axis_index("dp"), lax.axis_index("seq")
    return lax.div(dp, 2), lax.rem(dp, 2), lax.div(seq, 2), lax.rem(seq, 2)


def device(z, x, y, core):
    return (2 * z + x, 2 * y + core)


def send(source, target, semaphores, index, to):
    leave, arrive = semaphores
    copy = pltpu.make_async_remote_copy(
        src_ref=source,
        dst_ref=target,
        send_sem=leave.at[index],
        recv_sem=arrive.at[index],
        device_id=to,
        device_id_type=pl.DeviceIdType.MESH,
    )
    copy.start()
    return copy


def meet(z, x, y, core):
    barrier = pltpu.get_barrier_semaphore()
    others = [device(z, 1 - x, y, core), device(z, x, 1 - y, core), device(z, x, y, 1 - core)]
    others += [device(lax.rem(z + t, 4), x, y, core) for t in (1, 2, 3)]
    for other in others:
        pl.semaphore_signal(barrier, inc=1, device_id=other, device_id_type=pl.DeviceIdType.MESH)
    pl.semaphore_wait(barrier, len(others))


def gather_kernel(
    token_ref, weight_ref, *rest
):
    vector_refs, (all_tokens, all_half, all_tiny, tiny_ref, local_sem), semaphores = rest[:8], rest[8:13], rest[13:]
    z, x, y, core = position()
    tiny_ref[...] = jnp.zeros_like(tiny_ref)
    for i, vector_ref in enumerate(vector_refs):
        tiny_ref[i, : vector_ref.shape[0]] = vector_ref[...].astype(F32)
    token_sems, half_sems, tiny_sems = [semaphores[2 * i : 2 * i + 2] for i in range(3)]
    meet(z, x, y, core)
    core_twin, y_twin, x_twin = device(z, x, y, 1 - core), device(z, x, 1 - y, core), device(z, 1 - x, y, core)
    columns = all_half.shape[5] // 3

    def weight_part(part, c):
        first = pl.multiple_of(part * 2 * columns + c * columns, PAIR)
        return weight_ref.at[:, pl.ds(first, columns)]

    streams = [(all_half, half_sems), (all_tiny, tiny_sems)]
    sent = []
    local = [
        pltpu.make_async_copy(token_ref.at[y], all_tokens.at[y, core], local_sem.at[0]),
        pltpu.make_async_copy(tiny_ref, all_tiny.at[z, x, y, core], local_sem.at[1]),
    ]
    swaps = [send(tiny_ref, all_tiny.at[z, x, y, core], tiny_sems, 0, core_twin)]
    for part in range(3):
        mine = all_half.at[z, x, y, core, :, part * columns : (part + 1) * columns]
        local.append(pltpu.make_async_copy(weight_part(part, core), mine, local_sem.at[2 + part]))
        swaps.append(send(weight_part(part, 1 - core), mine, half_sems, (0, 16, 17)[part], core_twin))
    for copy in local[1:] + local[:1]:
        copy.start()
    for copy in local[1:]:
        copy.wait()
    for copy in swaps:
        copy.wait_recv()
    sent += swaps
    own = [(whole.at[z, x, y], sems) for whole, sems in streams]
    over_y = [send(piece, piece, sems, 1, y_twin) for piece, sems in own]
    token_y = send(token_ref.at[1 - y], all_tokens.at[y, core], token_sems, 0, y_twin)
    token_own = send(token_ref.at[y], all_tokens.at[y, core], token_sems, 1, core_twin)
    along_z, over_x = {}, []

    def spread_piece(p, pieces):
        for t in (1, 2, 3):
            for i, (piece, sems) in enumerate(pieces):
                along_z[p, t, i] = send(piece, piece, sems, 1 + 3 * p + t, device(lax.rem(z + t, 4), x, y, core))
        for piece, sems in pieces:
            over_x.append(send(piece, piece, sems, 8 + 4 * p, x_twin))

    spread_piece(0, own)
    for copy in over_y:
        copy.wait_recv()
    spread_piece(1, [(whole.at[z, x, 1 - y], sems) for whole, sems in streams])
    token_y.wait_recv()
    token_next = send(all_tokens.at[1 - y, core], all_tokens.at[1 - y, core], token_sems, 2, core_twin)
    for p in (0, 1):
        row = y if p == 0 else 1 - y
        for t in (1, 2, 3):
            source = lax.rem(z + 4 - t, 4)
            for i, (whole, sems) in enumerate(streams):
                along_z[p, t, i].wait_recv()
                piece = whole.at[source, x, row]
                over_x.append(send(piece, piece, sems, 8 + 4 * p + t, x_twin))
    for copy in over_x + [token_own, token_next]:
        copy.wait_recv()
    for copy in sent + over_y + [token_y, token_own, token_next] + list(along_z.values()) + over_x:
        copy.wait_send()
    local[0].wait()


def gather_first(tokens, weight, vectors):
    _, local_rows, width = tokens.shape
    rows, columns = weight.shape
    anywhere = pl.BlockSpec(memory_space=pl.ANY)
    near = pl.BlockSpec(memory_space=pltpu.VMEM)
    sems = pltpu.SemaphoreType.DMA
    return pl.pallas_call(
        gather_kernel,
        name="gather_first",
        out_shape=(
            jax.ShapeDtypeStruct((2, 2, local_rows, width), BF16),
            jax.ShapeDtypeStruct((4, 2, 2, 2, rows, columns // 2), BF16),
            jax.ShapeDtypeStruct((4, 2, 2, 2, 8, 128), F32),
        ),
        in_specs=[near] * (2 + len(vectors)),
        out_specs=[anywhere] * 3,
        scratch_shapes=[pltpu.VMEM((8, 128), F32), sems((5,)), sems((3,)), sems((3,)), sems((18,)), sems((18,)), sems((16,)), sems((16,))],
        compiler_params=pltpu.CompilerParams(collective_id=1, has_side_effects=True),
    )(tokens, weight, *vectors)


def reduce_kernel(big_ref, tiny_ref, own_ref, other_ref, sum_ref, *scratch):
    z, x, y, core = position()
    meet(z, x, y, core)
    streams = []
    for i, source in enumerate((big_ref, tiny_ref)):
        streams.append((source,) + scratch[10 * i : 10 * i + 10])
    first_twin = device(z, x + (1 - core) * (1 - 2 * x), y + core * (1 - 2 * y), core)
    second_twin = device(z, x + core * (1 - 2 * x), y + (1 - core) * (1 - 2 * y), core)
    keep = (1 - core) * y + core * x
    order = (1, 2, 3, 0)
    one, two, three = {}, {}, {}
    for t in order:
        k = lax.rem(z + t, 4)
        for j in (0, 1):
            ix = (1 - core) * (1 - x) + core * j
            iy = (1 - core) * j + core * (1 - y)
            for i, (source, came_one, *_, leave, arrive) in enumerate(streams):
                one[t, j, i] = send(source.at[k, ix, iy], came_one.at[t, j], (leave, arrive), 2 * t + j, first_twin)
    for t in order:
        k = lax.rem(z + t, 4)
        for i, (source, came_one, sum_one, came_two, *_, leave, arrive) in enumerate(streams):
            for j in (0, 1):
                one[t, j, i].wait_recv()
                ix = (1 - core) * x + core * j
                iy = (1 - core) * j + core * y
                total = source[k, ix, iy].astype(F32) + came_one[t, j].astype(F32)
                sum_one[t, j] = total.astype(sum_one.dtype)
            two[t, i] = send(sum_one.at[t, 1 - keep], came_two.at[t], (leave, arrive), 8 + t, second_twin)
    for t in order:
        for i, (_, _, sum_one, came_two, sum_two, came_three, total_ref, _, leave, arrive) in enumerate(
            [(s[0], s[1], s[2], s[3], s[4], s[5], s[6], s[7], s[9], s[10]) for s in streams]
        ):
            two[t, i].wait_recv()
            total = sum_one[t, keep].astype(F32) + came_two[t].astype(F32)
            if t == 0:
                total_ref[...] = total
            else:
                sum_two[t - 1] = total.astype(sum_two.dtype)
                to = device(lax.rem(z + t, 4), x, y, core)
                three[t, i] = send(sum_two.at[t - 1], came_three.at[t - 1], (leave, arrive), 11 + t, to)
    last = []
    for i, s in enumerate(streams):
        came_three, total_ref, came_last, leave, arrive = s[5], s[6], s[7], s[9], s[10]
        for t in (1, 2, 3):
            three[t, i].wait_recv()
        total_ref[...] += sum(came_three[t].astype(F32) for t in range(3))
        rows = came_last.shape[0]
        piece = total_ref.at[pl.ds(pl.multiple_of((1 - core) * rows, 8), rows)]
        last.append(send(piece, came_last, (leave, arrive), 15, device(z, x, y, 1 - core)))
    rows = own_ref.shape[0]
    own_ref[...] = streams[0][6][pl.ds(pl.multiple_of(core * rows, 8), rows)]
    for copy in last:
        copy.wait_recv()
    other_ref[...] = streams[0][7][...]
    sum_ref[...] = streams[1][6][pl.ds(pl.multiple_of(core * 8, 8), 8)] + streams[1][7][...]
    for copy in list(one.values()) + list(two.values()) + list(three.values()) + last:
        copy.wait_send()


def reduce_last(big, tiny):
    rows, half_columns = big.shape[3:]
    near = pl.BlockSpec(memory_space=pltpu.VMEM)
    scratch = []
    for shape, kind, kept in (((rows, half_columns), BF16, (rows // 2, half_columns)), ((16, 128), F32, (8, 128))):
        scratch += [
            pltpu.VMEM((4, 2) + shape, kind),
            pltpu.VMEM((4, 2) + shape, kind),
            pltpu.VMEM((4,) + shape, kind),
            pltpu.VMEM((3,) + shape, kind),
            pltpu.VMEM((3,) + shape, kind),
            pltpu.VMEM(shape, F32),
            pltpu.VMEM(kept, F32),
            pltpu.SemaphoreType.DMA((1,)),
            pltpu.SemaphoreType.DMA((16,)),
            pltpu.SemaphoreType.DMA((16,)),
        ]
    return pl.pallas_call(
        reduce_kernel,
        name="reduce_last",
        out_shape=(
            jax.ShapeDtypeStruct((rows // 2, half_columns), F32),
            jax.ShapeDtypeStruct((rows // 2, half_columns), F32),
            jax.ShapeDtypeStruct((8, 128), F32),
        ),
        in_specs=[near, near],
        out_specs=[near, near, near],
        scratch_shapes=scratch,
        compiler_params=pltpu.CompilerParams(collective_id=2, has_side_effects=True),
    )(big, tiny)


def gather_rows(shard):
    return lax.all_gather(shard, ("dp", "seq"), axis=0, tiled=True)


def scatter_sum(full):
    return lax.psum_scatter(full, ("dp", "seq"), scatter_dimension=0, tiled=True)


def local(
    tokens,
    cotangent,
    lengths,
    gain_first,
    shift_first,
    packed_weight,
    packed_bias,
    output_weight,
    output_bias,
    gain_second,
    shift_second,
    expand_weight,
    expand_bias,
    reduce_weight,
    reduce_bias,
):
    micro_count, local_rows, width = tokens.shape
    groups = lax.axis_size("seq")
    devices = groups * lax.axis_size("dp")
    share = groups // micro_count
    bucket = local_rows * groups
    hidden_width = expand_weight.shape[1]
    columns = width // share
    place = lax.axis_index("seq")
    mine, core = place // share, place % share
    swap_micro = [(s, (s + share) % groups) for s in range(groups)]
    swap_core = [(s, s ^ 1) for s in range(groups)]

    def swap_of(both):
        return lax.dynamic_index_in_dim(both, 1 - mine, 0, keepdims=False)

    def placed(both, came):
        kept = lax.dynamic_index_in_dim(both, mine, 0, keepdims=False)
        return jnp.stack([jnp.where(mine == 0, kept, came), jnp.where(mine == 0, came, kept)])

    def own_micro(both):
        return placed(both, lax.ppermute(swap_of(both), "seq", swap_micro))

    def home_micro(blocks):
        kept = lax.dynamic_index_in_dim(blocks, mine, 0, keepdims=False)
        sent = lax.dynamic_index_in_dim(blocks, 1 - mine, 0, keepdims=False)
        came = lax.ppermute(sent, "seq", swap_micro)
        return jnp.stack([jnp.where(mine == 0, kept, came), jnp.where(mine == 0, came, kept)])

    def interleave(own, other):
        first, second = jnp.where(core == 0, own, other), jnp.where(core == 0, other, own)
        return jnp.stack([first, second], axis=1).reshape((bucket,) + own.shape[2:])


    vectors = (gain_first, shift_first, packed_bias, output_bias, gain_second, shift_second, expand_bias, reduce_bias)
    sizes = [v.shape[0] for v in vectors]
    small_count = sum(sizes)
    pieces_per_row = hidden_width // width
    rows = output_weight.shape[0]
    own_kernels = devices == 32 and groups == 4
    if own_kernels:
        all_tokens, half_packed, all_tiny = gather_first(tokens, packed_weight, vectors)
        everyone = all_tokens.reshape(bucket, width)
        own_tokens = lax.dynamic_index_in_dim(all_tokens, core, 1, keepdims=False)
        half_packed = half_packed.reshape(width, 3 * columns)
    else:
        own_tokens = own_micro(tokens)
        everyone = interleave(own_tokens, lax.ppermute(own_tokens, "seq", swap_core))
        full_packed = gather_rows(packed_weight)
        half_packed = jnp.concatenate(
            [lax.dynamic_slice(full_packed, (0, part * width + core * columns), (width, columns)) for part in range(3)], axis=1
        )
        tiny = jnp.concatenate([jnp.pad(v.astype(F32), (0, 128 - v.shape[0])) for v in vectors]).reshape(8, 128)
        all_tiny = gather_rows(tiny)
    small_all = all_tiny.reshape(devices, 8, 128)
    expand_blocks = [expand_weight[:, j * width : (j + 1) * width] for j in range(pieces_per_row)]
    second_shard = jnp.concatenate([output_weight] + expand_blocks + [reduce_weight])
    second = gather_rows(second_shard).reshape(devices, -1, width)
    full_output = second[:, :rows].reshape(width, width)
    full_expand = jnp.concatenate(
        [second[:, rows * (j + 1) : rows * (j + 2)].reshape(width, width) for j in range(pieces_per_row)], axis=1
    )
    full_reduce = second[:, rows * (pieces_per_row + 1) :].reshape(hidden_width, width)
    pieces = [small_all[:, i, :size].reshape(-1) for i, size in enumerate(sizes)]
    gain_one, shift_one, packed_shift, output_shift, gain_two, shift_two, expand_shift, reduce_shift = pieces

    places = jnp.arange(bucket, dtype=jnp.int32)
    bucket_lengths = lax.dynamic_index_in_dim(lengths, mine, 0, keepdims=False)[0]
    slot_count = lengths.shape[-1]
    ends = jnp.cumsum(bucket_lengths)
    past = (places[:, None] >= ends[None, :]).astype(jnp.int32)
    begins = jnp.sum(past * bucket_lengths[None, :], axis=1)
    block_ids = jnp.arange(bucket // TILE, dtype=jnp.int32)
    first_begin, last_begin = begins[::TILE], begins[TILE - 1 :: TILE]
    low = first_begin // TILE
    low_blocks = jnp.stack([low, jnp.minimum(-(-last_begin // TILE), block_ids)])
    high = jnp.sum((low[None, :] <= block_ids[:, None]).astype(jnp.int32), axis=1)
    free = jnp.sum((last_begin[None, :] <= block_ids[:, None] * TILE).astype(jnp.int32), axis=1)
    high_blocks = jnp.stack([high, jnp.clip(free, block_ids + 1, high)])
    begins = begins[None, :]
    valid_all = (jnp.sum(past, axis=1) < slot_count - 1).astype(F32).reshape(2, share, local_rows)
    valid = lax.dynamic_index_in_dim(valid_all, core, 1, keepdims=False).reshape(-1, 1)

    inputs = own_tokens.reshape(-1, width).astype(F32)
    normed_low = layer_norm(everyone.astype(F32), gain_one, shift_one).astype(BF16)
    bias_row = jnp.concatenate([packed_shift[:width], jnp.zeros((width,), F32), packed_shift[width:]])
    half_bias = jnp.concatenate(
        [lax.dynamic_slice(bias_row, (part * width + core * columns,), (columns,)) for part in range(3)]
    )
    packed = (jnp.dot(normed_low, half_packed, preferred_element_type=F32) + half_bias).astype(BF16)
    packed, cotangent_sent = lax.optimization_barrier((packed, swap_of(cotangent)))
    attended_heads, logsum = attend_forward(packed, low_blocks, begins)
    attended_heads, cotangent_came = lax.optimization_barrier(
        (attended_heads, lax.ppermute(cotangent_sent, "seq", swap_micro))
    )
    own_cotangent = placed(cotangent, cotangent_came)

    by_core = attended_heads.reshape(2, share, local_rows, columns)
    kept = lax.dynamic_index_in_dim(by_core, core, 1, keepdims=False)
    came = lax.ppermute(lax.dynamic_index_in_dim(by_core, 1 - core, 1, keepdims=False), "seq", swap_core)
    attended = jnp.concatenate(
        [jnp.where(core == 0, kept, came), jnp.where(core == 0, came, kept)], axis=-1
    ).reshape(-1, width)

    middle = inputs + BRANCH_SCALE * (
        jnp.dot(attended, full_output, preferred_element_type=F32) + output_shift
    )
    normed_two, norm_back_two = jax.vjp(layer_norm, middle, gain_two, shift_two)
    normed_two_low = normed_two.astype(BF16)
    activated, gelu_back = jax.vjp(
        gelu_tanh, jnp.dot(normed_two_low, full_expand, preferred_element_type=F32) + expand_shift
    )
    active_low = activated.astype(BF16)
    branch_out = jnp.dot(active_low, full_reduce, preferred_element_type=F32) + reduce_shift
    layer_rows = ((middle + BRANCH_SCALE * branch_out) * valid).astype(BF16)

    grad_rows = own_cotangent.reshape(-1, width).astype(F32) * valid
    grad_branch = (BRANCH_SCALE * grad_rows).astype(BF16)
    reduce_weight_grad = outer_sum(active_low, grad_branch)
    reduce_bias_grad = jnp.sum(grad_branch.astype(F32), axis=0)
    (grad_hidden,) = gelu_back(against_rows(grad_branch, full_reduce))
    grad_hidden = grad_hidden.astype(BF16)
    expand_weight_grad = outer_sum(normed_two_low, grad_hidden)
    expand_bias_grad = jnp.sum(grad_hidden.astype(F32), axis=0)
    middle_part, gain_two_grad, shift_two_grad = norm_back_two(against_rows(grad_hidden, full_expand))
    grad_middle = grad_rows + middle_part
    grad_proj = (BRANCH_SCALE * grad_middle).astype(BF16)
    output_weight_grad = outer_sum(attended, grad_proj)
    output_bias_grad = jnp.sum(grad_proj.astype(F32), axis=0)
    expand_grads = [
        expand_weight_grad[:, j * width : (j + 1) * width].astype(BF16).reshape(devices, rows, width)
        for j in range(pieces_per_row)
    ]
    early = jnp.concatenate(
        [output_weight_grad.astype(BF16).reshape(devices, rows, width)]
        + expand_grads
        + [reduce_weight_grad.astype(BF16).reshape(devices, -1, width)],
        axis=1,
    )
    grad_attended = against_rows(grad_proj, full_output).astype(BF16)
    take = lambda c: lax.dynamic_slice(grad_attended, (0, c * columns), (2 * local_rows, columns))
    kept = take(core).reshape(2, local_rows, columns)
    came = lax.ppermute(take(1 - core), "seq", swap_core).reshape(2, local_rows, columns)
    grad_heads, early = lax.optimization_barrier((interleave(kept, came), early))
    early_sum = scatter_sum(early.reshape(-1, width)).astype(F32)
    grad_packed = attend_backward(packed, attended_heads, grad_heads, logsum, high_blocks, begins)
    half_grad = outer_sum(normed_low, grad_packed).astype(BF16)
    half_sums = jnp.sum(grad_packed.astype(F32), axis=0).reshape(3, columns)
    part_grad = against_rows(grad_packed, half_packed).astype(BF16)
    by_core = part_grad.reshape(2, share, local_rows, width)
    kept = lax.dynamic_index_in_dim(by_core, core, 1, keepdims=False)
    came = lax.ppermute(lax.dynamic_index_in_dim(by_core, 1 - core, 1, keepdims=False), "seq", swap_core)
    norm_grad = (kept.astype(F32) + came.astype(F32)).reshape(-1, width)
    _, norm_back_one = jax.vjp(layer_norm, inputs, gain_one, shift_one)
    input_part, gain_one_grad, shift_one_grad = norm_back_one(norm_grad)
    input_rows = (grad_middle + input_part).astype(BF16)

    layer_output = home_micro(layer_rows.reshape(2, local_rows, width))
    input_grad = home_micro(input_rows.reshape(2, local_rows, width))

    def spread(half):
        nothing = jnp.zeros_like(half)
        return [jnp.where(core == place_of, half, nothing) for place_of in range(share)]

    packed_bias_grad = jnp.concatenate([block for part in (0, 2) for block in spread(half_sums[part])])
    small_grads = [gain_one_grad, shift_one_grad, packed_bias_grad, output_bias_grad, gain_two_grad, shift_two_grad, expand_bias_grad, reduce_bias_grad]
    if own_kernels:
        small_rows = jnp.stack(
            [jnp.pad(g.reshape(devices, -1), ((0, 0), (0, 128 - g.size // devices))) for g in small_grads], axis=1
        ).reshape(4, 2, 2, share * 8, 128)
        own_half, other_half, small_sum = reduce_last(half_grad.reshape(4, 2, 2, share * rows, 3 * columns), small_rows)
        packed_halves = [jnp.where(core == c, own_half, other_half) for c in range(share)]
        pieces = [small_sum[i, :size] for i, size in enumerate(sizes)]
    else:
        both_halves = scatter_sum(jnp.concatenate(spread(half_grad), axis=1)).astype(F32)
        packed_halves = [both_halves[:, c * 3 * columns : (c + 1) * 3 * columns] for c in range(share)]
        small_sum = scatter_sum(jnp.concatenate([g.reshape(devices, -1) for g in small_grads], axis=1))[0]
        pieces, at = [], 0
        for size in sizes:
            pieces.append(small_sum[at : at + size])
            at += size
    packed_sum = jnp.concatenate(
        [
            packed_halves[c][:, part * columns : (part + 1) * columns]
            for part in range(3)
            for c in range(share)
        ],
        axis=1,
    )
    expand_sum = jnp.concatenate(
        [early_sum[rows * (j + 1) : rows * (j + 2)] for j in range(pieces_per_row)], axis=1
    )
    big = (early_sum[rows * (pieces_per_row + 1) :], expand_sum, early_sum[:rows], packed_sum)
    return (
        layer_output,
        input_grad,
        pieces[0],
        pieces[1],
        big[3],
        pieces[2],
        big[2],
        pieces[3],
        pieces[4],
        pieces[5],
        big[1],
        pieces[6],
        big[0],
        pieces[7],
    )


def solution(mesh):
    both = ("dp", "seq")
    token_spec = P(None, both, None)
    vector, matrix = P(both), P(both, None)
    in_specs = (
        token_spec,
        token_spec,
        P(None, "dp", None),
        vector,
        vector,
        matrix,
        vector,
        matrix,
        vector,
        vector,
        vector,
        matrix,
        vector,
        matrix,
        vector,
    )
    out_specs = (
        token_spec,
        token_spec,
        vector,
        vector,
        matrix,
        vector,
        matrix,
        vector,
        vector,
        vector,
        matrix,
        vector,
        matrix,
        vector,
    )
    return jax.shard_map(local, mesh=mesh, in_specs=in_specs, out_specs=out_specs, check_vma=False)
```

```python
import functools

import jax
import jax.numpy as jnp
from jax import lax
from jax.experimental import pallas as pl
from jax.experimental.pallas import tpu as pltpu
from jax.sharding import PartitionSpec as P

H = 12
HD = 64
BRANCH_SCALE = 12 ** (-0.5)
EPSILON = 1e-05
GELU_SCALE = 0.7978845608028654
GELU_CUBE = 0.044715
F32 = jnp.float32
BF16 = jnp.bfloat16
TILE = 256
PAIR = 2 * HD
MASKED = -1e30


def outer_sum(first, second):
    return lax.dot_general(first, second, (((0,), (0,)), ((), ())), preferred_element_type=F32)


def against_rows(first, second):
    return lax.dot_general(first, second, (((1,), (1,)), ((), ())), preferred_element_type=F32)


def layer_norm(values, norm_gain, norm_shift):
    center = values - jnp.mean(values, axis=-1, keepdims=True)
    spread = jnp.mean(center * center, axis=-1, keepdims=True)
    return center * lax.rsqrt(spread + EPSILON) * norm_gain + norm_shift


def gelu_and_slope(values):
    square = values * values
    bend = jnp.tanh(GELU_SCALE * values * (1.0 + GELU_CUBE * square))
    half = 0.5 * (1.0 + bend)
    slope = half + (0.5 * GELU_SCALE) * values * (1.0 - bend * bend) * (1.0 + (3.0 * GELU_CUBE) * square)
    return values * half, slope


def split_pair(rows):
    lane = lax.broadcasted_iota(jnp.int32, rows.shape, 1)
    nothing = jnp.zeros_like(rows)
    return jnp.where(lane < HD, rows, nothing), jnp.where(lane < HD, nothing, rows)


def third(packed, part, g):
    first = part * (packed.shape[1] // 3) + g * PAIR
    return slice(first, first + PAIR)


def allowed_in(key_block, row_block, begins, diagonal):
    keys = key_block * TILE + lax.broadcasted_iota(jnp.int32, (TILE, TILE), 0)
    allowed = keys >= begins
    if diagonal:
        rows = row_block * TILE + lax.broadcasted_iota(jnp.int32, (TILE, TILE), 1)
        allowed = allowed & (keys <= rows)
    return allowed


def attend_kernel(bounds_ref, packed_ref, begin_ref, out_ref, logsum_ref, value_t, held):
    blocks = packed_ref.shape[0] // TILE
    groups = out_ref.shape[1] // PAIR
    count = 2 * groups
    for g in range(groups):
        for block in range(blocks):
            at = slice(block * TILE, (block + 1) * TILE)
            value_t[g * PAIR : (g + 1) * PAIR, at] = packed_ref[at, third(packed_ref, 2, g)].T

    def one_row_block(i, carry):
        here = pl.ds(pl.multiple_of(i * TILE, TILE), TILE)
        begins = begin_ref[:, here]
        heads = []
        for g in range(groups):
            heads += split_pair(packed_ref[here, third(packed_ref, 0, g)] * HD ** (-0.5))

        def score(j, tops, masked, diagonal):
            there = pl.ds(pl.multiple_of(j * TILE, TILE), TILE)
            allowed = allowed_in(j, i, begins, diagonal) if masked else None
            new_tops = []
            for h in range(count):
                g = h // 2
                key_rows = packed_ref[there, third(packed_ref, 1, g)]
                scores = against_rows(key_rows, heads[h])
                if masked:
                    scores = jnp.where(allowed, scores, MASKED)
                held[h, there, :] = scores
                top = jnp.max(scores, axis=0, keepdims=True)
                new_tops.append(top if tops is None else jnp.maximum(top, tops[h]))
            return tuple(new_tops)

        tops = score(i, None, True, True)
        tops = lax.fori_loop(bounds_ref[0, i], bounds_ref[1, i], lambda j, s: score(j, s, True, False), tops)
        tops = lax.fori_loop(bounds_ref[1, i], i, lambda j, s: score(j, s, False, False), tops)

        def mix(j, state):
            there = pl.ds(pl.multiple_of(j * TILE, TILE), TILE)
            new_state = []
            for h in range(count):
                weights = jnp.exp(held[h, there, :] - tops[h])
                total, mixed = state[h]
                total = total + jnp.sum(weights, axis=0, keepdims=True)
                mixed = mixed + jnp.dot(
                    value_t[h * HD : (h + 1) * HD, there], weights.astype(BF16), preferred_element_type=F32
                )
                new_state.append((total, mixed))
            return tuple(new_state)

        empty = (jnp.zeros((1, TILE), F32), jnp.zeros((HD, TILE), F32))
        state = lax.fori_loop(bounds_ref[0, i], i + 1, mix, (empty,) * count)
        for g in range(groups):
            mixed = [mix / total for total, mix in state[2 * g : 2 * g + 2]]
            out_ref[here, g * PAIR : (g + 1) * PAIR] = jnp.concatenate(mixed, axis=0).T.astype(BF16)
        logs = [top + jnp.log(total) for top, (total, _) in zip(tops, state)]
        logsum_ref[:, here] = jnp.concatenate(logs, axis=0)
        return carry

    lax.fori_loop(0, blocks, one_row_block, 0)


def attend_forward(packed, low_blocks, begins):
    bucket, columns = packed.shape
    groups = columns // 3 // PAIR
    return pl.pallas_call(
        attend_kernel,
        name="attend_forward",
        out_shape=(
            jax.ShapeDtypeStruct((bucket, columns // 3), BF16),
            jax.ShapeDtypeStruct((2 * groups, bucket), F32),
        ),
        grid_spec=pltpu.PrefetchScalarGridSpec(
            num_scalar_prefetch=1,
            grid=(1,),
            in_specs=[
                pl.BlockSpec((bucket, columns), lambda g, low: (0, 0)),
                pl.BlockSpec((1, bucket), lambda g, low: (0, 0)),
            ],
            out_specs=[
                pl.BlockSpec((bucket, columns // 3), lambda g, low: (0, 0)),
                pl.BlockSpec((2 * groups, bucket), lambda g, low: (0, 0)),
            ],
            scratch_shapes=[
                pltpu.VMEM((groups * PAIR, bucket), BF16),
                pltpu.VMEM((2 * groups, bucket, TILE), F32),
            ],
        ),
        cost_estimate=pl.CostEstimate(
            flops=4 * 2 * groups * bucket * bucket * HD // 2,
            bytes_accessed=bucket * columns * 3,
            transcendentals=2 * groups * bucket * bucket // 2,
        ),
    )(low_blocks, packed, begins)


def attend_back_kernel(
    bounds_ref, packed_ref, o_ref, go_ref, begin_ref, logsum_ref, out_ref, key_t, query_t, delta
):
    blocks = packed_ref.shape[0] // TILE
    groups = o_ref.shape[1] // PAIR
    half = lax.broadcasted_iota(jnp.int32, (8, PAIR), 1) // HD
    picks = (half == lax.broadcasted_iota(jnp.int32, (8, PAIR), 0)).astype(F32).astype(BF16)
    for g in range(groups):
        column = slice(g * PAIR, (g + 1) * PAIR)
        for block in range(blocks):
            at = slice(block * TILE, (block + 1) * TILE)
            key_t[column, at] = packed_ref[at, third(packed_ref, 1, g)].T
            query_t[column, at] = jnp.zeros((PAIR, TILE), F32)
            product = o_ref[at, column].astype(F32) * go_ref[at, column].astype(F32)
            coarse = product.astype(BF16)
            fine = (product - coarse.astype(F32)).astype(BF16)
            delta[g * 8 : (g + 1) * 8, at] = against_rows(picks, coarse) + against_rows(picks, fine)

    def one_key_block(j, carry):
        there = pl.ds(pl.multiple_of(j * TILE, TILE), TILE)

        def visit(i, state, masked, diagonal):
            here = pl.ds(pl.multiple_of(i * TILE, TILE), TILE)
            allowed = allowed_in(j, i, begin_ref[:, here], diagonal) if masked else None
            new_state = []
            for g in range(groups):
                key_rows = packed_ref[there, third(packed_ref, 1, g)]
                value_rows = packed_ref[there, third(packed_ref, 2, g)]
                queries = split_pair(packed_ref[here, third(packed_ref, 0, g)] * HD ** (-0.5))
                grads = split_pair(go_ref[here, g * PAIR : (g + 1) * PAIR])
                key_grad, value_grad = state[g]
                for which in range(2):
                    h = 2 * g + which
                    scores = against_rows(key_rows, queries[which])
                    if masked:
                        scores = jnp.where(allowed, scores, MASKED)
                    probs = jnp.exp(scores - logsum_ref[h : h + 1, here])
                    grad_probs = against_rows(value_rows, grads[which])
                    row = 8 * g + which
                    grad_scores = (probs * (grad_probs - delta[row : row + 1, here])).astype(BF16)
                    value_grad = value_grad + jnp.dot(
                        probs.astype(BF16), grads[which], preferred_element_type=F32
                    )
                    key_grad = key_grad + jnp.dot(
                        grad_scores, queries[which], preferred_element_type=F32
                    )
                    at = slice(h * HD, (h + 1) * HD)
                    query_t[at, here] += jnp.dot(
                        key_t[at, there], grad_scores, preferred_element_type=F32
                    )
                new_state.append((key_grad, value_grad))
            return tuple(new_state)

        zero = jnp.zeros((TILE, PAIR), F32)
        state = visit(j, ((zero, zero),) * groups, True, True)
        state = lax.fori_loop(j + 1, bounds_ref[1, j], lambda i, s: visit(i, s, False, False), state)
        state = lax.fori_loop(bounds_ref[1, j], bounds_ref[0, j], lambda i, s: visit(i, s, True, False), state)
        for g in range(groups):
            out_ref[there, third(packed_ref, 1, g)] = state[g][0].astype(BF16)
            out_ref[there, third(packed_ref, 2, g)] = state[g][1].astype(BF16)
        return carry

    lax.fori_loop(0, blocks, one_key_block, 0)
    for g in range(groups):
        for block in range(blocks):
            at = slice(block * TILE, (block + 1) * TILE)
            rows = query_t[g * PAIR : (g + 1) * PAIR, at].T * HD ** (-0.5)
            out_ref[at, third(packed_ref, 0, g)] = rows.astype(BF16)


def attend_backward(packed, attended, grad_attended, logsum, high_blocks, begins):
    bucket, columns = packed.shape
    groups = columns // 3 // PAIR
    whole = lambda rows, width: pl.BlockSpec((rows, width), lambda g, high: (0, 0))
    return pl.pallas_call(
        attend_back_kernel,
        name="attend_backward",
        out_shape=jax.ShapeDtypeStruct((bucket, columns), BF16),
        grid_spec=pltpu.PrefetchScalarGridSpec(
            num_scalar_prefetch=1,
            grid=(1,),
            in_specs=[
                whole(bucket, columns),
                whole(bucket, columns // 3),
                whole(bucket, columns // 3),
                whole(1, bucket),
                whole(2 * groups, bucket),
            ],
            out_specs=whole(bucket, columns),
            scratch_shapes=[
                pltpu.VMEM((groups * PAIR, bucket), BF16),
                pltpu.VMEM((groups * PAIR, bucket), F32),
                pltpu.VMEM((groups * 8, bucket), F32),
            ],
        ),
        cost_estimate=pl.CostEstimate(
            flops=10 * 2 * groups * bucket * bucket * HD // 2,
            bytes_accessed=bucket * columns * 6,
            transcendentals=2 * groups * bucket * bucket // 2,
        ),
    )(high_blocks, packed, attended, grad_attended, begins, logsum)


def position():
    dp, seq = lax.axis_index("dp"), lax.axis_index("seq")
    return lax.div(dp, 2), lax.rem(dp, 2), lax.div(seq, 2), lax.rem(seq, 2)


def device(z, x, y, core):
    return (2 * z + x, 2 * y + core)


def send(source, target, semaphores, index, to):
    leave, arrive = semaphores
    copy = pltpu.make_async_remote_copy(
        src_ref=source,
        dst_ref=target,
        send_sem=leave.at[index],
        recv_sem=arrive.at[index],
        device_id=to,
        device_id_type=pl.DeviceIdType.MESH,
    )
    copy.start()
    return copy


def meet(z, x, y, core):
    barrier = pltpu.get_barrier_semaphore()
    others = [device(z, 1 - x, y, core), device(z, x, 1 - y, core), device(z, x, y, 1 - core)]
    others += [device(lax.rem(z + t, 4), x, y, core) for t in (1, 2, 3)]
    for other in others:
        pl.semaphore_signal(barrier, inc=1, device_id=other, device_id_type=pl.DeviceIdType.MESH)
    pl.semaphore_wait(barrier, len(others))


def gather_kernel(
    token_ref, weight_ref, *rest
):
    vector_refs, (all_tokens, all_half, all_tiny, tiny_ref, local_sem), semaphores = rest[:8], rest[8:13], rest[13:]
    z, x, y, core = position()
    tiny_ref[...] = jnp.zeros_like(tiny_ref)
    for i, vector_ref in enumerate(vector_refs):
        tiny_ref[i, : vector_ref.shape[0]] = vector_ref[...].astype(F32)
    token_sems, half_sems, tiny_sems = [semaphores[2 * i : 2 * i + 2] for i in range(3)]
    meet(z, x, y, core)
    core_twin, y_twin, x_twin = device(z, x, y, 1 - core), device(z, x, 1 - y, core), device(z, 1 - x, y, core)
    columns = all_half.shape[5] // 3

    def weight_part(part, c):
        first = pl.multiple_of(part * 2 * columns + c * columns, PAIR)
        return weight_ref.at[:, pl.ds(first, columns)]

    streams = [(all_half, half_sems), (all_tiny, tiny_sems)]
    sent = []
    local = [
        pltpu.make_async_copy(token_ref.at[y], all_tokens.at[y, core], local_sem.at[0]),
        pltpu.make_async_copy(tiny_ref, all_tiny.at[z, x, y, core], local_sem.at[1]),
    ]
    swaps = [send(tiny_ref, all_tiny.at[z, x, y, core], tiny_sems, 0, core_twin)]
    for part in range(3):
        mine = all_half.at[z, x, y, core, :, part * columns : (part + 1) * columns]
        local.append(pltpu.make_async_copy(weight_part(part, core), mine, local_sem.at[2 + part]))
        swaps.append(send(weight_part(part, 1 - core), mine, half_sems, (0, 16, 17)[part], core_twin))
    for copy in local[1:] + local[:1]:
        copy.start()
    for copy in local[1:]:
        copy.wait()
    for copy in swaps:
        copy.wait_recv()
    sent += swaps
    own = [(whole.at[z, x, y], sems) for whole, sems in streams]
    over_y = [send(piece, piece, sems, 1, y_twin) for piece, sems in own]
    token_y = send(token_ref.at[1 - y], all_tokens.at[y, core], token_sems, 0, y_twin)
    token_own = send(token_ref.at[y], all_tokens.at[y, core], token_sems, 1, core_twin)
    along_z, over_x = {}, []

    def spread_piece(p, pieces):
        for t in (1, 2, 3):
            for i, (piece, sems) in enumerate(pieces):
                along_z[p, t, i] = send(piece, piece, sems, 1 + 3 * p + t, device(lax.rem(z + t, 4), x, y, core))
        for piece, sems in pieces:
            over_x.append(send(piece, piece, sems, 8 + 4 * p, x_twin))

    spread_piece(0, own)
    for copy in over_y:
        copy.wait_recv()
    spread_piece(1, [(whole.at[z, x, 1 - y], sems) for whole, sems in streams])
    token_y.wait_recv()
    token_next = send(all_tokens.at[1 - y, core], all_tokens.at[1 - y, core], token_sems, 2, core_twin)
    for p in (0, 1):
        row = y if p == 0 else 1 - y
        for t in (1, 2, 3):
            source = lax.rem(z + 4 - t, 4)
            for i, (whole, sems) in enumerate(streams):
                along_z[p, t, i].wait_recv()
                piece = whole.at[source, x, row]
                over_x.append(send(piece, piece, sems, 8 + 4 * p + t, x_twin))
    for copy in over_x + [token_own, token_next]:
        copy.wait_recv()
    for copy in sent + over_y + [token_y, token_own, token_next] + list(along_z.values()) + over_x:
        copy.wait_send()
    local[0].wait()


def gather_first(tokens, weight, vectors):
    _, local_rows, width = tokens.shape
    rows, columns = weight.shape
    anywhere = pl.BlockSpec(memory_space=pl.ANY)
    near = pl.BlockSpec(memory_space=pltpu.VMEM)
    sems = pltpu.SemaphoreType.DMA
    return pl.pallas_call(
        gather_kernel,
        name="gather_first",
        out_shape=(
            jax.ShapeDtypeStruct((2, 2, local_rows, width), BF16),
            jax.ShapeDtypeStruct((4, 2, 2, 2, rows, columns // 2), BF16),
            jax.ShapeDtypeStruct((4, 2, 2, 2, 8, 128), F32),
        ),
        in_specs=[near] * (2 + len(vectors)),
        out_specs=[anywhere] * 3,
        scratch_shapes=[pltpu.VMEM((8, 128), F32), sems((5,)), sems((3,)), sems((3,)), sems((18,)), sems((18,)), sems((16,)), sems((16,))],
        compiler_params=pltpu.CompilerParams(collective_id=1, has_side_effects=True),
    )(tokens, weight, *vectors)


def reduce_kernel(big_ref, tiny_ref, own_ref, other_ref, sum_ref, *scratch):
    z, x, y, core = position()
    meet(z, x, y, core)
    streams = []
    for i, source in enumerate((big_ref, tiny_ref)):
        streams.append((source,) + scratch[10 * i : 10 * i + 10])
    first_twin = device(z, x + (1 - core) * (1 - 2 * x), y + core * (1 - 2 * y), core)
    second_twin = device(z, x + core * (1 - 2 * x), y + (1 - core) * (1 - 2 * y), core)
    keep = (1 - core) * y + core * x
    order = (1, 2, 3, 0)
    one, two, three = {}, {}, {}
    for t in order:
        k = lax.rem(z + t, 4)
        for j in (0, 1):
            ix = (1 - core) * (1 - x) + core * j
            iy = (1 - core) * j + core * (1 - y)
            for i, (source, came_one, *_, leave, arrive) in enumerate(streams):
                one[t, j, i] = send(source.at[k, ix, iy], came_one.at[t, j], (leave, arrive), 2 * t + j, first_twin)
    for t in order:
        k = lax.rem(z + t, 4)
        for i, (source, came_one, sum_one, came_two, *_, leave, arrive) in enumerate(streams):
            for j in (0, 1):
                one[t, j, i].wait_recv()
                ix = (1 - core) * x + core * j
                iy = (1 - core) * j + core * y
                total = source[k, ix, iy].astype(F32) + came_one[t, j].astype(F32)
                sum_one[t, j] = total.astype(sum_one.dtype)
            two[t, i] = send(sum_one.at[t, 1 - keep], came_two.at[t], (leave, arrive), 8 + t, second_twin)
    for t in order:
        for i, (_, _, sum_one, came_two, sum_two, came_three, total_ref, _, leave, arrive) in enumerate(
            [(s[0], s[1], s[2], s[3], s[4], s[5], s[6], s[7], s[9], s[10]) for s in streams]
        ):
            two[t, i].wait_recv()
            total = sum_one[t, keep].astype(F32) + came_two[t].astype(F32)
            if t == 0:
                total_ref[...] = total
            else:
                sum_two[t - 1] = total.astype(sum_two.dtype)
                to = device(lax.rem(z + t, 4), x, y, core)
                three[t, i] = send(sum_two.at[t - 1], came_three.at[t - 1], (leave, arrive), 11 + t, to)
    last = []
    for i, s in enumerate(streams):
        came_three, total_ref, came_last, leave, arrive = s[5], s[6], s[7], s[9], s[10]
        for t in (1, 2, 3):
            three[t, i].wait_recv()
        total_ref[...] += sum(came_three[t].astype(F32) for t in range(3))
        rows = came_last.shape[0]
        piece = total_ref.at[pl.ds(pl.multiple_of((1 - core) * rows, 8), rows)]
        last.append(send(piece, came_last, (leave, arrive), 15, device(z, x, y, 1 - core)))
    rows = own_ref.shape[0]
    own_ref[...] = streams[0][6][pl.ds(pl.multiple_of(core * rows, 8), rows)]
    for copy in last:
        copy.wait_recv()
    other_ref[...] = streams[0][7][...]
    sum_ref[...] = streams[1][6][pl.ds(pl.multiple_of(core * 8, 8), 8)] + streams[1][7][...]
    for copy in list(one.values()) + list(two.values()) + list(three.values()) + last:
        copy.wait_send()


def reduce_last(big, tiny):
    rows, half_columns = big.shape[3:]
    near = pl.BlockSpec(memory_space=pltpu.VMEM)
    scratch = []
    for shape, kind, kept in (((rows, half_columns), BF16, (rows // 2, half_columns)), ((16, 128), F32, (8, 128))):
        scratch += [
            pltpu.VMEM((4, 2) + shape, kind),
            pltpu.VMEM((4, 2) + shape, kind),
            pltpu.VMEM((4,) + shape, kind),
            pltpu.VMEM((3,) + shape, kind),
            pltpu.VMEM((3,) + shape, kind),
            pltpu.VMEM(shape, F32),
            pltpu.VMEM(kept, F32),
            pltpu.SemaphoreType.DMA((1,)),
            pltpu.SemaphoreType.DMA((16,)),
            pltpu.SemaphoreType.DMA((16,)),
        ]
    return pl.pallas_call(
        reduce_kernel,
        name="reduce_last",
        out_shape=(
            jax.ShapeDtypeStruct((rows // 2, half_columns), F32),
            jax.ShapeDtypeStruct((rows // 2, half_columns), F32),
            jax.ShapeDtypeStruct((8, 128), F32),
        ),
        in_specs=[near, near],
        out_specs=[near, near, near],
        scratch_shapes=scratch,
        compiler_params=pltpu.CompilerParams(collective_id=2, has_side_effects=True),
    )(big, tiny)


def pack_kernel(output_ref, expand_ref, reduce_ref, out_ref):
    width = output_ref.shape[1]
    count = expand_ref.shape[1] // width
    out_ref[0] = output_ref[...]
    for j in range(count):
        out_ref[1 + j] = expand_ref[:, j * width : (j + 1) * width]
        out_ref[1 + count + j] = reduce_ref[j]


def pack_second(output_weight, expand_weight, reduce_weight):
    rows, width = output_weight.shape
    count = expand_weight.shape[1] // width
    near = pl.BlockSpec(memory_space=pltpu.VMEM)
    packed = pl.pallas_call(
        pack_kernel,
        name="pack_second",
        out_shape=jax.ShapeDtypeStruct((1 + 2 * count, rows, width), BF16),
        in_specs=[near] * 3,
        out_specs=near,
    )(output_weight, expand_weight, reduce_weight.reshape(count, rows, width))
    return packed.reshape(-1, width)


def gather_rows(shard):
    return lax.all_gather(shard, ("dp", "seq"), axis=0, tiled=True)


def scatter_sum(full):
    return lax.psum_scatter(full, ("dp", "seq"), scatter_dimension=0, tiled=True)


def local(
    tokens,
    cotangent,
    lengths,
    gain_first,
    shift_first,
    packed_weight,
    packed_bias,
    output_weight,
    output_bias,
    gain_second,
    shift_second,
    expand_weight,
    expand_bias,
    reduce_weight,
    reduce_bias,
):
    micro_count, local_rows, width = tokens.shape
    groups = lax.axis_size("seq")
    devices = groups * lax.axis_size("dp")
    share = groups // micro_count
    bucket = local_rows * groups
    hidden_width = expand_weight.shape[1]
    columns = width // share
    place = lax.axis_index("seq")
    mine, core = place // share, place % share
    swap_micro = [(s, (s + share) % groups) for s in range(groups)]
    swap_core = [(s, s ^ 1) for s in range(groups)]

    def swap_of(both):
        return lax.dynamic_index_in_dim(both, 1 - mine, 0, keepdims=False)

    def placed(both, came):
        kept = lax.dynamic_index_in_dim(both, mine, 0, keepdims=False)
        return jnp.stack([jnp.where(mine == 0, kept, came), jnp.where(mine == 0, came, kept)])

    def own_micro(both):
        return placed(both, lax.ppermute(swap_of(both), "seq", swap_micro))

    def home_micro(blocks):
        kept = lax.dynamic_index_in_dim(blocks, mine, 0, keepdims=False)
        sent = lax.dynamic_index_in_dim(blocks, 1 - mine, 0, keepdims=False)
        came = lax.ppermute(sent, "seq", swap_micro)
        return jnp.stack([jnp.where(mine == 0, kept, came), jnp.where(mine == 0, came, kept)])

    def interleave(own, other):
        first, second = jnp.where(core == 0, own, other), jnp.where(core == 0, other, own)
        return jnp.stack([first, second], axis=1).reshape((bucket,) + own.shape[2:])


    vectors = (gain_first, shift_first, packed_bias, output_bias, gain_second, shift_second, expand_bias, reduce_bias)
    sizes = [v.shape[0] for v in vectors]
    small_count = sum(sizes)
    pieces_per_row = hidden_width // width
    rows = output_weight.shape[0]
    own_kernels = devices == 32 and groups == 4
    if own_kernels:
        all_tokens, half_packed, all_tiny = gather_first(tokens, packed_weight, vectors)
        everyone = all_tokens.reshape(bucket, width)
        own_tokens = lax.dynamic_index_in_dim(all_tokens, core, 1, keepdims=False)
        half_packed = half_packed.reshape(width, 3 * columns)
    else:
        own_tokens = own_micro(tokens)
        everyone = interleave(own_tokens, lax.ppermute(own_tokens, "seq", swap_core))
        full_packed = gather_rows(packed_weight)
        half_packed = jnp.concatenate(
            [lax.dynamic_slice(full_packed, (0, part * width + core * columns), (width, columns)) for part in range(3)], axis=1
        )
        tiny = jnp.concatenate([jnp.pad(v.astype(F32), (0, 128 - v.shape[0])) for v in vectors]).reshape(8, 128)
        all_tiny = gather_rows(tiny)
    small_all = all_tiny.reshape(devices, 8, 128)
    if own_kernels:
        second_shard = pack_second(output_weight, expand_weight, reduce_weight)
    else:
        expand_blocks = [expand_weight[:, j * width : (j + 1) * width] for j in range(pieces_per_row)]
        second_shard = jnp.concatenate([output_weight] + expand_blocks + [reduce_weight])
    second = gather_rows(second_shard).reshape(devices, -1, width)
    full_output = second[:, :rows].reshape(width, width)
    full_expand = jnp.concatenate(
        [second[:, rows * (j + 1) : rows * (j + 2)].reshape(width, width) for j in range(pieces_per_row)], axis=1
    )
    full_reduce = second[:, rows * (pieces_per_row + 1) :].reshape(hidden_width, width)
    pieces = [small_all[:, i, :size].reshape(-1) for i, size in enumerate(sizes)]
    gain_one, shift_one, packed_shift, output_shift, gain_two, shift_two, expand_shift, reduce_shift = pieces

    places = jnp.arange(bucket, dtype=jnp.int32)
    bucket_lengths = lax.dynamic_index_in_dim(lengths, mine, 0, keepdims=False)[0]
    slot_count = lengths.shape[-1]
    ends = jnp.cumsum(bucket_lengths)
    past = (places[:, None] >= ends[None, :]).astype(jnp.int32)
    begins = jnp.sum(past * bucket_lengths[None, :], axis=1)
    block_ids = jnp.arange(bucket // TILE, dtype=jnp.int32)
    first_begin, last_begin = begins[::TILE], begins[TILE - 1 :: TILE]
    low = first_begin // TILE
    low_blocks = jnp.stack([low, jnp.minimum(-(-last_begin // TILE), block_ids)])
    high = jnp.sum((low[None, :] <= block_ids[:, None]).astype(jnp.int32), axis=1)
    free = jnp.sum((last_begin[None, :] <= block_ids[:, None] * TILE).astype(jnp.int32), axis=1)
    high_blocks = jnp.stack([high, jnp.clip(free, block_ids + 1, high)])
    begins = begins[None, :]
    valid_all = (jnp.sum(past, axis=1) < slot_count - 1).astype(F32).reshape(2, share, local_rows)
    valid = lax.dynamic_index_in_dim(valid_all, core, 1, keepdims=False).reshape(-1, 1)

    inputs = own_tokens.reshape(-1, width).astype(F32)
    normed_low = layer_norm(everyone.astype(F32), gain_one, shift_one).astype(BF16)
    bias_row = jnp.concatenate([packed_shift[:width], jnp.zeros((width,), F32), packed_shift[width:]])
    half_bias = jnp.concatenate(
        [lax.dynamic_slice(bias_row, (part * width + core * columns,), (columns,)) for part in range(3)]
    )
    packed = (jnp.dot(normed_low, half_packed, preferred_element_type=F32) + half_bias).astype(BF16)
    packed, cotangent_sent = lax.optimization_barrier((packed, swap_of(cotangent)))
    attended_heads, logsum = attend_forward(packed, low_blocks, begins)
    attended_heads, cotangent_came = lax.optimization_barrier(
        (attended_heads, lax.ppermute(cotangent_sent, "seq", swap_micro))
    )
    own_cotangent = placed(cotangent, cotangent_came)

    by_core = attended_heads.reshape(2, share, local_rows, columns)
    kept = lax.dynamic_index_in_dim(by_core, core, 1, keepdims=False)
    came = lax.ppermute(lax.dynamic_index_in_dim(by_core, 1 - core, 1, keepdims=False), "seq", swap_core)
    attended = jnp.concatenate(
        [jnp.where(core == 0, kept, came), jnp.where(core == 0, came, kept)], axis=-1
    ).reshape(-1, width)

    middle = inputs + BRANCH_SCALE * (
        jnp.dot(attended, full_output, preferred_element_type=F32) + output_shift
    )
    normed_two, norm_back_two = jax.vjp(layer_norm, middle, gain_two, shift_two)
    normed_two_low = normed_two.astype(BF16)
    activated, slope = gelu_and_slope(
        jnp.dot(normed_two_low, full_expand, preferred_element_type=F32) + expand_shift
    )
    active_low, slope_low = lax.optimization_barrier((activated.astype(BF16), slope.astype(BF16)))
    branch_out = jnp.dot(active_low, full_reduce, preferred_element_type=F32) + reduce_shift
    layer_rows = ((middle + BRANCH_SCALE * branch_out) * valid).astype(BF16)

    grad_rows = own_cotangent.reshape(-1, width).astype(F32) * valid
    grad_branch = (BRANCH_SCALE * grad_rows).astype(BF16)
    reduce_weight_grad = outer_sum(active_low, grad_branch)
    reduce_bias_grad = jnp.sum(grad_branch.astype(F32), axis=0)
    grad_hidden = (against_rows(grad_branch, full_reduce) * slope_low.astype(F32)).astype(BF16)
    expand_weight_grad = outer_sum(normed_two_low, grad_hidden)
    expand_bias_grad = jnp.sum(grad_hidden.astype(F32), axis=0)
    middle_part, gain_two_grad, shift_two_grad = norm_back_two(against_rows(grad_hidden, full_expand))
    grad_middle = grad_rows + middle_part
    grad_proj = (BRANCH_SCALE * grad_middle).astype(BF16)
    output_weight_grad = outer_sum(attended, grad_proj)
    output_bias_grad = jnp.sum(grad_proj.astype(F32), axis=0)
    expand_grads = [
        expand_weight_grad[:, j * width : (j + 1) * width].astype(BF16).reshape(devices, rows, width)
        for j in range(pieces_per_row)
    ]
    early = jnp.concatenate(
        [output_weight_grad.astype(BF16).reshape(devices, rows, width)]
        + expand_grads
        + [reduce_weight_grad.astype(BF16).reshape(devices, -1, width)],
        axis=1,
    )
    grad_attended = against_rows(grad_proj, full_output).astype(BF16)
    take = lambda c: lax.dynamic_slice(grad_attended, (0, c * columns), (2 * local_rows, columns))
    kept = take(core).reshape(2, local_rows, columns)
    came = lax.ppermute(take(1 - core), "seq", swap_core).reshape(2, local_rows, columns)
    grad_heads, early = lax.optimization_barrier((interleave(kept, came), early))
    early_sum = scatter_sum(early.reshape(-1, width)).astype(F32)
    grad_packed = attend_backward(packed, attended_heads, grad_heads, logsum, high_blocks, begins)
    half_grad = outer_sum(normed_low, grad_packed).astype(BF16)
    half_sums = jnp.sum(grad_packed.astype(F32), axis=0).reshape(3, columns)
    part_grad = against_rows(grad_packed, half_packed).astype(BF16)
    by_core = part_grad.reshape(2, share, local_rows, width)
    kept = lax.dynamic_index_in_dim(by_core, core, 1, keepdims=False)
    came = lax.ppermute(lax.dynamic_index_in_dim(by_core, 1 - core, 1, keepdims=False), "seq", swap_core)
    norm_grad = (kept.astype(F32) + came.astype(F32)).reshape(-1, width)
    _, norm_back_one = jax.vjp(layer_norm, inputs, gain_one, shift_one)
    input_part, gain_one_grad, shift_one_grad = norm_back_one(norm_grad)
    input_rows = (grad_middle + input_part).astype(BF16)

    layer_output = home_micro(layer_rows.reshape(2, local_rows, width))
    input_grad = home_micro(input_rows.reshape(2, local_rows, width))

    def spread(half):
        nothing = jnp.zeros_like(half)
        return [jnp.where(core == place_of, half, nothing) for place_of in range(share)]

    packed_bias_grad = jnp.concatenate([block for part in (0, 2) for block in spread(half_sums[part])])
    small_grads = [gain_one_grad, shift_one_grad, packed_bias_grad, output_bias_grad, gain_two_grad, shift_two_grad, expand_bias_grad, reduce_bias_grad]
    if own_kernels:
        small_rows = jnp.stack(
            [jnp.pad(g.reshape(devices, -1), ((0, 0), (0, 128 - g.size // devices))) for g in small_grads], axis=1
        ).reshape(4, 2, 2, share * 8, 128)
        own_half, other_half, small_sum = reduce_last(half_grad.reshape(4, 2, 2, share * rows, 3 * columns), small_rows)
        packed_halves = [jnp.where(core == c, own_half, other_half) for c in range(share)]
        pieces = [small_sum[i, :size] for i, size in enumerate(sizes)]
    else:
        both_halves = scatter_sum(jnp.concatenate(spread(half_grad), axis=1)).astype(F32)
        packed_halves = [both_halves[:, c * 3 * columns : (c + 1) * 3 * columns] for c in range(share)]
        small_sum = scatter_sum(jnp.concatenate([g.reshape(devices, -1) for g in small_grads], axis=1))[0]
        pieces, at = [], 0
        for size in sizes:
            pieces.append(small_sum[at : at + size])
            at += size
    packed_sum = jnp.concatenate(
        [
            packed_halves[c][:, part * columns : (part + 1) * columns]
            for part in range(3)
            for c in range(share)
        ],
        axis=1,
    )
    expand_sum = jnp.concatenate(
        [early_sum[rows * (j + 1) : rows * (j + 2)] for j in range(pieces_per_row)], axis=1
    )
    big = (early_sum[rows * (pieces_per_row + 1) :], expand_sum, early_sum[:rows], packed_sum)
    return (
        layer_output,
        input_grad,
        pieces[0],
        pieces[1],
        big[3],
        pieces[2],
        big[2],
        pieces[3],
        pieces[4],
        pieces[5],
        big[1],
        pieces[6],
        big[0],
        pieces[7],
    )


def solution(mesh):
    both = ("dp", "seq")
    token_spec = P(None, both, None)
    vector, matrix = P(both), P(both, None)
    in_specs = (
        token_spec,
        token_spec,
        P(None, "dp", None),
        vector,
        vector,
        matrix,
        vector,
        matrix,
        vector,
        vector,
        vector,
        matrix,
        vector,
        matrix,
        vector,
    )
    out_specs = (
        token_spec,
        token_spec,
        vector,
        vector,
        matrix,
        vector,
        matrix,
        vector,
        vector,
        vector,
        matrix,
        vector,
        matrix,
        vector,
    )
    return jax.shard_map(local, mesh=mesh, in_specs=in_specs, out_specs=out_specs, check_vma=False)
```

```python
import functools

import jax
import jax.numpy as jnp
from jax import lax
from jax.experimental import pallas as pl
from jax.experimental.pallas import tpu as pltpu
from jax.sharding import PartitionSpec as P

H = 12
HD = 64
BRANCH_SCALE = 12 ** (-0.5)
EPSILON = 1e-05
GELU_SCALE = 0.7978845608028654
GELU_CUBE = 0.044715
F32 = jnp.float32
BF16 = jnp.bfloat16
TILE = 256
PAIR = 2 * HD
MASKED = -1e30


def outer_sum(first, second):
    return lax.dot_general(first, second, (((0,), (0,)), ((), ())), preferred_element_type=F32)


def against_rows(first, second):
    return lax.dot_general(first, second, (((1,), (1,)), ((), ())), preferred_element_type=F32)


def layer_norm(values, norm_gain, norm_shift):
    center = values - jnp.mean(values, axis=-1, keepdims=True)
    spread = jnp.mean(center * center, axis=-1, keepdims=True)
    return center * lax.rsqrt(spread + EPSILON) * norm_gain + norm_shift


def gelu_and_slope(values):
    square = values * values
    bend = jnp.tanh(values * (GELU_SCALE + (GELU_SCALE * GELU_CUBE) * square))
    half = 0.5 + 0.5 * bend
    active = values * half
    slope = half + active * (1.0 - half) * (2.0 * GELU_SCALE + (6.0 * GELU_SCALE * GELU_CUBE) * square)
    return active, slope


def split_pair(rows):
    lane = lax.broadcasted_iota(jnp.int32, rows.shape, 1)
    nothing = jnp.zeros_like(rows)
    return jnp.where(lane < HD, rows, nothing), jnp.where(lane < HD, nothing, rows)


def third(packed, part, g):
    first = part * (packed.shape[1] // 3) + g * PAIR
    return slice(first, first + PAIR)


def allowed_in(key_block, row_block, begins, diagonal):
    keys = key_block * TILE + lax.broadcasted_iota(jnp.int32, (TILE, TILE), 0)
    allowed = keys >= begins
    if diagonal:
        rows = row_block * TILE + lax.broadcasted_iota(jnp.int32, (TILE, TILE), 1)
        allowed = allowed & (keys <= rows)
    return allowed


def attend_kernel(bounds_ref, packed_ref, begin_ref, out_ref, logsum_ref, value_t, held):
    blocks = packed_ref.shape[0] // TILE
    groups = out_ref.shape[1] // PAIR
    count = 2 * groups
    for g in range(groups):
        for block in range(blocks):
            at = slice(block * TILE, (block + 1) * TILE)
            value_t[g * PAIR : (g + 1) * PAIR, at] = packed_ref[at, third(packed_ref, 2, g)].T

    def one_row_block(i, carry):
        here = pl.ds(pl.multiple_of(i * TILE, TILE), TILE)
        begins = begin_ref[:, here]
        heads = []
        for g in range(groups):
            heads += split_pair(packed_ref[here, third(packed_ref, 0, g)] * HD ** (-0.5))

        def score(j, tops, masked, diagonal):
            there = pl.ds(pl.multiple_of(j * TILE, TILE), TILE)
            allowed = allowed_in(j, i, begins, diagonal) if masked else None
            new_tops = []
            for h in range(count):
                g = h // 2
                key_rows = packed_ref[there, third(packed_ref, 1, g)]
                scores = against_rows(key_rows, heads[h])
                if masked:
                    scores = jnp.where(allowed, scores, MASKED)
                held[h, there, :] = scores
                top = jnp.max(scores, axis=0, keepdims=True)
                new_tops.append(top if tops is None else jnp.maximum(top, tops[h]))
            return tuple(new_tops)

        tops = score(i, None, True, True)
        tops = lax.fori_loop(bounds_ref[0, i], bounds_ref[1, i], lambda j, s: score(j, s, True, False), tops)
        tops = lax.fori_loop(bounds_ref[1, i], i, lambda j, s: score(j, s, False, False), tops)

        def mix(j, state):
            there = pl.ds(pl.multiple_of(j * TILE, TILE), TILE)
            new_state = []
            for h in range(count):
                weights = jnp.exp(held[h, there, :] - tops[h])
                total, mixed = state[h]
                total = total + jnp.sum(weights, axis=0, keepdims=True)
                mixed = mixed + jnp.dot(
                    value_t[h * HD : (h + 1) * HD, there], weights.astype(BF16), preferred_element_type=F32
                )
                new_state.append((total, mixed))
            return tuple(new_state)

        empty = (jnp.zeros((1, TILE), F32), jnp.zeros((HD, TILE), F32))
        state = lax.fori_loop(bounds_ref[0, i], i + 1, mix, (empty,) * count)
        for g in range(groups):
            mixed = [mix / total for total, mix in state[2 * g : 2 * g + 2]]
            out_ref[here, g * PAIR : (g + 1) * PAIR] = jnp.concatenate(mixed, axis=0).T.astype(BF16)
        logs = [top + jnp.log(total) for top, (total, _) in zip(tops, state)]
        logsum_ref[:, here] = jnp.concatenate(logs, axis=0)
        return carry

    lax.fori_loop(0, blocks, one_row_block, 0)


def attend_forward(packed, low_blocks, begins):
    bucket, columns = packed.shape
    groups = columns // 3 // PAIR
    return pl.pallas_call(
        attend_kernel,
        name="attend_forward",
        out_shape=(
            jax.ShapeDtypeStruct((bucket, columns // 3), BF16),
            jax.ShapeDtypeStruct((2 * groups, bucket), F32),
        ),
        grid_spec=pltpu.PrefetchScalarGridSpec(
            num_scalar_prefetch=1,
            grid=(1,),
            in_specs=[
                pl.BlockSpec((bucket, columns), lambda g, low: (0, 0)),
                pl.BlockSpec((1, bucket), lambda g, low: (0, 0)),
            ],
            out_specs=[
                pl.BlockSpec((bucket, columns // 3), lambda g, low: (0, 0)),
                pl.BlockSpec((2 * groups, bucket), lambda g, low: (0, 0)),
            ],
            scratch_shapes=[
                pltpu.VMEM((groups * PAIR, bucket), BF16),
                pltpu.VMEM((2 * groups, bucket, TILE), F32),
            ],
        ),
        cost_estimate=pl.CostEstimate(
            flops=4 * 2 * groups * bucket * bucket * HD // 2,
            bytes_accessed=bucket * columns * 3,
            transcendentals=2 * groups * bucket * bucket // 2,
        ),
    )(low_blocks, packed, begins)


def attend_back_kernel(
    bounds_ref, packed_ref, o_ref, go_ref, begin_ref, logsum_ref, out_ref, key_t, query_t, delta
):
    blocks = packed_ref.shape[0] // TILE
    groups = o_ref.shape[1] // PAIR
    half = lax.broadcasted_iota(jnp.int32, (8, PAIR), 1) // HD
    picks = (half == lax.broadcasted_iota(jnp.int32, (8, PAIR), 0)).astype(F32).astype(BF16)
    for g in range(groups):
        column = slice(g * PAIR, (g + 1) * PAIR)
        for block in range(blocks):
            at = slice(block * TILE, (block + 1) * TILE)
            key_t[column, at] = packed_ref[at, third(packed_ref, 1, g)].T
            query_t[column, at] = jnp.zeros((PAIR, TILE), F32)
            product = o_ref[at, column].astype(F32) * go_ref[at, column].astype(F32)
            coarse = product.astype(BF16)
            fine = (product - coarse.astype(F32)).astype(BF16)
            delta[g * 8 : (g + 1) * 8, at] = against_rows(picks, coarse) + against_rows(picks, fine)

    def one_key_block(j, carry):
        there = pl.ds(pl.multiple_of(j * TILE, TILE), TILE)

        def visit(i, state, masked, diagonal):
            here = pl.ds(pl.multiple_of(i * TILE, TILE), TILE)
            allowed = allowed_in(j, i, begin_ref[:, here], diagonal) if masked else None
            new_state = []
            for g in range(groups):
                key_rows = packed_ref[there, third(packed_ref, 1, g)]
                value_rows = packed_ref[there, third(packed_ref, 2, g)]
                queries = split_pair(packed_ref[here, third(packed_ref, 0, g)] * HD ** (-0.5))
                grads = split_pair(go_ref[here, g * PAIR : (g + 1) * PAIR])
                key_grad, value_grad = state[g]
                for which in range(2):
                    h = 2 * g + which
                    scores = against_rows(key_rows, queries[which])
                    if masked:
                        scores = jnp.where(allowed, scores, MASKED)
                    probs = jnp.exp(scores - logsum_ref[h : h + 1, here])
                    grad_probs = against_rows(value_rows, grads[which])
                    row = 8 * g + which
                    grad_scores = (probs * (grad_probs - delta[row : row + 1, here])).astype(BF16)
                    value_grad = value_grad + jnp.dot(
                        probs.astype(BF16), grads[which], preferred_element_type=F32
                    )
                    key_grad = key_grad + jnp.dot(
                        grad_scores, queries[which], preferred_element_type=F32
                    )
                    at = slice(h * HD, (h + 1) * HD)
                    query_t[at, here] += jnp.dot(
                        key_t[at, there], grad_scores, preferred_element_type=F32
                    )
                new_state.append((key_grad, value_grad))
            return tuple(new_state)

        zero = jnp.zeros((TILE, PAIR), F32)
        state = visit(j, ((zero, zero),) * groups, True, True)
        state = lax.fori_loop(j + 1, bounds_ref[1, j], lambda i, s: visit(i, s, False, False), state)
        state = lax.fori_loop(bounds_ref[1, j], bounds_ref[0, j], lambda i, s: visit(i, s, True, False), state)
        for g in range(groups):
            out_ref[there, third(packed_ref, 1, g)] = state[g][0].astype(BF16)
            out_ref[there, third(packed_ref, 2, g)] = state[g][1].astype(BF16)
        return carry

    lax.fori_loop(0, blocks, one_key_block, 0)
    for g in range(groups):
        for block in range(blocks):
            at = slice(block * TILE, (block + 1) * TILE)
            rows = query_t[g * PAIR : (g + 1) * PAIR, at].T * HD ** (-0.5)
            out_ref[at, third(packed_ref, 0, g)] = rows.astype(BF16)


def attend_backward(packed, attended, grad_attended, logsum, high_blocks, begins):
    bucket, columns = packed.shape
    groups = columns // 3 // PAIR
    whole = lambda rows, width: pl.BlockSpec((rows, width), lambda g, high: (0, 0))
    return pl.pallas_call(
        attend_back_kernel,
        name="attend_backward",
        out_shape=jax.ShapeDtypeStruct((bucket, columns), BF16),
        grid_spec=pltpu.PrefetchScalarGridSpec(
            num_scalar_prefetch=1,
            grid=(1,),
            in_specs=[
                whole(bucket, columns),
                whole(bucket, columns // 3),
                whole(bucket, columns // 3),
                whole(1, bucket),
                whole(2 * groups, bucket),
            ],
            out_specs=whole(bucket, columns),
            scratch_shapes=[
                pltpu.VMEM((groups * PAIR, bucket), BF16),
                pltpu.VMEM((groups * PAIR, bucket), F32),
                pltpu.VMEM((groups * 8, bucket), F32),
            ],
        ),
        cost_estimate=pl.CostEstimate(
            flops=groups * bucket * bucket,
            bytes_accessed=bucket * columns,
            transcendentals=bucket,
        ),
    )(high_blocks, packed, attended, grad_attended, begins, logsum)


def position():
    dp, seq = lax.axis_index("dp"), lax.axis_index("seq")
    return lax.div(dp, 2), lax.rem(dp, 2), lax.div(seq, 2), lax.rem(seq, 2)


def device(z, x, y, core):
    return (2 * z + x, 2 * y + core)


def send(source, target, semaphores, index, to):
    leave, arrive = semaphores
    copy = pltpu.make_async_remote_copy(
        src_ref=source,
        dst_ref=target,
        send_sem=leave.at[index],
        recv_sem=arrive.at[index],
        device_id=to,
        device_id_type=pl.DeviceIdType.MESH,
    )
    copy.start()
    return copy


def meet(z, x, y, core):
    barrier = pltpu.get_barrier_semaphore()
    others = [device(z, 1 - x, y, core), device(z, x, 1 - y, core), device(z, x, y, 1 - core)]
    others += [device(lax.rem(z + t, 4), x, y, core) for t in (1, 2, 3)]
    for other in others:
        pl.semaphore_signal(barrier, inc=1, device_id=other, device_id_type=pl.DeviceIdType.MESH)
    pl.semaphore_wait(barrier, len(others))


def gather_kernel(
    token_ref, weight_ref, *rest
):
    vector_refs, (all_tokens, all_half, all_tiny, tiny_ref, local_sem), semaphores = rest[:8], rest[8:13], rest[13:]
    z, x, y, core = position()
    tiny_ref[...] = jnp.zeros_like(tiny_ref)
    for i, vector_ref in enumerate(vector_refs):
        tiny_ref[i, : vector_ref.shape[0]] = vector_ref[...].astype(F32)
    token_sems, half_sems, tiny_sems = [semaphores[2 * i : 2 * i + 2] for i in range(3)]
    meet(z, x, y, core)
    core_twin, y_twin, x_twin = device(z, x, y, 1 - core), device(z, x, 1 - y, core), device(z, 1 - x, y, core)
    columns = all_half.shape[5] // 3

    def weight_part(part, c):
        first = pl.multiple_of(part * 2 * columns + c * columns, PAIR)
        return weight_ref.at[:, pl.ds(first, columns)]

    streams = [(all_half, half_sems), (all_tiny, tiny_sems)]
    sent = []
    local = [
        pltpu.make_async_copy(token_ref.at[y], all_tokens.at[y, core], local_sem.at[0]),
        pltpu.make_async_copy(tiny_ref, all_tiny.at[z, x, y, core], local_sem.at[1]),
    ]
    swaps = [send(tiny_ref, all_tiny.at[z, x, y, core], tiny_sems, 0, core_twin)]
    for part in range(3):
        mine = all_half.at[z, x, y, core, :, part * columns : (part + 1) * columns]
        local.append(pltpu.make_async_copy(weight_part(part, core), mine, local_sem.at[2 + part]))
        swaps.append(send(weight_part(part, 1 - core), mine, half_sems, (0, 16, 17)[part], core_twin))
    for copy in local[1:] + local[:1]:
        copy.start()
    for copy in local[1:]:
        copy.wait()
    for copy in swaps:
        copy.wait_recv()
    sent += swaps
    own = [(whole.at[z, x, y], sems) for whole, sems in streams]
    over_y = [send(piece, piece, sems, 1, y_twin) for piece, sems in own]
    token_y = send(token_ref.at[1 - y], all_tokens.at[y, core], token_sems, 0, y_twin)
    token_own = send(token_ref.at[y], all_tokens.at[y, core], token_sems, 1, core_twin)
    along_z, over_x = {}, []

    def spread_piece(p, pieces):
        for t in (1, 2, 3):
            for i, (piece, sems) in enumerate(pieces):
                along_z[p, t, i] = send(piece, piece, sems, 1 + 3 * p + t, device(lax.rem(z + t, 4), x, y, core))
        for piece, sems in pieces:
            over_x.append(send(piece, piece, sems, 8 + 4 * p, x_twin))

    spread_piece(0, own)
    for copy in over_y:
        copy.wait_recv()
    spread_piece(1, [(whole.at[z, x, 1 - y], sems) for whole, sems in streams])
    token_y.wait_recv()
    token_next = send(all_tokens.at[1 - y, core], all_tokens.at[1 - y, core], token_sems, 2, core_twin)
    for p in (0, 1):
        row = y if p == 0 else 1 - y
        for t in (1, 2, 3):
            source = lax.rem(z + 4 - t, 4)
            for i, (whole, sems) in enumerate(streams):
                along_z[p, t, i].wait_recv()
                piece = whole.at[source, x, row]
                over_x.append(send(piece, piece, sems, 8 + 4 * p + t, x_twin))
    for copy in over_x + [token_own, token_next]:
        copy.wait_recv()
    for copy in sent + over_y + [token_y, token_own, token_next] + list(along_z.values()) + over_x:
        copy.wait_send()
    local[0].wait()


def gather_first(tokens, weight, vectors):
    _, local_rows, width = tokens.shape
    rows, columns = weight.shape
    anywhere = pl.BlockSpec(memory_space=pl.ANY)
    near = pl.BlockSpec(memory_space=pltpu.VMEM)
    sems = pltpu.SemaphoreType.DMA
    return pl.pallas_call(
        gather_kernel,
        name="gather_first",
        out_shape=(
            jax.ShapeDtypeStruct((2, 2, local_rows, width), BF16),
            jax.ShapeDtypeStruct((4, 2, 2, 2, rows, columns // 2), BF16),
            jax.ShapeDtypeStruct((4, 2, 2, 2, 8, 128), F32),
        ),
        in_specs=[near] * (2 + len(vectors)),
        out_specs=[anywhere] * 3,
        scratch_shapes=[pltpu.VMEM((8, 128), F32), sems((5,)), sems((3,)), sems((3,)), sems((18,)), sems((18,)), sems((16,)), sems((16,))],
        compiler_params=pltpu.CompilerParams(collective_id=1, has_side_effects=True),
    )(tokens, weight, *vectors)


def reduce_kernel(big_ref, flat_ref, tiny_ref, own_ref, other_ref, own_flat, other_flat, sum_ref, *scratch):
    z, x, y, core = position()
    meet(z, x, y, core)
    streams = []
    for i, source in enumerate((big_ref, flat_ref, tiny_ref)):
        streams.append((source,) + scratch[10 * i : 10 * i + 10])
    first_twin = device(z, x + (1 - core) * (1 - 2 * x), y + core * (1 - 2 * y), core)
    second_twin = device(z, x + core * (1 - 2 * x), y + (1 - core) * (1 - 2 * y), core)
    keep = (1 - core) * y + core * x
    order = (1, 2, 3, 0)
    one, two, three = {}, {}, {}
    for t in order:
        k = lax.rem(z + t, 4)
        for j in (0, 1):
            ix = (1 - core) * (1 - x) + core * j
            iy = (1 - core) * j + core * (1 - y)
            for i, (source, came_one, *_, leave, arrive) in enumerate(streams):
                one[t, j, i] = send(source.at[k, ix, iy], came_one.at[t, j], (leave, arrive), 2 * t + j, first_twin)
    for t in order:
        k = lax.rem(z + t, 4)
        for i, (source, came_one, sum_one, came_two, *_, leave, arrive) in enumerate(streams):
            for j in (0, 1):
                one[t, j, i].wait_recv()
                ix = (1 - core) * x + core * j
                iy = (1 - core) * j + core * y
                total = source[k, ix, iy].astype(F32) + came_one[t, j].astype(F32)
                sum_one[t, j] = total.astype(sum_one.dtype)
            two[t, i] = send(sum_one.at[t, 1 - keep], came_two.at[t], (leave, arrive), 8 + t, second_twin)
    for t in order:
        for i, (_, _, sum_one, came_two, sum_two, came_three, total_ref, _, leave, arrive) in enumerate(
            [(s[0], s[1], s[2], s[3], s[4], s[5], s[6], s[7], s[9], s[10]) for s in streams]
        ):
            two[t, i].wait_recv()
            total = sum_one[t, keep].astype(F32) + came_two[t].astype(F32)
            if t == 0:
                total_ref[...] = total
            else:
                sum_two[t - 1] = total.astype(sum_two.dtype)
                to = device(lax.rem(z + t, 4), x, y, core)
                three[t, i] = send(sum_two.at[t - 1], came_three.at[t - 1], (leave, arrive), 11 + t, to)
    last = []
    for i, s in enumerate(streams):
        came_three, total_ref, came_last, leave, arrive = s[5], s[6], s[7], s[9], s[10]
        for t in (1, 2, 3):
            three[t, i].wait_recv()
        total_ref[...] += sum(came_three[t].astype(F32) for t in range(3))
        rows = came_last.shape[0]
        piece = total_ref.at[pl.ds(pl.multiple_of((1 - core) * rows, 8), rows)]
        last.append(send(piece, came_last, (leave, arrive), 15, device(z, x, y, 1 - core)))
    rows = own_ref.shape[0]
    mine = pl.ds(pl.multiple_of(core * rows, 8), rows)
    own_ref[...] = streams[0][6][mine]
    own_flat[...] = streams[1][6][mine]
    for copy in last:
        copy.wait_recv()
    other_ref[...] = streams[0][7][...]
    other_flat[...] = streams[1][7][...]
    sum_ref[...] = streams[2][6][pl.ds(pl.multiple_of(core * 8, 8), 8)] + streams[2][7][...]
    for copy in list(one.values()) + list(two.values()) + list(three.values()) + last:
        copy.wait_send()


def reduce_last(big, flat, tiny):
    rows, half_columns = big.shape[3:]
    flat_columns = flat.shape[4]
    near = pl.BlockSpec(memory_space=pltpu.VMEM)
    scratch = []
    for shape, kind, kept in (
        ((rows, half_columns), BF16, (rows // 2, half_columns)),
        ((rows, flat_columns), BF16, (rows // 2, flat_columns)),
        ((16, 128), F32, (8, 128)),
    ):
        scratch += [
            pltpu.VMEM((4, 2) + shape, kind),
            pltpu.VMEM((4, 2) + shape, kind),
            pltpu.VMEM((4,) + shape, kind),
            pltpu.VMEM((3,) + shape, kind),
            pltpu.VMEM((3,) + shape, kind),
            pltpu.VMEM(shape, F32),
            pltpu.VMEM(kept, F32),
            pltpu.SemaphoreType.DMA((1,)),
            pltpu.SemaphoreType.DMA((16,)),
            pltpu.SemaphoreType.DMA((16,)),
        ]
    return pl.pallas_call(
        reduce_kernel,
        name="reduce_last",
        out_shape=(
            jax.ShapeDtypeStruct((rows // 2, half_columns), F32),
            jax.ShapeDtypeStruct((rows // 2, half_columns), F32),
            jax.ShapeDtypeStruct((rows // 2, flat_columns), F32),
            jax.ShapeDtypeStruct((rows // 2, flat_columns), F32),
            jax.ShapeDtypeStruct((8, 128), F32),
        ),
        in_specs=[near] * 3,
        out_specs=[near] * 5,
        scratch_shapes=scratch,
        compiler_params=pltpu.CompilerParams(collective_id=2, has_side_effects=True),
    )(big, flat, tiny)


def pack_kernel(output_ref, expand_ref, reduce_ref, out_ref):
    width = output_ref.shape[1]
    count = expand_ref.shape[1] // width
    out_ref[0] = output_ref[...]
    for j in range(count):
        out_ref[1 + j] = expand_ref[:, j * width : (j + 1) * width]
        out_ref[1 + count + j] = reduce_ref[j]


def pack_second(output_weight, expand_weight, reduce_weight):
    rows, width = output_weight.shape
    count = expand_weight.shape[1] // width
    near = pl.BlockSpec(memory_space=pltpu.VMEM)
    packed = pl.pallas_call(
        pack_kernel,
        name="pack_second",
        out_shape=jax.ShapeDtypeStruct((1 + 2 * count, rows, width), BF16),
        in_specs=[near] * 3,
        out_specs=near,
    )(output_weight, expand_weight, reduce_weight.reshape(count, rows, width))
    return packed.reshape(-1, width)


def gather_rows(shard):
    return lax.all_gather(shard, ("dp", "seq"), axis=0, tiled=True)


def scatter_sum(full):
    return lax.psum_scatter(full, ("dp", "seq"), scatter_dimension=0, tiled=True)


def local(
    tokens,
    cotangent,
    lengths,
    gain_first,
    shift_first,
    packed_weight,
    packed_bias,
    output_weight,
    output_bias,
    gain_second,
    shift_second,
    expand_weight,
    expand_bias,
    reduce_weight,
    reduce_bias,
):
    micro_count, local_rows, width = tokens.shape
    groups = lax.axis_size("seq")
    devices = groups * lax.axis_size("dp")
    share = groups // micro_count
    bucket = local_rows * groups
    hidden_width = expand_weight.shape[1]
    columns = width // share
    place = lax.axis_index("seq")
    mine, core = place // share, place % share
    swap_micro = [(s, (s + share) % groups) for s in range(groups)]
    swap_core = [(s, s ^ 1) for s in range(groups)]

    def swap_of(both):
        return lax.dynamic_index_in_dim(both, 1 - mine, 0, keepdims=False)

    def placed(both, came):
        kept = lax.dynamic_index_in_dim(both, mine, 0, keepdims=False)
        return jnp.stack([jnp.where(mine == 0, kept, came), jnp.where(mine == 0, came, kept)])

    def own_micro(both):
        return placed(both, lax.ppermute(swap_of(both), "seq", swap_micro))

    def home_micro(blocks):
        kept = lax.dynamic_index_in_dim(blocks, mine, 0, keepdims=False)
        sent = lax.dynamic_index_in_dim(blocks, 1 - mine, 0, keepdims=False)
        came = lax.ppermute(sent, "seq", swap_micro)
        return jnp.stack([jnp.where(mine == 0, kept, came), jnp.where(mine == 0, came, kept)])

    def interleave(own, other):
        first, second = jnp.where(core == 0, own, other), jnp.where(core == 0, other, own)
        return jnp.stack([first, second], axis=1).reshape((bucket,) + own.shape[2:])


    vectors = (gain_first, shift_first, packed_bias, output_bias, gain_second, shift_second, expand_bias, reduce_bias)
    sizes = [v.shape[0] for v in vectors]
    small_count = sum(sizes)
    pieces_per_row = hidden_width // width
    rows = output_weight.shape[0]
    own_kernels = devices == 32 and groups == 4
    if own_kernels:
        all_tokens, half_packed, all_tiny = gather_first(tokens, packed_weight, vectors)
        everyone = all_tokens.reshape(bucket, width)
        own_tokens = lax.dynamic_index_in_dim(all_tokens, core, 1, keepdims=False)
        half_packed = half_packed.reshape(width, 3 * columns)
    else:
        own_tokens = own_micro(tokens)
        everyone = interleave(own_tokens, lax.ppermute(own_tokens, "seq", swap_core))
        full_packed = gather_rows(packed_weight)
        half_packed = jnp.concatenate(
            [lax.dynamic_slice(full_packed, (0, part * width + core * columns), (width, columns)) for part in range(3)], axis=1
        )
        tiny = jnp.concatenate([jnp.pad(v.astype(F32), (0, 128 - v.shape[0])) for v in vectors]).reshape(8, 128)
        all_tiny = gather_rows(tiny)
    small_all = all_tiny.reshape(devices, 8, 128)
    if own_kernels:
        second_shard = pack_second(output_weight, expand_weight, reduce_weight)
    else:
        expand_blocks = [expand_weight[:, j * width : (j + 1) * width] for j in range(pieces_per_row)]
        second_shard = jnp.concatenate([output_weight] + expand_blocks + [reduce_weight])
    second = gather_rows(second_shard).reshape(devices, -1, width)
    full_output = second[:, :rows].reshape(width, width)
    full_expand = jnp.concatenate(
        [second[:, rows * (j + 1) : rows * (j + 2)].reshape(width, width) for j in range(pieces_per_row)], axis=1
    )
    full_reduce = second[:, rows * (pieces_per_row + 1) :].reshape(hidden_width, width)
    pieces = [small_all[:, i, :size].reshape(-1) for i, size in enumerate(sizes)]
    gain_one, shift_one, packed_shift, output_shift, gain_two, shift_two, expand_shift, reduce_shift = pieces

    places = jnp.arange(bucket, dtype=jnp.int32)
    bucket_lengths = lax.dynamic_index_in_dim(lengths, mine, 0, keepdims=False)[0]
    slot_count = lengths.shape[-1]
    ends = jnp.cumsum(bucket_lengths)
    past = (places[:, None] >= ends[None, :]).astype(jnp.int32)
    begins = jnp.sum(past * bucket_lengths[None, :], axis=1)
    block_ids = jnp.arange(bucket // TILE, dtype=jnp.int32)
    first_begin, last_begin = begins[::TILE], begins[TILE - 1 :: TILE]
    low = first_begin // TILE
    low_blocks = jnp.stack([low, jnp.minimum(-(-last_begin // TILE), block_ids)])
    high = jnp.sum((low[None, :] <= block_ids[:, None]).astype(jnp.int32), axis=1)
    free = jnp.sum((last_begin[None, :] <= block_ids[:, None] * TILE).astype(jnp.int32), axis=1)
    high_blocks = jnp.stack([high, jnp.clip(free, block_ids + 1, high)])
    begins = begins[None, :]
    valid_all = (jnp.sum(past, axis=1) < slot_count - 1).astype(F32).reshape(2, share, local_rows)
    valid = lax.dynamic_index_in_dim(valid_all, core, 1, keepdims=False).reshape(-1, 1)

    inputs = own_tokens.reshape(-1, width).astype(F32)
    normed_low = layer_norm(everyone.astype(F32), gain_one, shift_one).astype(BF16)
    bias_row = jnp.concatenate([packed_shift[:width], jnp.zeros((width,), F32), packed_shift[width:]])
    half_bias = jnp.concatenate(
        [lax.dynamic_slice(bias_row, (part * width + core * columns,), (columns,)) for part in range(3)]
    )
    packed = (jnp.dot(normed_low, half_packed, preferred_element_type=F32) + half_bias).astype(BF16)
    packed, cotangent_sent = lax.optimization_barrier((packed, swap_of(cotangent)))
    attended_heads, logsum = attend_forward(packed, low_blocks, begins)
    attended_heads, cotangent_came = lax.optimization_barrier(
        (attended_heads, lax.ppermute(cotangent_sent, "seq", swap_micro))
    )
    own_cotangent = placed(cotangent, cotangent_came)

    by_core = attended_heads.reshape(2, share, local_rows, columns)
    kept = lax.dynamic_index_in_dim(by_core, core, 1, keepdims=False)
    came = lax.ppermute(lax.dynamic_index_in_dim(by_core, 1 - core, 1, keepdims=False), "seq", swap_core)
    attended = jnp.concatenate(
        [jnp.where(core == 0, kept, came), jnp.where(core == 0, came, kept)], axis=-1
    ).reshape(-1, width)

    middle = inputs + BRANCH_SCALE * (
        jnp.dot(attended, full_output, preferred_element_type=F32) + output_shift
    )
    normed_two, norm_back_two = jax.vjp(layer_norm, middle, gain_two, shift_two)
    normed_two_low = normed_two.astype(BF16)
    activated, slope = gelu_and_slope(
        jnp.dot(normed_two_low, full_expand, preferred_element_type=F32) + expand_shift
    )
    active_low, slope_low = lax.optimization_barrier((activated.astype(BF16), slope.astype(BF16)))
    branch_out = jnp.dot(active_low, full_reduce, preferred_element_type=F32) + reduce_shift
    layer_rows = ((middle + BRANCH_SCALE * branch_out) * valid).astype(BF16)

    grad_rows = own_cotangent.reshape(-1, width).astype(F32) * valid
    grad_branch = (BRANCH_SCALE * grad_rows).astype(BF16)
    reduce_weight_grad = outer_sum(active_low, grad_branch)
    reduce_bias_grad = jnp.sum(grad_branch.astype(F32), axis=0)
    grad_hidden = (against_rows(grad_branch, full_reduce) * slope_low.astype(F32)).astype(BF16)
    expand_weight_grad = outer_sum(normed_two_low, grad_hidden)
    expand_bias_grad = jnp.sum(grad_hidden.astype(F32), axis=0)
    early = jnp.concatenate(
        [
            expand_weight_grad[:, j * width : (j + 1) * width].astype(BF16).reshape(devices, rows, width)
            for j in range(pieces_per_row)
        ]
        + [reduce_weight_grad.astype(BF16).reshape(devices, -1, width)],
        axis=1,
    )
    early, grad_hidden = lax.optimization_barrier((early, grad_hidden))
    early_sum = scatter_sum(early.reshape(-1, width)).astype(F32)
    middle_part, gain_two_grad, shift_two_grad = norm_back_two(against_rows(grad_hidden, full_expand))
    grad_middle = grad_rows + middle_part
    grad_proj = (BRANCH_SCALE * grad_middle).astype(BF16)
    output_weight_grad = outer_sum(attended, grad_proj).astype(BF16)
    output_bias_grad = jnp.sum(grad_proj.astype(F32), axis=0)
    grad_attended = against_rows(grad_proj, full_output).astype(BF16)
    take = lambda c: lax.dynamic_slice(grad_attended, (0, c * columns), (2 * local_rows, columns))
    kept = take(core).reshape(2, local_rows, columns)
    came = lax.ppermute(take(1 - core), "seq", swap_core).reshape(2, local_rows, columns)
    grad_heads = interleave(kept, came)
    grad_packed = attend_backward(packed, attended_heads, grad_heads, logsum, high_blocks, begins)
    half_grad = outer_sum(normed_low, grad_packed).astype(BF16)
    half_sums = jnp.sum(grad_packed.astype(F32), axis=0).reshape(3, columns)
    part_grad = against_rows(grad_packed, half_packed).astype(BF16)
    by_core = part_grad.reshape(2, share, local_rows, width)
    kept = lax.dynamic_index_in_dim(by_core, core, 1, keepdims=False)
    came = lax.ppermute(lax.dynamic_index_in_dim(by_core, 1 - core, 1, keepdims=False), "seq", swap_core)
    norm_grad = (kept.astype(F32) + came.astype(F32)).reshape(-1, width)
    _, norm_back_one = jax.vjp(layer_norm, inputs, gain_one, shift_one)
    input_part, gain_one_grad, shift_one_grad = norm_back_one(norm_grad)
    input_rows = (grad_middle + input_part).astype(BF16)

    layer_output = home_micro(layer_rows.reshape(2, local_rows, width))
    input_grad = home_micro(input_rows.reshape(2, local_rows, width))

    def spread(half):
        nothing = jnp.zeros_like(half)
        return [jnp.where(core == place_of, half, nothing) for place_of in range(share)]

    packed_bias_grad = jnp.concatenate([block for part in (0, 2) for block in spread(half_sums[part])])
    small_grads = [gain_one_grad, shift_one_grad, packed_bias_grad, output_bias_grad, gain_two_grad, shift_two_grad, expand_bias_grad, reduce_bias_grad]
    if own_kernels:
        small_rows = jnp.stack(
            [jnp.pad(g.reshape(devices, -1), ((0, 0), (0, 128 - g.size // devices))) for g in small_grads], axis=1
        ).reshape(4, 2, 2, share * 8, 128)
        half_output = lambda c: lax.dynamic_slice(output_weight_grad, (0, c * columns), (width, columns))
        came = lax.ppermute(half_output(1 - core), "seq", swap_core)
        flat = (half_output(core).astype(F32) + came.astype(F32)).astype(BF16)
        own_half, other_half, own_flat, other_flat, small_sum = reduce_last(
            half_grad.reshape(4, 2, 2, share * rows, 3 * columns), flat.reshape(4, 2, 2, share * rows, columns), small_rows
        )
        output_sum = jnp.concatenate([jnp.where(core == c, own_flat, other_flat) for c in range(share)], axis=1)
        packed_halves = [jnp.where(core == c, own_half, other_half) for c in range(share)]
        pieces = [small_sum[i, :size] for i, size in enumerate(sizes)]
    else:
        output_sum = scatter_sum(output_weight_grad).astype(F32)
        both_halves = scatter_sum(jnp.concatenate(spread(half_grad), axis=1)).astype(F32)
        packed_halves = [both_halves[:, c * 3 * columns : (c + 1) * 3 * columns] for c in range(share)]
        small_sum = scatter_sum(jnp.concatenate([g.reshape(devices, -1) for g in small_grads], axis=1))[0]
        pieces, at = [], 0
        for size in sizes:
            pieces.append(small_sum[at : at + size])
            at += size
    packed_sum = jnp.concatenate(
        [
            packed_halves[c][:, part * columns : (part + 1) * columns]
            for part in range(3)
            for c in range(share)
        ],
        axis=1,
    )
    expand_sum = jnp.concatenate(
        [early_sum[rows * j : rows * (j + 1)] for j in range(pieces_per_row)], axis=1
    )
    big = (early_sum[rows * pieces_per_row :], expand_sum, output_sum, packed_sum)
    return (
        layer_output,
        input_grad,
        pieces[0],
        pieces[1],
        big[3],
        pieces[2],
        big[2],
        pieces[3],
        pieces[4],
        pieces[5],
        big[1],
        pieces[6],
        big[0],
        pieces[7],
    )


def solution(mesh):
    both = ("dp", "seq")
    token_spec = P(None, both, None)
    vector, matrix = P(both), P(both, None)
    in_specs = (
        token_spec,
        token_spec,
        P(None, "dp", None),
        vector,
        vector,
        matrix,
        vector,
        matrix,
        vector,
        vector,
        vector,
        matrix,
        vector,
        matrix,
        vector,
    )
    out_specs = (
        token_spec,
        token_spec,
        vector,
        vector,
        matrix,
        vector,
        matrix,
        vector,
        vector,
        vector,
        matrix,
        vector,
        matrix,
        vector,
    )
    return jax.shard_map(local, mesh=mesh, in_specs=in_specs, out_specs=out_specs, check_vma=False)
```

```python
import functools

import jax
import jax.numpy as jnp
from jax import lax
from jax.experimental import pallas as pl
from jax.experimental.pallas import tpu as pltpu
from jax.sharding import PartitionSpec as P

H = 12
HD = 64
BRANCH_SCALE = 12 ** (-0.5)
EPSILON = 1e-05
GELU_SCALE = 0.7978845608028654
GELU_CUBE = 0.044715
F32 = jnp.float32
BF16 = jnp.bfloat16
TILE = 256
PAIR = 2 * HD
MASKED = -1e30


def outer_sum(first, second):
    return lax.dot_general(first, second, (((0,), (0,)), ((), ())), preferred_element_type=F32)


def against_rows(first, second):
    return lax.dot_general(first, second, (((1,), (1,)), ((), ())), preferred_element_type=F32)


def layer_norm(values, norm_gain, norm_shift):
    center = values - jnp.mean(values, axis=-1, keepdims=True)
    spread = jnp.mean(center * center, axis=-1, keepdims=True)
    return center * lax.rsqrt(spread + EPSILON) * norm_gain + norm_shift


def gelu_and_slope(values):
    square = values * values
    bend = jnp.tanh(values * (GELU_SCALE + (GELU_SCALE * GELU_CUBE) * square))
    half = 0.5 + 0.5 * bend
    active = values * half
    slope = half + active * (1.0 - half) * (2.0 * GELU_SCALE + (6.0 * GELU_SCALE * GELU_CUBE) * square)
    return active, slope


def split_pair(rows):
    lane = lax.broadcasted_iota(jnp.int32, rows.shape, 1)
    nothing = jnp.zeros_like(rows)
    return jnp.where(lane < HD, rows, nothing), jnp.where(lane < HD, nothing, rows)


def third(packed, part, g):
    first = part * (packed.shape[1] // 3) + g * PAIR
    return slice(first, first + PAIR)


def allowed_in(key_block, row_block, begins, diagonal):
    keys = key_block * TILE + lax.broadcasted_iota(jnp.int32, (TILE, TILE), 0)
    allowed = keys >= begins
    if diagonal:
        rows = row_block * TILE + lax.broadcasted_iota(jnp.int32, (TILE, TILE), 1)
        allowed = allowed & (keys <= rows)
    return allowed


def attend_kernel(bounds_ref, packed_ref, begin_ref, out_ref, logsum_ref, value_t, held):
    blocks = packed_ref.shape[0] // TILE
    groups = out_ref.shape[1] // PAIR
    count = 2 * groups
    for g in range(groups):
        for block in range(blocks):
            at = slice(block * TILE, (block + 1) * TILE)
            value_t[g * PAIR : (g + 1) * PAIR, at] = packed_ref[at, third(packed_ref, 2, g)].T

    def one_row_block(i, carry):
        here = pl.ds(pl.multiple_of(i * TILE, TILE), TILE)
        begins = begin_ref[:, here]
        heads = []
        for g in range(groups):
            heads += split_pair(packed_ref[here, third(packed_ref, 0, g)] * HD ** (-0.5))

        def score(j, tops, masked, diagonal):
            there = pl.ds(pl.multiple_of(j * TILE, TILE), TILE)
            allowed = allowed_in(j, i, begins, diagonal) if masked else None
            new_tops = []
            for h in range(count):
                g = h // 2
                key_rows = packed_ref[there, third(packed_ref, 1, g)]
                scores = against_rows(key_rows, heads[h])
                if masked:
                    scores = jnp.where(allowed, scores, MASKED)
                held[h, there, :] = scores
                top = jnp.max(scores, axis=0, keepdims=True)
                new_tops.append(top if tops is None else jnp.maximum(top, tops[h]))
            return tuple(new_tops)

        tops = score(i, None, True, True)
        tops = lax.fori_loop(bounds_ref[0, i], bounds_ref[1, i], lambda j, s: score(j, s, True, False), tops)
        tops = lax.fori_loop(bounds_ref[1, i], i, lambda j, s: score(j, s, False, False), tops)

        def mix(j, state):
            there = pl.ds(pl.multiple_of(j * TILE, TILE), TILE)
            new_state = []
            for h in range(count):
                weights = jnp.exp(held[h, there, :] - tops[h])
                total, mixed = state[h]
                total = total + jnp.sum(weights, axis=0, keepdims=True)
                mixed = mixed + jnp.dot(
                    value_t[h * HD : (h + 1) * HD, there], weights.astype(BF16), preferred_element_type=F32
                )
                new_state.append((total, mixed))
            return tuple(new_state)

        empty = (jnp.zeros((1, TILE), F32), jnp.zeros((HD, TILE), F32))
        state = lax.fori_loop(bounds_ref[0, i], i + 1, mix, (empty,) * count)
        for g in range(groups):
            mixed = [mix / total for total, mix in state[2 * g : 2 * g + 2]]
            out_ref[here, g * PAIR : (g + 1) * PAIR] = jnp.concatenate(mixed, axis=0).T.astype(BF16)
        logs = [top + jnp.log(total) for top, (total, _) in zip(tops, state)]
        logsum_ref[:, here] = jnp.concatenate(logs, axis=0)
        return carry

    lax.fori_loop(0, blocks, one_row_block, 0)


def attend_forward(packed, low_blocks, begins):
    bucket, columns = packed.shape
    groups = columns // 3 // PAIR
    return pl.pallas_call(
        attend_kernel,
        name="attend_forward",
        out_shape=(
            jax.ShapeDtypeStruct((bucket, columns // 3), BF16),
            jax.ShapeDtypeStruct((2 * groups, bucket), F32),
        ),
        grid_spec=pltpu.PrefetchScalarGridSpec(
            num_scalar_prefetch=1,
            grid=(1,),
            in_specs=[
                pl.BlockSpec((bucket, columns), lambda g, low: (0, 0)),
                pl.BlockSpec((1, bucket), lambda g, low: (0, 0)),
            ],
            out_specs=[
                pl.BlockSpec((bucket, columns // 3), lambda g, low: (0, 0)),
                pl.BlockSpec((2 * groups, bucket), lambda g, low: (0, 0)),
            ],
            scratch_shapes=[
                pltpu.VMEM((groups * PAIR, bucket), BF16),
                pltpu.VMEM((2 * groups, bucket, TILE), F32),
            ],
        ),
        cost_estimate=pl.CostEstimate(
            flops=4 * 2 * groups * bucket * bucket * HD // 2,
            bytes_accessed=bucket * columns * 3,
            transcendentals=2 * groups * bucket * bucket // 2,
        ),
    )(low_blocks, packed, begins)


def attend_back_kernel(
    bounds_ref, packed_ref, o_ref, go_ref, begin_ref, logsum_ref, out_ref, key_t, query_t, delta
):
    blocks = packed_ref.shape[0] // TILE
    groups = o_ref.shape[1] // PAIR
    half = lax.broadcasted_iota(jnp.int32, (8, PAIR), 1) // HD
    picks = (half == lax.broadcasted_iota(jnp.int32, (8, PAIR), 0)).astype(F32).astype(BF16)
    for g in range(groups):
        column = slice(g * PAIR, (g + 1) * PAIR)
        for block in range(blocks):
            at = slice(block * TILE, (block + 1) * TILE)
            key_t[column, at] = packed_ref[at, third(packed_ref, 1, g)].T
            query_t[column, at] = jnp.zeros((PAIR, TILE), F32)
            product = o_ref[at, column].astype(F32) * go_ref[at, column].astype(F32)
            coarse = product.astype(BF16)
            fine = (product - coarse.astype(F32)).astype(BF16)
            delta[g * 8 : (g + 1) * 8, at] = against_rows(picks, coarse) + against_rows(picks, fine)

    def one_key_block(j, carry):
        there = pl.ds(pl.multiple_of(j * TILE, TILE), TILE)

        def visit(i, state, masked, diagonal):
            here = pl.ds(pl.multiple_of(i * TILE, TILE), TILE)
            allowed = allowed_in(j, i, begin_ref[:, here], diagonal) if masked else None
            new_state = []
            for g in range(groups):
                key_rows = packed_ref[there, third(packed_ref, 1, g)]
                value_rows = packed_ref[there, third(packed_ref, 2, g)]
                queries = split_pair(packed_ref[here, third(packed_ref, 0, g)] * HD ** (-0.5))
                grads = split_pair(go_ref[here, g * PAIR : (g + 1) * PAIR])
                key_grad, value_grad = state[g]
                for which in range(2):
                    h = 2 * g + which
                    scores = against_rows(key_rows, queries[which])
                    if masked:
                        scores = jnp.where(allowed, scores, MASKED)
                    probs = jnp.exp(scores - logsum_ref[h : h + 1, here])
                    grad_probs = against_rows(value_rows, grads[which])
                    row = 8 * g + which
                    grad_scores = (probs * (grad_probs - delta[row : row + 1, here])).astype(BF16)
                    value_grad = value_grad + jnp.dot(
                        probs.astype(BF16), grads[which], preferred_element_type=F32
                    )
                    key_grad = key_grad + jnp.dot(
                        grad_scores, queries[which], preferred_element_type=F32
                    )
                    at = slice(h * HD, (h + 1) * HD)
                    query_t[at, here] += jnp.dot(
                        key_t[at, there], grad_scores, preferred_element_type=F32
                    )
                new_state.append((key_grad, value_grad))
            return tuple(new_state)

        zero = jnp.zeros((TILE, PAIR), F32)
        state = visit(j, ((zero, zero),) * groups, True, True)
        state = lax.fori_loop(j + 1, bounds_ref[1, j], lambda i, s: visit(i, s, False, False), state)
        state = lax.fori_loop(bounds_ref[1, j], bounds_ref[0, j], lambda i, s: visit(i, s, True, False), state)
        for g in range(groups):
            out_ref[there, third(packed_ref, 1, g)] = state[g][0].astype(BF16)
            out_ref[there, third(packed_ref, 2, g)] = state[g][1].astype(BF16)
        return carry

    lax.fori_loop(0, blocks, one_key_block, 0)
    for g in range(groups):
        for block in range(blocks):
            at = slice(block * TILE, (block + 1) * TILE)
            rows = query_t[g * PAIR : (g + 1) * PAIR, at].T * HD ** (-0.5)
            out_ref[at, third(packed_ref, 0, g)] = rows.astype(BF16)


def attend_backward(packed, attended, grad_attended, logsum, high_blocks, begins):
    bucket, columns = packed.shape
    groups = columns // 3 // PAIR
    whole = lambda rows, width: pl.BlockSpec((rows, width), lambda g, high: (0, 0))
    return pl.pallas_call(
        attend_back_kernel,
        name="attend_backward",
        out_shape=jax.ShapeDtypeStruct((bucket, columns), BF16),
        grid_spec=pltpu.PrefetchScalarGridSpec(
            num_scalar_prefetch=1,
            grid=(1,),
            in_specs=[
                whole(bucket, columns),
                whole(bucket, columns // 3),
                whole(bucket, columns // 3),
                whole(1, bucket),
                whole(2 * groups, bucket),
            ],
            out_specs=whole(bucket, columns),
            scratch_shapes=[
                pltpu.VMEM((groups * PAIR, bucket), BF16),
                pltpu.VMEM((groups * PAIR, bucket), F32),
                pltpu.VMEM((groups * 8, bucket), F32),
            ],
        ),
        cost_estimate=pl.CostEstimate(
            flops=groups * bucket * bucket,
            bytes_accessed=bucket * columns,
            transcendentals=bucket,
        ),
    )(high_blocks, packed, attended, grad_attended, begins, logsum)


def position():
    dp, seq = lax.axis_index("dp"), lax.axis_index("seq")
    return lax.div(dp, 2), lax.rem(dp, 2), lax.div(seq, 2), lax.rem(seq, 2)


def device(z, x, y, core):
    return (2 * z + x, 2 * y + core)


def send(source, target, semaphores, index, to):
    leave, arrive = semaphores
    copy = pltpu.make_async_remote_copy(
        src_ref=source,
        dst_ref=target,
        send_sem=leave.at[index],
        recv_sem=arrive.at[index],
        device_id=to,
        device_id_type=pl.DeviceIdType.MESH,
    )
    copy.start()
    return copy


def meet(z, x, y, core):
    barrier = pltpu.get_barrier_semaphore()
    others = [device(z, 1 - x, y, core), device(z, x, 1 - y, core), device(z, x, y, 1 - core)]
    others += [device(lax.rem(z + t, 4), x, y, core) for t in (1, 2, 3)]
    for other in others:
        pl.semaphore_signal(barrier, inc=1, device_id=other, device_id_type=pl.DeviceIdType.MESH)
    pl.semaphore_wait(barrier, len(others))


def gather_kernel(
    token_ref, weight_ref, *rest
):
    vector_refs, (all_tokens, all_half, all_tiny, tiny_ref, local_sem), semaphores = rest[:8], rest[8:13], rest[13:]
    z, x, y, core = position()
    tiny_ref[...] = jnp.zeros_like(tiny_ref)
    for i, vector_ref in enumerate(vector_refs):
        tiny_ref[i, : vector_ref.shape[0]] = vector_ref[...].astype(F32)
    token_sems, half_sems, tiny_sems = [semaphores[2 * i : 2 * i + 2] for i in range(3)]
    meet(z, x, y, core)
    core_twin, y_twin, x_twin = device(z, x, y, 1 - core), device(z, x, 1 - y, core), device(z, 1 - x, y, core)
    columns = all_half.shape[5] // 3

    def weight_part(part, c):
        first = pl.multiple_of(part * 2 * columns + c * columns, PAIR)
        return weight_ref.at[:, pl.ds(first, columns)]

    streams = [(all_half, half_sems), (all_tiny, tiny_sems)]
    sent = []
    local = [
        pltpu.make_async_copy(token_ref.at[y], all_tokens.at[y, core], local_sem.at[0]),
        pltpu.make_async_copy(tiny_ref, all_tiny.at[z, x, y, core], local_sem.at[1]),
    ]
    swaps = [send(tiny_ref, all_tiny.at[z, x, y, core], tiny_sems, 0, core_twin)]
    for part in range(3):
        mine = all_half.at[z, x, y, core, :, part * columns : (part + 1) * columns]
        local.append(pltpu.make_async_copy(weight_part(part, core), mine, local_sem.at[2 + part]))
        swaps.append(send(weight_part(part, 1 - core), mine, half_sems, (0, 16, 17)[part], core_twin))
    for copy in local[1:] + local[:1]:
        copy.start()
    for copy in local[1:]:
        copy.wait()
    for copy in swaps:
        copy.wait_recv()
    sent += swaps
    own = [(whole.at[z, x, y], sems) for whole, sems in streams]
    over_y = [send(piece, piece, sems, 1, y_twin) for piece, sems in own]
    token_y = send(token_ref.at[1 - y], all_tokens.at[y, core], token_sems, 0, y_twin)
    token_own = send(token_ref.at[y], all_tokens.at[y, core], token_sems, 1, core_twin)
    along_z, over_x = {}, []

    def spread_piece(p, pieces):
        for t in (1, 2, 3):
            for i, (piece, sems) in enumerate(pieces):
                along_z[p, t, i] = send(piece, piece, sems, 1 + 3 * p + t, device(lax.rem(z + t, 4), x, y, core))
        for piece, sems in pieces:
            over_x.append(send(piece, piece, sems, 8 + 4 * p, x_twin))

    spread_piece(0, own)
    for copy in over_y:
        copy.wait_recv()
    spread_piece(1, [(whole.at[z, x, 1 - y], sems) for whole, sems in streams])
    token_y.wait_recv()
    token_next = send(all_tokens.at[1 - y, core], all_tokens.at[1 - y, core], token_sems, 2, core_twin)
    for p in (0, 1):
        row = y if p == 0 else 1 - y
        for t in (1, 2, 3):
            source = lax.rem(z + 4 - t, 4)
            for i, (whole, sems) in enumerate(streams):
                along_z[p, t, i].wait_recv()
                piece = whole.at[source, x, row]
                over_x.append(send(piece, piece, sems, 8 + 4 * p + t, x_twin))
    for copy in over_x + [token_own, token_next]:
        copy.wait_recv()
    for copy in sent + over_y + [token_y, token_own, token_next] + list(along_z.values()) + over_x:
        copy.wait_send()
    local[0].wait()


def gather_first(tokens, weight, vectors):
    _, local_rows, width = tokens.shape
    rows, columns = weight.shape
    anywhere = pl.BlockSpec(memory_space=pl.ANY)
    near = pl.BlockSpec(memory_space=pltpu.VMEM)
    sems = pltpu.SemaphoreType.DMA
    return pl.pallas_call(
        gather_kernel,
        name="gather_first",
        out_shape=(
            jax.ShapeDtypeStruct((2, 2, local_rows, width), BF16),
            jax.ShapeDtypeStruct((4, 2, 2, 2, rows, columns // 2), BF16),
            jax.ShapeDtypeStruct((4, 2, 2, 2, 8, 128), F32),
        ),
        in_specs=[near] * (2 + len(vectors)),
        out_specs=[anywhere] * 3,
        scratch_shapes=[pltpu.VMEM((8, 128), F32), sems((5,)), sems((3,)), sems((3,)), sems((18,)), sems((18,)), sems((16,)), sems((16,))],
        compiler_params=pltpu.CompilerParams(collective_id=1, has_side_effects=True),
    )(tokens, weight, *vectors)


def reduce_kernel(big_ref, flat_ref, tiny_ref, own_ref, other_ref, own_flat, other_flat, sum_ref, *scratch):
    z, x, y, core = position()
    meet(z, x, y, core)
    streams = []
    for i, source in enumerate((big_ref, flat_ref, tiny_ref)):
        streams.append((source,) + scratch[10 * i : 10 * i + 10])
    first_twin, second_twin = device(z, 1 - x, y, core), device(z, x, 1 - y, core)
    order = (1, 2, 3, 0)
    one, two, three = {}, {}, {}
    for t in order:
        k = lax.rem(z + t, 4)
        for j in (0, 1):
            for i, (source, came_one, *_, leave, arrive) in enumerate(streams):
                one[t, j, i] = send(source.at[k, 1 - x, j], came_one.at[t, j], (leave, arrive), 2 * t + j, first_twin)
    for t in order:
        k = lax.rem(z + t, 4)
        for i, (source, came_one, sum_one, came_two, *_, leave, arrive) in enumerate(streams):
            for j in (0, 1):
                one[t, j, i].wait_recv()
                total = source[k, x, j].astype(F32) + came_one[t, j].astype(F32)
                sum_one[t, j] = total.astype(sum_one.dtype)
            two[t, i] = send(sum_one.at[t, 1 - y], came_two.at[t], (leave, arrive), 8 + t, second_twin)
    for t in order:
        for i, (_, _, sum_one, came_two, sum_two, came_three, total_ref, _, leave, arrive) in enumerate(
            [(s[0], s[1], s[2], s[3], s[4], s[5], s[6], s[7], s[9], s[10]) for s in streams]
        ):
            two[t, i].wait_recv()
            total = sum_one[t, y].astype(F32) + came_two[t].astype(F32)
            if t == 0:
                total_ref[...] = total
            else:
                sum_two[t - 1] = total.astype(sum_two.dtype)
                to = device(lax.rem(z + t, 4), x, y, core)
                three[t, i] = send(sum_two.at[t - 1], came_three.at[t - 1], (leave, arrive), 11 + t, to)
    last = []
    for i, s in enumerate(streams):
        came_three, total_ref, came_last, leave, arrive = s[5], s[6], s[7], s[9], s[10]
        for t in (1, 2, 3):
            three[t, i].wait_recv()
        total_ref[...] += sum(came_three[t].astype(F32) for t in range(3))
        rows = came_last.shape[0]
        piece = total_ref.at[pl.ds(pl.multiple_of((1 - core) * rows, 8), rows)]
        last.append(send(piece, came_last, (leave, arrive), 15, device(z, x, y, 1 - core)))
    rows = own_ref.shape[0]
    mine = pl.ds(pl.multiple_of(core * rows, 8), rows)
    own_ref[...] = streams[0][6][mine]
    own_flat[...] = streams[1][6][mine]
    for copy in last:
        copy.wait_recv()
    other_ref[...] = streams[0][7][...]
    other_flat[...] = streams[1][7][...]
    sum_ref[...] = streams[2][6][pl.ds(pl.multiple_of(core * 8, 8), 8)] + streams[2][7][...]
    for copy in list(one.values()) + list(two.values()) + list(three.values()) + last:
        copy.wait_send()


def reduce_last(big, flat, tiny):
    rows, half_columns = big.shape[3:]
    flat_columns = flat.shape[4]
    near = pl.BlockSpec(memory_space=pltpu.VMEM)
    scratch = []
    for shape, kind, kept in (
        ((rows, half_columns), BF16, (rows // 2, half_columns)),
        ((rows, flat_columns), BF16, (rows // 2, flat_columns)),
        ((16, 128), F32, (8, 128)),
    ):
        scratch += [
            pltpu.VMEM((4, 2) + shape, kind),
            pltpu.VMEM((4, 2) + shape, kind),
            pltpu.VMEM((4,) + shape, kind),
            pltpu.VMEM((3,) + shape, kind),
            pltpu.VMEM((3,) + shape, kind),
            pltpu.VMEM(shape, F32),
            pltpu.VMEM(kept, F32),
            pltpu.SemaphoreType.DMA((1,)),
            pltpu.SemaphoreType.DMA((16,)),
            pltpu.SemaphoreType.DMA((16,)),
        ]
    return pl.pallas_call(
        reduce_kernel,
        name="reduce_last",
        out_shape=(
            jax.ShapeDtypeStruct((rows // 2, half_columns), F32),
            jax.ShapeDtypeStruct((rows // 2, half_columns), F32),
            jax.ShapeDtypeStruct((rows // 2, flat_columns), F32),
            jax.ShapeDtypeStruct((rows // 2, flat_columns), F32),
            jax.ShapeDtypeStruct((8, 128), F32),
        ),
        in_specs=[near] * 3,
        out_specs=[near] * 5,
        scratch_shapes=scratch,
        compiler_params=pltpu.CompilerParams(collective_id=2, has_side_effects=True),
    )(big, flat, tiny)


def pack_kernel(output_ref, expand_ref, reduce_ref, out_ref):
    width = output_ref.shape[1]
    count = expand_ref.shape[1] // width
    out_ref[0] = output_ref[...]
    for j in range(count):
        out_ref[1 + j] = expand_ref[:, j * width : (j + 1) * width]
        out_ref[1 + count + j] = reduce_ref[j]


def pack_second(output_weight, expand_weight, reduce_weight):
    rows, width = output_weight.shape
    count = expand_weight.shape[1] // width
    near = pl.BlockSpec(memory_space=pltpu.VMEM)
    packed = pl.pallas_call(
        pack_kernel,
        name="pack_second",
        out_shape=jax.ShapeDtypeStruct((1 + 2 * count, rows, width), BF16),
        in_specs=[near] * 3,
        out_specs=near,
    )(output_weight, expand_weight, reduce_weight.reshape(count, rows, width))
    return packed.reshape(-1, width)


def gather_rows(shard):
    return lax.all_gather(shard, ("dp", "seq"), axis=0, tiled=True)


def scatter_sum(full):
    return lax.psum_scatter(full, ("dp", "seq"), scatter_dimension=0, tiled=True)


def local(
    tokens,
    cotangent,
    lengths,
    gain_first,
    shift_first,
    packed_weight,
    packed_bias,
    output_weight,
    output_bias,
    gain_second,
    shift_second,
    expand_weight,
    expand_bias,
    reduce_weight,
    reduce_bias,
):
    micro_count, local_rows, width = tokens.shape
    groups = lax.axis_size("seq")
    devices = groups * lax.axis_size("dp")
    share = groups // micro_count
    bucket = local_rows * groups
    hidden_width = expand_weight.shape[1]
    columns = width // share
    place = lax.axis_index("seq")
    mine, core = place // share, place % share
    swap_micro = [(s, (s + share) % groups) for s in range(groups)]
    swap_core = [(s, s ^ 1) for s in range(groups)]

    def swap_of(both):
        return lax.dynamic_index_in_dim(both, 1 - mine, 0, keepdims=False)

    def placed(both, came):
        kept = lax.dynamic_index_in_dim(both, mine, 0, keepdims=False)
        return jnp.where((jnp.arange(micro_count) == mine)[:, None, None], kept[None], came[None])

    def own_micro(both):
        return placed(both, lax.ppermute(swap_of(both), "seq", swap_micro))

    def home_micro(blocks):
        kept = lax.dynamic_index_in_dim(blocks, mine, 0, keepdims=False)
        sent = lax.dynamic_index_in_dim(blocks, 1 - mine, 0, keepdims=False)
        came = lax.ppermute(sent, "seq", swap_micro)
        return jnp.where((jnp.arange(micro_count) == mine)[:, None, None], kept[None], came[None])

    def interleave(own, other):
        here = (jnp.arange(share) == core)[None, :, None, None]
        return jnp.where(here, own[:, None], other[:, None]).reshape((bucket,) + own.shape[2:])


    vectors = (gain_first, shift_first, packed_bias, output_bias, gain_second, shift_second, expand_bias, reduce_bias)
    sizes = [v.shape[0] for v in vectors]
    small_count = sum(sizes)
    pieces_per_row = hidden_width // width
    rows = output_weight.shape[0]
    own_kernels = devices == 32 and groups == 4
    if own_kernels:
        all_tokens, half_packed, all_tiny = gather_first(tokens, packed_weight, vectors)
        everyone = all_tokens.reshape(bucket, width)
        own_tokens = lax.dynamic_index_in_dim(all_tokens, core, 1, keepdims=False)
        half_packed = half_packed.reshape(width, 3 * columns)
    else:
        own_tokens = own_micro(tokens)
        everyone = interleave(own_tokens, lax.ppermute(own_tokens, "seq", swap_core))
        full_packed = gather_rows(packed_weight)
        half_packed = jnp.concatenate(
            [lax.dynamic_slice(full_packed, (0, part * width + core * columns), (width, columns)) for part in range(3)], axis=1
        )
        tiny = jnp.concatenate([jnp.pad(v.astype(F32), (0, 128 - v.shape[0])) for v in vectors]).reshape(8, 128)
        all_tiny = gather_rows(tiny)
    small_all = all_tiny.reshape(devices, 8, 128)
    if own_kernels:
        second_shard = pack_second(output_weight, expand_weight, reduce_weight)
    else:
        expand_blocks = [expand_weight[:, j * width : (j + 1) * width] for j in range(pieces_per_row)]
        second_shard = jnp.concatenate([output_weight] + expand_blocks + [reduce_weight])
    second = gather_rows(second_shard).reshape(devices, -1, width)
    full_output = second[:, :rows].reshape(width, width)
    full_expand = jnp.concatenate(
        [second[:, rows * (j + 1) : rows * (j + 2)].reshape(width, width) for j in range(pieces_per_row)], axis=1
    )
    full_reduce = second[:, rows * (pieces_per_row + 1) :].reshape(hidden_width, width)
    pieces = [small_all[:, i, :size].reshape(-1) for i, size in enumerate(sizes)]
    gain_one, shift_one, packed_shift, output_shift, gain_two, shift_two, expand_shift, reduce_shift = pieces

    places = jnp.arange(bucket, dtype=jnp.int32)
    bucket_lengths = lax.dynamic_index_in_dim(lengths, mine, 0, keepdims=False)[0]
    slot_count = lengths.shape[-1]
    ends = jnp.cumsum(bucket_lengths)
    past = (places[:, None] >= ends[None, :]).astype(jnp.int32)
    begins = jnp.sum(past * bucket_lengths[None, :], axis=1)
    block_ids = jnp.arange(bucket // TILE, dtype=jnp.int32)
    first_begin, last_begin = begins[::TILE], begins[TILE - 1 :: TILE]
    low = first_begin // TILE
    low_blocks = jnp.stack([low, jnp.minimum(-(-last_begin // TILE), block_ids)])
    high = jnp.sum((low[None, :] <= block_ids[:, None]).astype(jnp.int32), axis=1)
    free = jnp.sum((last_begin[None, :] <= block_ids[:, None] * TILE).astype(jnp.int32), axis=1)
    high_blocks = jnp.stack([high, jnp.clip(free, block_ids + 1, high)])
    begins = begins[None, :]
    valid_all = (jnp.sum(past, axis=1) < slot_count - 1).astype(F32).reshape(2, share, local_rows)
    valid = lax.dynamic_index_in_dim(valid_all, core, 1, keepdims=False).reshape(-1, 1)

    inputs = own_tokens.reshape(-1, width).astype(F32)
    normed_low = layer_norm(everyone.astype(F32), gain_one, shift_one).astype(BF16)
    bias_row = jnp.concatenate([packed_shift[:width], jnp.zeros((width,), F32), packed_shift[width:]])
    half_bias = jnp.concatenate(
        [lax.dynamic_slice(bias_row, (part * width + core * columns,), (columns,)) for part in range(3)]
    )
    packed = (jnp.dot(normed_low, half_packed, preferred_element_type=F32) + half_bias).astype(BF16)
    packed, cotangent_sent = lax.optimization_barrier((packed, swap_of(cotangent)))
    attended_heads, logsum = attend_forward(packed, low_blocks, begins)
    attended_heads, cotangent_came = lax.optimization_barrier(
        (attended_heads, lax.ppermute(cotangent_sent, "seq", swap_micro))
    )
    own_cotangent = placed(cotangent, cotangent_came)

    by_core = attended_heads.reshape(2, share, local_rows, columns)
    kept = lax.dynamic_index_in_dim(by_core, core, 1, keepdims=False)
    came = lax.ppermute(lax.dynamic_index_in_dim(by_core, 1 - core, 1, keepdims=False), "seq", swap_core)
    attended = jnp.concatenate(
        [jnp.where(core == 0, kept, came), jnp.where(core == 0, came, kept)], axis=-1
    ).reshape(-1, width)

    middle = inputs + BRANCH_SCALE * (
        jnp.dot(attended, full_output, preferred_element_type=F32) + output_shift
    )
    normed_two, norm_back_two = jax.vjp(layer_norm, middle, gain_two, shift_two)
    normed_two_low = normed_two.astype(BF16)
    activated, slope = gelu_and_slope(
        jnp.dot(normed_two_low, full_expand, preferred_element_type=F32) + expand_shift
    )
    active_low, slope_low = lax.optimization_barrier((activated.astype(BF16), slope.astype(BF16)))
    branch_out = jnp.dot(active_low, full_reduce, preferred_element_type=F32) + reduce_shift
    layer_rows = ((middle + BRANCH_SCALE * branch_out) * valid).astype(BF16)

    grad_rows = own_cotangent.reshape(-1, width).astype(F32) * valid
    grad_branch = (BRANCH_SCALE * grad_rows).astype(BF16)
    reduce_weight_grad = outer_sum(active_low, grad_branch)
    reduce_bias_grad = jnp.sum(grad_branch.astype(F32), axis=0)
    grad_hidden = (against_rows(grad_branch, full_reduce) * slope_low.astype(F32)).astype(BF16)
    expand_weight_grad = outer_sum(normed_two_low, grad_hidden)
    expand_bias_grad = jnp.sum(grad_hidden.astype(F32), axis=0)
    early = jnp.concatenate(
        [
            expand_weight_grad[:, j * width : (j + 1) * width].astype(BF16).reshape(devices, rows, width)
            for j in range(pieces_per_row)
        ]
        + [reduce_weight_grad.astype(BF16).reshape(devices, -1, width)],
        axis=1,
    )
    early, grad_hidden = lax.optimization_barrier((early, grad_hidden))
    early_sum = scatter_sum(early.reshape(-1, width)).astype(F32)
    middle_part, gain_two_grad, shift_two_grad = norm_back_two(against_rows(grad_hidden, full_expand))
    grad_middle = grad_rows + middle_part
    grad_proj = (BRANCH_SCALE * grad_middle).astype(BF16)
    output_weight_grad = outer_sum(attended, grad_proj).astype(BF16)
    output_bias_grad = jnp.sum(grad_proj.astype(F32), axis=0)
    grad_attended = against_rows(grad_proj, full_output).astype(BF16)
    take = lambda c: lax.dynamic_slice(grad_attended, (0, c * columns), (2 * local_rows, columns))
    kept = take(core).reshape(2, local_rows, columns)
    came = lax.ppermute(take(1 - core), "seq", swap_core).reshape(2, local_rows, columns)
    grad_heads = interleave(kept, came)
    grad_packed = attend_backward(packed, attended_heads, grad_heads, logsum, high_blocks, begins)
    half_grad = outer_sum(normed_low, grad_packed).astype(BF16)
    half_sums = jnp.sum(grad_packed.astype(F32), axis=0).reshape(3, columns)
    part_grad = against_rows(grad_packed, half_packed).astype(BF16)
    by_core = part_grad.reshape(2, share, local_rows, width)
    kept = lax.dynamic_index_in_dim(by_core, core, 1, keepdims=False)
    came = lax.ppermute(lax.dynamic_index_in_dim(by_core, 1 - core, 1, keepdims=False), "seq", swap_core)
    norm_grad = (kept.astype(F32) + came.astype(F32)).reshape(-1, width)
    _, norm_back_one = jax.vjp(layer_norm, inputs, gain_one, shift_one)
    input_part, gain_one_grad, shift_one_grad = norm_back_one(norm_grad)
    input_rows = (grad_middle + input_part).astype(BF16)

    layer_output = home_micro(layer_rows.reshape(2, local_rows, width))
    input_grad = home_micro(input_rows.reshape(2, local_rows, width))

    def spread(half):
        nothing = jnp.zeros_like(half)
        return [jnp.where(core == place_of, half, nothing) for place_of in range(share)]

    packed_bias_grad = jnp.concatenate([block for part in (0, 2) for block in spread(half_sums[part])])
    small_grads = [gain_one_grad, shift_one_grad, packed_bias_grad, output_bias_grad, gain_two_grad, shift_two_grad, expand_bias_grad, reduce_bias_grad]
    if own_kernels:
        small_rows = jnp.stack(
            [jnp.pad(g.reshape(devices, -1), ((0, 0), (0, 128 - g.size // devices))) for g in small_grads], axis=1
        ).reshape(4, 2, 2, share * 8, 128)
        half_output = lambda c: lax.dynamic_slice(output_weight_grad, (0, c * columns), (width, columns))
        came = lax.ppermute(half_output(1 - core), "seq", swap_core)
        flat = (half_output(core).astype(F32) + came.astype(F32)).astype(BF16)
        own_half, other_half, own_flat, other_flat, small_sum = reduce_last(
            half_grad.reshape(4, 2, 2, share * rows, 3 * columns), flat.reshape(4, 2, 2, share * rows, columns), small_rows
        )
        output_sum = jnp.concatenate([jnp.where(core == c, own_flat, other_flat) for c in range(share)], axis=1)
        packed_halves = [jnp.where(core == c, own_half, other_half) for c in range(share)]
        pieces = [small_sum[i, :size] for i, size in enumerate(sizes)]
    else:
        output_sum = scatter_sum(output_weight_grad).astype(F32)
        both_halves = scatter_sum(jnp.concatenate(spread(half_grad), axis=1)).astype(F32)
        packed_halves = [both_halves[:, c * 3 * columns : (c + 1) * 3 * columns] for c in range(share)]
        small_sum = scatter_sum(jnp.concatenate([g.reshape(devices, -1) for g in small_grads], axis=1))[0]
        pieces, at = [], 0
        for size in sizes:
            pieces.append(small_sum[at : at + size])
            at += size
    packed_sum = jnp.concatenate(
        [
            packed_halves[c][:, part * columns : (part + 1) * columns]
            for part in range(3)
            for c in range(share)
        ],
        axis=1,
    )
    expand_sum = jnp.concatenate(
        [early_sum[rows * j : rows * (j + 1)] for j in range(pieces_per_row)], axis=1
    )
    big = (early_sum[rows * pieces_per_row :], expand_sum, output_sum, packed_sum)
    return (
        layer_output,
        input_grad,
        pieces[0],
        pieces[1],
        big[3],
        pieces[2],
        big[2],
        pieces[3],
        pieces[4],
        pieces[5],
        big[1],
        pieces[6],
        big[0],
        pieces[7],
    )


def solution(mesh):
    both = ("dp", "seq")
    token_spec = P(None, both, None)
    vector, matrix = P(both), P(both, None)
    in_specs = (
        token_spec,
        token_spec,
        P(None, "dp", None),
        vector,
        vector,
        matrix,
        vector,
        matrix,
        vector,
        vector,
        vector,
        matrix,
        vector,
        matrix,
        vector,
    )
    out_specs = (
        token_spec,
        token_spec,
        vector,
        vector,
        matrix,
        vector,
        matrix,
        vector,
        vector,
        vector,
        matrix,
        vector,
        matrix,
        vector,
    )
    return jax.shard_map(local, mesh=mesh, in_specs=in_specs, out_specs=out_specs, check_vma=False)
```

```python
import functools

import jax
import jax.numpy as jnp
from jax import lax
from jax.experimental import pallas as pl
from jax.experimental.pallas import tpu as pltpu
from jax.sharding import PartitionSpec as P

H = 12
HD = 64
BRANCH_SCALE = 12 ** (-0.5)
EPSILON = 1e-05
GELU_SCALE = 0.7978845608028654
GELU_CUBE = 0.044715
F32 = jnp.float32
BF16 = jnp.bfloat16
TILE = 256
PAIR = 2 * HD
MASKED = -1e30


def outer_sum(first, second):
    return lax.dot_general(first, second, (((0,), (0,)), ((), ())), preferred_element_type=F32)


def against_rows(first, second):
    return lax.dot_general(first, second, (((1,), (1,)), ((), ())), preferred_element_type=F32)


def layer_norm(values, norm_gain, norm_shift):
    center = values - jnp.mean(values, axis=-1, keepdims=True)
    spread = jnp.mean(center * center, axis=-1, keepdims=True)
    return center * lax.rsqrt(spread + EPSILON) * norm_gain + norm_shift


def gelu_and_slope(values):
    square = values * values
    bend = jnp.tanh(values * (GELU_SCALE + (GELU_SCALE * GELU_CUBE) * square))
    half = 0.5 + 0.5 * bend
    active = values * half
    slope = half + active * (1.0 - half) * (2.0 * GELU_SCALE + (6.0 * GELU_SCALE * GELU_CUBE) * square)
    return active, slope


def split_pair(rows):
    lane = lax.broadcasted_iota(jnp.int32, rows.shape, 1)
    nothing = jnp.zeros_like(rows)
    return jnp.where(lane < HD, rows, nothing), jnp.where(lane < HD, nothing, rows)


def third(packed, part, g):
    first = part * (packed.shape[1] // 3) + g * PAIR
    return slice(first, first + PAIR)


def allowed_in(key_block, row_block, begins, diagonal):
    keys = key_block * TILE + lax.broadcasted_iota(jnp.int32, (TILE, TILE), 0)
    allowed = keys >= begins
    if diagonal:
        rows = row_block * TILE + lax.broadcasted_iota(jnp.int32, (TILE, TILE), 1)
        allowed = allowed & (keys <= rows)
    return allowed


def attend_kernel(bounds_ref, packed_ref, begin_ref, out_ref, logsum_ref, value_t, held):
    blocks = packed_ref.shape[0] // TILE
    groups = out_ref.shape[1] // PAIR
    count = 2 * groups
    for g in range(groups):
        for block in range(blocks):
            at = slice(block * TILE, (block + 1) * TILE)
            value_t[g * PAIR : (g + 1) * PAIR, at] = packed_ref[at, third(packed_ref, 2, g)].T

    def one_row_block(i, carry):
        here = pl.ds(pl.multiple_of(i * TILE, TILE), TILE)
        begins = begin_ref[:, here]
        heads = []
        for g in range(groups):
            heads += split_pair(packed_ref[here, third(packed_ref, 0, g)] * HD ** (-0.5))

        def score(j, tops, masked, diagonal):
            there = pl.ds(pl.multiple_of(j * TILE, TILE), TILE)
            allowed = allowed_in(j, i, begins, diagonal) if masked else None
            new_tops = []
            for h in range(count):
                g = h // 2
                key_rows = packed_ref[there, third(packed_ref, 1, g)]
                scores = against_rows(key_rows, heads[h])
                if masked:
                    scores = jnp.where(allowed, scores, MASKED)
                held[h, there, :] = scores
                top = jnp.max(scores, axis=0, keepdims=True)
                new_tops.append(top if tops is None else jnp.maximum(top, tops[h]))
            return tuple(new_tops)

        tops = score(i, None, True, True)
        tops = lax.fori_loop(bounds_ref[0, i], bounds_ref[1, i], lambda j, s: score(j, s, True, False), tops)
        tops = lax.fori_loop(bounds_ref[1, i], i, lambda j, s: score(j, s, False, False), tops)

        def mix(j, state):
            there = pl.ds(pl.multiple_of(j * TILE, TILE), TILE)
            new_state = []
            for h in range(count):
                weights = jnp.exp(held[h, there, :] - tops[h])
                total, mixed = state[h]
                total = total + jnp.sum(weights, axis=0, keepdims=True)
                mixed = mixed + jnp.dot(
                    value_t[h * HD : (h + 1) * HD, there], weights.astype(BF16), preferred_element_type=F32
                )
                new_state.append((total, mixed))
            return tuple(new_state)

        empty = (jnp.zeros((1, TILE), F32), jnp.zeros((HD, TILE), F32))
        state = lax.fori_loop(bounds_ref[0, i], i + 1, mix, (empty,) * count)
        for g in range(groups):
            mixed = [mix / total for total, mix in state[2 * g : 2 * g + 2]]
            out_ref[here, g * PAIR : (g + 1) * PAIR] = jnp.concatenate(mixed, axis=0).T.astype(BF16)
        logs = [top + jnp.log(total) for top, (total, _) in zip(tops, state)]
        logsum_ref[:, here] = jnp.concatenate(logs, axis=0)
        return carry

    lax.fori_loop(0, blocks, one_row_block, 0)


def attend_forward(packed, low_blocks, begins):
    bucket, columns = packed.shape
    groups = columns // 3 // PAIR
    return pl.pallas_call(
        attend_kernel,
        name="attend_forward",
        out_shape=(
            jax.ShapeDtypeStruct((bucket, columns // 3), BF16),
            jax.ShapeDtypeStruct((2 * groups, bucket), F32),
        ),
        grid_spec=pltpu.PrefetchScalarGridSpec(
            num_scalar_prefetch=1,
            grid=(1,),
            in_specs=[
                pl.BlockSpec((bucket, columns), lambda g, low: (0, 0)),
                pl.BlockSpec((1, bucket), lambda g, low: (0, 0)),
            ],
            out_specs=[
                pl.BlockSpec((bucket, columns // 3), lambda g, low: (0, 0)),
                pl.BlockSpec((2 * groups, bucket), lambda g, low: (0, 0)),
            ],
            scratch_shapes=[
                pltpu.VMEM((groups * PAIR, bucket), BF16),
                pltpu.VMEM((2 * groups, bucket, TILE), F32),
            ],
        ),
        cost_estimate=pl.CostEstimate(
            flops=4 * 2 * groups * bucket * bucket * HD // 2,
            bytes_accessed=bucket * columns * 3,
            transcendentals=2 * groups * bucket * bucket // 2,
        ),
    )(low_blocks, packed, begins)


def attend_back_kernel(
    bounds_ref, packed_ref, o_ref, go_ref, begin_ref, logsum_ref, out_ref, key_t, query_t, delta
):
    blocks = packed_ref.shape[0] // TILE
    groups = o_ref.shape[1] // PAIR
    half = lax.broadcasted_iota(jnp.int32, (8, PAIR), 1) // HD
    picks = (half == lax.broadcasted_iota(jnp.int32, (8, PAIR), 0)).astype(F32).astype(BF16)
    for g in range(groups):
        column = slice(g * PAIR, (g + 1) * PAIR)
        for block in range(blocks):
            at = slice(block * TILE, (block + 1) * TILE)
            key_t[column, at] = packed_ref[at, third(packed_ref, 1, g)].T
            query_t[column, at] = jnp.zeros((PAIR, TILE), F32)
            product = o_ref[at, column].astype(F32) * go_ref[at, column].astype(F32)
            coarse = product.astype(BF16)
            fine = (product - coarse.astype(F32)).astype(BF16)
            delta[g * 8 : (g + 1) * 8, at] = against_rows(picks, coarse) + against_rows(picks, fine)

    def one_key_block(j, carry):
        there = pl.ds(pl.multiple_of(j * TILE, TILE), TILE)

        def visit(i, state, masked, diagonal):
            here = pl.ds(pl.multiple_of(i * TILE, TILE), TILE)
            allowed = allowed_in(j, i, begin_ref[:, here], diagonal) if masked else None
            new_state = []
            for g in range(groups):
                key_rows = packed_ref[there, third(packed_ref, 1, g)]
                value_rows = packed_ref[there, third(packed_ref, 2, g)]
                queries = split_pair(packed_ref[here, third(packed_ref, 0, g)] * HD ** (-0.5))
                grads = split_pair(go_ref[here, g * PAIR : (g + 1) * PAIR])
                key_grad, value_grad = state[g]
                for which in range(2):
                    h = 2 * g + which
                    scores = against_rows(key_rows, queries[which])
                    if masked:
                        scores = jnp.where(allowed, scores, MASKED)
                    probs = jnp.exp(scores - logsum_ref[h : h + 1, here])
                    grad_probs = against_rows(value_rows, grads[which])
                    row = 8 * g + which
                    grad_scores = (probs * (grad_probs - delta[row : row + 1, here])).astype(BF16)
                    value_grad = value_grad + jnp.dot(
                        probs.astype(BF16), grads[which], preferred_element_type=F32
                    )
                    key_grad = key_grad + jnp.dot(
                        grad_scores, queries[which], preferred_element_type=F32
                    )
                    at = slice(h * HD, (h + 1) * HD)
                    query_t[at, here] += jnp.dot(
                        key_t[at, there], grad_scores, preferred_element_type=F32
                    )
                new_state.append((key_grad, value_grad))
            return tuple(new_state)

        zero = jnp.zeros((TILE, PAIR), F32)
        state = visit(j, ((zero, zero),) * groups, True, True)
        state = lax.fori_loop(j + 1, bounds_ref[1, j], lambda i, s: visit(i, s, False, False), state)
        state = lax.fori_loop(bounds_ref[1, j], bounds_ref[0, j], lambda i, s: visit(i, s, True, False), state)
        for g in range(groups):
            out_ref[there, third(packed_ref, 1, g)] = state[g][0].astype(BF16)
            out_ref[there, third(packed_ref, 2, g)] = state[g][1].astype(BF16)
        return carry

    lax.fori_loop(0, blocks, one_key_block, 0)
    for g in range(groups):
        for block in range(blocks):
            at = slice(block * TILE, (block + 1) * TILE)
            rows = query_t[g * PAIR : (g + 1) * PAIR, at].T * HD ** (-0.5)
            out_ref[at, third(packed_ref, 0, g)] = rows.astype(BF16)


def attend_backward(packed, attended, grad_attended, logsum, high_blocks, begins):
    bucket, columns = packed.shape
    groups = columns // 3 // PAIR
    whole = lambda rows, width: pl.BlockSpec((rows, width), lambda g, high: (0, 0))
    return pl.pallas_call(
        attend_back_kernel,
        name="attend_backward",
        out_shape=jax.ShapeDtypeStruct((bucket, columns), BF16),
        grid_spec=pltpu.PrefetchScalarGridSpec(
            num_scalar_prefetch=1,
            grid=(1,),
            in_specs=[
                whole(bucket, columns),
                whole(bucket, columns // 3),
                whole(bucket, columns // 3),
                whole(1, bucket),
                whole(2 * groups, bucket),
            ],
            out_specs=whole(bucket, columns),
            scratch_shapes=[
                pltpu.VMEM((groups * PAIR, bucket), BF16),
                pltpu.VMEM((groups * PAIR, bucket), F32),
                pltpu.VMEM((groups * 8, bucket), F32),
            ],
        ),
        cost_estimate=pl.CostEstimate(
            flops=groups * bucket * bucket,
            bytes_accessed=bucket * columns,
            transcendentals=bucket,
        ),
    )(high_blocks, packed, attended, grad_attended, begins, logsum)


def position():
    dp, seq = lax.axis_index("dp"), lax.axis_index("seq")
    return lax.div(dp, 2), lax.rem(dp, 2), lax.div(seq, 2), lax.rem(seq, 2)


def device(z, x, y, core):
    return (2 * z + x, 2 * y + core)


def send(source, target, semaphores, index, to):
    leave, arrive = semaphores
    copy = pltpu.make_async_remote_copy(
        src_ref=source,
        dst_ref=target,
        send_sem=leave.at[index],
        recv_sem=arrive.at[index],
        device_id=to,
        device_id_type=pl.DeviceIdType.MESH,
    )
    copy.start()
    return copy


def meet(z, x, y, core):
    barrier = pltpu.get_barrier_semaphore()
    others = [device(z, 1 - x, y, core), device(z, x, 1 - y, core), device(z, x, y, 1 - core)]
    others += [device(lax.rem(z + t, 4), x, y, core) for t in (1, 2, 3)]
    for other in others:
        pl.semaphore_signal(barrier, inc=1, device_id=other, device_id_type=pl.DeviceIdType.MESH)
    pl.semaphore_wait(barrier, len(others))


def gather_kernel(
    token_ref, weight_ref, *rest
):
    vector_refs, (all_tokens, all_half, all_tiny, tiny_ref, local_sem), semaphores = rest[:8], rest[8:13], rest[13:]
    z, x, y, core = position()
    tiny_ref[...] = jnp.zeros_like(tiny_ref)
    for i, vector_ref in enumerate(vector_refs):
        tiny_ref[i, : vector_ref.shape[0]] = vector_ref[...].astype(F32)
    token_sems, half_sems, tiny_sems = [semaphores[2 * i : 2 * i + 2] for i in range(3)]
    meet(z, x, y, core)
    core_twin, y_twin, x_twin = device(z, x, y, 1 - core), device(z, x, 1 - y, core), device(z, 1 - x, y, core)
    columns = all_half.shape[5] // 3

    def weight_part(part, c):
        first = pl.multiple_of(part * 2 * columns + c * columns, PAIR)
        return weight_ref.at[:, pl.ds(first, columns)]

    streams = [(all_half, half_sems), (all_tiny, tiny_sems)]
    sent = []
    local = [
        pltpu.make_async_copy(token_ref.at[y], all_tokens.at[y, core], local_sem.at[0]),
        pltpu.make_async_copy(tiny_ref, all_tiny.at[z, x, y, core], local_sem.at[1]),
    ]
    swaps = [send(tiny_ref, all_tiny.at[z, x, y, core], tiny_sems, 0, core_twin)]
    for part in range(3):
        mine = all_half.at[z, x, y, core, :, part * columns : (part + 1) * columns]
        local.append(pltpu.make_async_copy(weight_part(part, core), mine, local_sem.at[2 + part]))
        swaps.append(send(weight_part(part, 1 - core), mine, half_sems, (0, 16, 17)[part], core_twin))
    for copy in local[1:] + local[:1]:
        copy.start()
    for copy in local[1:]:
        copy.wait()
    for copy in swaps:
        copy.wait_recv()
    sent += swaps
    own = [(whole.at[z, x, y], sems) for whole, sems in streams]
    over_y = [send(piece, piece, sems, 1, y_twin) for piece, sems in own]
    token_y = send(token_ref.at[1 - y], all_tokens.at[y, core], token_sems, 0, y_twin)
    token_own = send(token_ref.at[y], all_tokens.at[y, core], token_sems, 1, core_twin)
    along_z, over_x = {}, []

    def spread_piece(p, pieces):
        for t in (1, 2, 3):
            for i, (piece, sems) in enumerate(pieces):
                along_z[p, t, i] = send(piece, piece, sems, 1 + 3 * p + t, device(lax.rem(z + t, 4), x, y, core))
        for piece, sems in pieces:
            over_x.append(send(piece, piece, sems, 8 + 4 * p, x_twin))

    spread_piece(0, own)
    for copy in over_y:
        copy.wait_recv()
    spread_piece(1, [(whole.at[z, x, 1 - y], sems) for whole, sems in streams])
    token_y.wait_recv()
    token_next = send(all_tokens.at[1 - y, core], all_tokens.at[1 - y, core], token_sems, 2, core_twin)
    for p in (0, 1):
        row = y if p == 0 else 1 - y
        for t in (1, 2, 3):
            source = lax.rem(z + 4 - t, 4)
            for i, (whole, sems) in enumerate(streams):
                along_z[p, t, i].wait_recv()
                piece = whole.at[source, x, row]
                over_x.append(send(piece, piece, sems, 8 + 4 * p + t, x_twin))
    for copy in over_x + [token_own, token_next]:
        copy.wait_recv()
    for copy in sent + over_y + [token_y, token_own, token_next] + list(along_z.values()) + over_x:
        copy.wait_send()
    local[0].wait()


def gather_first(tokens, weight, vectors):
    _, local_rows, width = tokens.shape
    rows, columns = weight.shape
    anywhere = pl.BlockSpec(memory_space=pl.ANY)
    near = pl.BlockSpec(memory_space=pltpu.VMEM)
    sems = pltpu.SemaphoreType.DMA
    return pl.pallas_call(
        gather_kernel,
        name="gather_first",
        out_shape=(
            jax.ShapeDtypeStruct((2, 2, local_rows, width), BF16),
            jax.ShapeDtypeStruct((4, 2, 2, 2, rows, columns // 2), BF16),
            jax.ShapeDtypeStruct((4, 2, 2, 2, 8, 128), F32),
        ),
        in_specs=[near] * (2 + len(vectors)),
        out_specs=[anywhere] * 3,
        scratch_shapes=[pltpu.VMEM((8, 128), F32), sems((5,)), sems((3,)), sems((3,)), sems((18,)), sems((18,)), sems((16,)), sems((16,))],
        compiler_params=pltpu.CompilerParams(collective_id=1, has_side_effects=True),
    )(tokens, weight, *vectors)


def reduce_kernel(big_ref, flat_ref, tiny_ref, own_ref, other_ref, own_flat, other_flat, sum_ref, *scratch):
    z, x, y, core = position()
    meet(z, x, y, core)
    streams = []
    for i, source in enumerate((big_ref, flat_ref, tiny_ref)):
        streams.append((source,) + scratch[10 * i : 10 * i + 10])
    first_twin, second_twin = device(z, 1 - x, y, core), device(z, x, 1 - y, core)
    order = (1, 2, 3, 0)
    one, two, three = {}, {}, {}
    for t in order:
        k = lax.rem(z + t, 4)
        for j in (0, 1):
            for i, (source, came_one, *_, leave, arrive) in enumerate(streams):
                one[t, j, i] = send(source.at[k, 1 - x, j], came_one.at[t, j], (leave, arrive), 2 * t + j, first_twin)
    for t in order:
        k = lax.rem(z + t, 4)
        for i, (source, came_one, sum_one, came_two, *_, leave, arrive) in enumerate(streams):
            for j in (0, 1):
                one[t, j, i].wait_recv()
                total = source[k, x, j].astype(F32) + came_one[t, j].astype(F32)
                sum_one[t, j] = total.astype(sum_one.dtype)
            two[t, i] = send(sum_one.at[t, 1 - y], came_two.at[t], (leave, arrive), 8 + t, second_twin)
    for t in order:
        for i, (_, _, sum_one, came_two, sum_two, came_three, total_ref, _, leave, arrive) in enumerate(
            [(s[0], s[1], s[2], s[3], s[4], s[5], s[6], s[7], s[9], s[10]) for s in streams]
        ):
            two[t, i].wait_recv()
            total = sum_one[t, y].astype(F32) + came_two[t].astype(F32)
            if t == 0:
                total_ref[...] = total
            else:
                sum_two[t - 1] = total.astype(sum_two.dtype)
                to = device(lax.rem(z + t, 4), x, y, core)
                three[t, i] = send(sum_two.at[t - 1], came_three.at[t - 1], (leave, arrive), 11 + t, to)
    last = []
    for i, s in enumerate(streams):
        came_three, total_ref, came_last, leave, arrive = s[5], s[6], s[7], s[9], s[10]
        for t in (1, 2, 3):
            three[t, i].wait_recv()
        total_ref[...] += sum(came_three[t].astype(F32) for t in range(3))
        rows = came_last.shape[0]
        piece = total_ref.at[pl.ds(pl.multiple_of((1 - core) * rows, 8), rows)]
        last.append(send(piece, came_last, (leave, arrive), 15, device(z, x, y, 1 - core)))
    rows = own_ref.shape[0]
    mine = pl.ds(pl.multiple_of(core * rows, 8), rows)
    own_ref[...] = streams[0][6][mine]
    own_flat[...] = streams[1][6][mine]
    for copy in last:
        copy.wait_recv()
    other_ref[...] = streams[0][7][...]
    other_flat[...] = streams[1][7][...]
    sum_ref[...] = streams[2][6][pl.ds(pl.multiple_of(core * 8, 8), 8)] + streams[2][7][...]
    for copy in list(one.values()) + list(two.values()) + list(three.values()) + last:
        copy.wait_send()


def reduce_last(big, flat, tiny):
    rows, half_columns = big.shape[3:]
    flat_columns = flat.shape[4]
    near = pl.BlockSpec(memory_space=pltpu.VMEM)
    scratch = []
    for shape, kind, kept in (
        ((rows, half_columns), BF16, (rows // 2, half_columns)),
        ((rows, flat_columns), BF16, (rows // 2, flat_columns)),
        ((16, 128), F32, (8, 128)),
    ):
        scratch += [
            pltpu.VMEM((4, 2) + shape, kind),
            pltpu.VMEM((4, 2) + shape, kind),
            pltpu.VMEM((4,) + shape, kind),
            pltpu.VMEM((3,) + shape, kind),
            pltpu.VMEM((3,) + shape, kind),
            pltpu.VMEM(shape, F32),
            pltpu.VMEM(kept, F32),
            pltpu.SemaphoreType.DMA((1,)),
            pltpu.SemaphoreType.DMA((16,)),
            pltpu.SemaphoreType.DMA((16,)),
        ]
    return pl.pallas_call(
        reduce_kernel,
        name="reduce_last",
        out_shape=(
            jax.ShapeDtypeStruct((rows // 2, half_columns), F32),
            jax.ShapeDtypeStruct((rows // 2, half_columns), F32),
            jax.ShapeDtypeStruct((rows // 2, flat_columns), F32),
            jax.ShapeDtypeStruct((rows // 2, flat_columns), F32),
            jax.ShapeDtypeStruct((8, 128), F32),
        ),
        in_specs=[near] * 3,
        out_specs=[near] * 5,
        scratch_shapes=scratch,
        compiler_params=pltpu.CompilerParams(collective_id=2, has_side_effects=True),
    )(big, flat, tiny)


def pack_kernel(output_ref, expand_ref, reduce_ref, out_ref):
    width = output_ref.shape[1]
    count = expand_ref.shape[1] // width
    out_ref[0] = output_ref[...]
    for j in range(count):
        out_ref[1 + j] = expand_ref[:, j * width : (j + 1) * width]
        out_ref[1 + count + j] = reduce_ref[j]


def pack_second(output_weight, expand_weight, reduce_weight):
    rows, width = output_weight.shape
    count = expand_weight.shape[1] // width
    near = pl.BlockSpec(memory_space=pltpu.VMEM)
    packed = pl.pallas_call(
        pack_kernel,
        name="pack_second",
        out_shape=jax.ShapeDtypeStruct((1 + 2 * count, rows, width), BF16),
        in_specs=[near] * 3,
        out_specs=near,
    )(output_weight, expand_weight, reduce_weight.reshape(count, rows, width))
    return packed.reshape(-1, width)


def gather_rows(shard):
    return lax.all_gather(shard, ("dp", "seq"), axis=0, tiled=True)


def scatter_sum(full):
    return lax.psum_scatter(full, ("dp", "seq"), scatter_dimension=0, tiled=True)


def local(
    tokens,
    cotangent,
    lengths,
    gain_first,
    shift_first,
    packed_weight,
    packed_bias,
    output_weight,
    output_bias,
    gain_second,
    shift_second,
    expand_weight,
    expand_bias,
    reduce_weight,
    reduce_bias,
):
    micro_count, local_rows, width = tokens.shape
    groups = lax.axis_size("seq")
    devices = groups * lax.axis_size("dp")
    share = groups // micro_count
    bucket = local_rows * groups
    hidden_width = expand_weight.shape[1]
    columns = width // share
    place = lax.axis_index("seq")
    mine, core = place // share, place % share
    swap_micro = [(s, (s + share) % groups) for s in range(groups)]
    swap_core = [(s, s ^ 1) for s in range(groups)]

    def swap_of(both):
        return lax.dynamic_index_in_dim(both, 1 - mine, 0, keepdims=False)

    def placed(both, came):
        kept = lax.dynamic_index_in_dim(both, mine, 0, keepdims=False)
        return jnp.stack([jnp.where(mine == 0, kept, came), jnp.where(mine == 0, came, kept)])

    def own_micro(both):
        return placed(both, lax.ppermute(swap_of(both), "seq", swap_micro))

    def home_micro(blocks):
        kept = lax.dynamic_index_in_dim(blocks, mine, 0, keepdims=False)
        sent = lax.dynamic_index_in_dim(blocks, 1 - mine, 0, keepdims=False)
        came = lax.ppermute(sent, "seq", swap_micro)
        return jnp.stack([jnp.where(mine == 0, kept, came), jnp.where(mine == 0, came, kept)])

    def interleave(own, other):
        first, second = jnp.where(core == 0, own, other), jnp.where(core == 0, other, own)
        return jnp.stack([first, second], axis=1).reshape((bucket,) + own.shape[2:])


    vectors = (gain_first, shift_first, packed_bias, output_bias, gain_second, shift_second, expand_bias, reduce_bias)
    sizes = [v.shape[0] for v in vectors]
    small_count = sum(sizes)
    pieces_per_row = hidden_width // width
    rows = output_weight.shape[0]
    own_kernels = devices == 32 and groups == 4
    if own_kernels:
        all_tokens, half_packed, all_tiny = gather_first(tokens, packed_weight, vectors)
        everyone = all_tokens.reshape(bucket, width)
        own_tokens = lax.dynamic_index_in_dim(all_tokens, core, 1, keepdims=False)
        half_packed = half_packed.reshape(width, 3 * columns)
    else:
        own_tokens = own_micro(tokens)
        everyone = interleave(own_tokens, lax.ppermute(own_tokens, "seq", swap_core))
        full_packed = gather_rows(packed_weight)
        half_packed = jnp.concatenate(
            [lax.dynamic_slice(full_packed, (0, part * width + core * columns), (width, columns)) for part in range(3)], axis=1
        )
        tiny = jnp.concatenate([jnp.pad(v.astype(F32), (0, 128 - v.shape[0])) for v in vectors]).reshape(8, 128)
        all_tiny = gather_rows(tiny)
    small_all = all_tiny.reshape(devices, 8, 128)
    if own_kernels:
        second_shard = pack_second(output_weight, expand_weight, reduce_weight)
    else:
        expand_blocks = [expand_weight[:, j * width : (j + 1) * width] for j in range(pieces_per_row)]
        second_shard = jnp.concatenate([output_weight] + expand_blocks + [reduce_weight])
    second = gather_rows(second_shard).reshape(devices, -1, width)
    full_output = second[:, :rows].reshape(width, width)
    full_expand = jnp.concatenate(
        [second[:, rows * (j + 1) : rows * (j + 2)].reshape(width, width) for j in range(pieces_per_row)], axis=1
    )
    full_reduce = second[:, rows * (pieces_per_row + 1) :].reshape(hidden_width, width)
    pieces = [small_all[:, i, :size].reshape(-1) for i, size in enumerate(sizes)]
    gain_one, shift_one, packed_shift, output_shift, gain_two, shift_two, expand_shift, reduce_shift = pieces

    places = jnp.arange(bucket, dtype=jnp.int32)
    bucket_lengths = lax.dynamic_index_in_dim(lengths, mine, 0, keepdims=False)[0]
    slot_count = lengths.shape[-1]
    ends = jnp.cumsum(bucket_lengths)
    past = (places[:, None] >= ends[None, :]).astype(jnp.int32)
    begins = jnp.sum(past * bucket_lengths[None, :], axis=1)
    block_ids = jnp.arange(bucket // TILE, dtype=jnp.int32)
    first_begin, last_begin = begins[::TILE], begins[TILE - 1 :: TILE]
    low = first_begin // TILE
    low_blocks = jnp.stack([low, jnp.minimum(-(-last_begin // TILE), block_ids)])
    high = jnp.sum((low[None, :] <= block_ids[:, None]).astype(jnp.int32), axis=1)
    free = jnp.sum((last_begin[None, :] <= block_ids[:, None] * TILE).astype(jnp.int32), axis=1)
    high_blocks = jnp.stack([high, jnp.clip(free, block_ids + 1, high)])
    begins = begins[None, :]
    valid_all = (jnp.sum(past, axis=1) < slot_count - 1).astype(F32).reshape(2, share, local_rows)
    valid = lax.dynamic_index_in_dim(valid_all, core, 1, keepdims=False).reshape(-1, 1)

    inputs = own_tokens.reshape(-1, width).astype(F32)
    normed_low = layer_norm(everyone.astype(F32), gain_one, shift_one).astype(BF16)
    bias_row = jnp.concatenate([packed_shift[:width], jnp.zeros((width,), F32), packed_shift[width:]])
    half_bias = jnp.concatenate(
        [lax.dynamic_slice(bias_row, (part * width + core * columns,), (columns,)) for part in range(3)]
    )
    packed = (jnp.dot(normed_low, half_packed, preferred_element_type=F32) + half_bias).astype(BF16)
    packed, cotangent_sent = lax.optimization_barrier((packed, swap_of(cotangent)))
    attended_heads, logsum = attend_forward(packed, low_blocks, begins)
    attended_heads, cotangent_came = lax.optimization_barrier(
        (attended_heads, lax.ppermute(cotangent_sent, "seq", swap_micro))
    )
    own_cotangent = placed(cotangent, cotangent_came)

    by_core = attended_heads.reshape(2, share, local_rows, columns)
    kept = lax.dynamic_index_in_dim(by_core, core, 1, keepdims=False)
    came = lax.ppermute(lax.dynamic_index_in_dim(by_core, 1 - core, 1, keepdims=False), "seq", swap_core)
    attended = jnp.concatenate(
        [jnp.where(core == 0, kept, came), jnp.where(core == 0, came, kept)], axis=-1
    ).reshape(-1, width)

    middle = inputs + BRANCH_SCALE * (
        jnp.dot(attended, full_output, preferred_element_type=F32) + output_shift
    )
    normed_two, norm_back_two = jax.vjp(layer_norm, middle, gain_two, shift_two)
    normed_two_low = normed_two.astype(BF16)
    activated, slope = gelu_and_slope(
        jnp.dot(normed_two_low, full_expand, preferred_element_type=F32) + expand_shift
    )
    active_low, slope_low = lax.optimization_barrier((activated.astype(BF16), slope.astype(BF16)))
    branch_out = jnp.dot(active_low, full_reduce, preferred_element_type=F32) + reduce_shift
    layer_rows = ((middle + BRANCH_SCALE * branch_out) * valid).astype(BF16)

    grad_rows = own_cotangent.reshape(-1, width).astype(F32) * valid
    grad_branch = (BRANCH_SCALE * grad_rows).astype(BF16)
    reduce_weight_grad = outer_sum(active_low, grad_branch)
    reduce_bias_grad = jnp.sum(grad_branch.astype(F32), axis=0)
    grad_hidden = (against_rows(grad_branch, full_reduce) * slope_low.astype(F32)).astype(BF16)
    expand_weight_grad = outer_sum(normed_two_low, grad_hidden)
    expand_bias_grad = jnp.sum(grad_hidden.astype(F32), axis=0)
    early = jnp.concatenate(
        [
            expand_weight_grad[:, j * width : (j + 1) * width].astype(BF16).reshape(devices, rows, width)
            for j in range(pieces_per_row)
        ]
        + [reduce_weight_grad.astype(BF16).reshape(devices, -1, width)],
        axis=1,
    )
    early, grad_hidden = lax.optimization_barrier((early, grad_hidden))
    early_sum = scatter_sum(early.reshape(-1, width)).astype(F32)
    middle_part, gain_two_grad, shift_two_grad = norm_back_two(against_rows(grad_hidden, full_expand))
    grad_middle = grad_rows + middle_part
    grad_proj = (BRANCH_SCALE * grad_middle).astype(BF16)
    output_weight_grad = outer_sum(attended, grad_proj).astype(BF16)
    output_bias_grad = jnp.sum(grad_proj.astype(F32), axis=0)
    grad_attended = against_rows(grad_proj, full_output).astype(BF16)
    take = lambda c: lax.dynamic_slice(grad_attended, (0, c * columns), (2 * local_rows, columns))
    kept = take(core).reshape(2, local_rows, columns)
    came = lax.ppermute(take(1 - core), "seq", swap_core).reshape(2, local_rows, columns)
    grad_heads = interleave(kept, came)
    grad_packed = attend_backward(packed, attended_heads, grad_heads, logsum, high_blocks, begins)
    half_grad = outer_sum(normed_low, grad_packed).astype(BF16)
    half_sums = jnp.sum(grad_packed.astype(F32), axis=0).reshape(3, columns)
    part_grad = against_rows(grad_packed, half_packed).astype(BF16)
    by_core = part_grad.reshape(2, share, local_rows, width)
    kept = lax.dynamic_index_in_dim(by_core, core, 1, keepdims=False)
    came = lax.ppermute(lax.dynamic_index_in_dim(by_core, 1 - core, 1, keepdims=False), "seq", swap_core)
    norm_grad = (kept.astype(F32) + came.astype(F32)).reshape(-1, width)
    _, norm_back_one = jax.vjp(layer_norm, inputs, gain_one, shift_one)
    input_part, gain_one_grad, shift_one_grad = norm_back_one(norm_grad)
    input_rows = (grad_middle + input_part).astype(BF16)

    layer_output = home_micro(layer_rows.reshape(2, local_rows, width))
    input_grad = home_micro(input_rows.reshape(2, local_rows, width))

    def spread(half):
        nothing = jnp.zeros_like(half)
        return [jnp.where(core == place_of, half, nothing) for place_of in range(share)]

    packed_bias_grad = jnp.concatenate([block for part in (0, 2) for block in spread(half_sums[part])])
    small_grads = [gain_one_grad, shift_one_grad, packed_bias_grad, output_bias_grad, gain_two_grad, shift_two_grad, expand_bias_grad, reduce_bias_grad]
    if own_kernels:
        small_rows = jnp.stack(
            [jnp.pad(g.reshape(devices, -1), ((0, 0), (0, 128 - g.size // devices))) for g in small_grads], axis=1
        ).reshape(4, 2, 2, share * 8, 128)
        half_output = lambda c: lax.dynamic_slice(output_weight_grad, (0, c * columns), (width, columns))
        came = lax.ppermute(half_output(1 - core), "seq", swap_core)
        flat = (half_output(core).astype(F32) + came.astype(F32)).astype(BF16)
        own_half, other_half, own_flat, other_flat, small_sum = reduce_last(
            half_grad.reshape(4, 2, 2, share * rows, 3 * columns), flat.reshape(4, 2, 2, share * rows, columns), small_rows
        )
        output_sum = jnp.concatenate([jnp.where(core == c, own_flat, other_flat) for c in range(share)], axis=1)
        packed_halves = [jnp.where(core == c, own_half, other_half) for c in range(share)]
        pieces = [small_sum[i, :size] for i, size in enumerate(sizes)]
    else:
        output_sum = scatter_sum(output_weight_grad).astype(F32)
        both_halves = scatter_sum(jnp.concatenate(spread(half_grad), axis=1)).astype(F32)
        packed_halves = [both_halves[:, c * 3 * columns : (c + 1) * 3 * columns] for c in range(share)]
        small_sum = scatter_sum(jnp.concatenate([g.reshape(devices, -1) for g in small_grads], axis=1))[0]
        pieces, at = [], 0
        for size in sizes:
            pieces.append(small_sum[at : at + size])
            at += size
    packed_sum = jnp.concatenate(
        [
            packed_halves[c][:, part * columns : (part + 1) * columns]
            for part in range(3)
            for c in range(share)
        ],
        axis=1,
    )
    expand_sum = jnp.concatenate(
        [early_sum[rows * j : rows * (j + 1)] for j in range(pieces_per_row)], axis=1
    )
    big = (early_sum[rows * pieces_per_row :], expand_sum, output_sum, packed_sum)
    return (
        layer_output,
        input_grad,
        pieces[0],
        pieces[1],
        big[3],
        pieces[2],
        big[2],
        pieces[3],
        pieces[4],
        pieces[5],
        big[1],
        pieces[6],
        big[0],
        pieces[7],
    )


def solution(mesh):
    both = ("dp", "seq")
    token_spec = P(None, both, None)
    vector, matrix = P(both), P(both, None)
    in_specs = (
        token_spec,
        token_spec,
        P(None, "dp", None),
        vector,
        vector,
        matrix,
        vector,
        matrix,
        vector,
        vector,
        vector,
        matrix,
        vector,
        matrix,
        vector,
    )
    out_specs = (
        token_spec,
        token_spec,
        vector,
        vector,
        matrix,
        vector,
        matrix,
        vector,
        vector,
        vector,
        matrix,
        vector,
        matrix,
        vector,
    )
    return jax.shard_map(local, mesh=mesh, in_specs=in_specs, out_specs=out_specs, check_vma=False)
```
